32 devices in a mesh: ves: 4 (over x, core), shard: 8 (over z, y).
Axes of the slice: x: 2, y: 2, z: 4, core: 2. Of those that a mesh axis runs over, the one named last changes fastest.
Arguments:
- displacement: float32 [3, 8, 256, 128], P(None, 'ves', 'shard'), may hold values from -6 to 6
- tension: float32 [8], P('ves'), may hold values from 2 to 8
- bending: float32 [8], P('ves'), may hold values from 0.2 to 0.8
- offset: float32 [3, 8, 256, 128], P(None, 'ves', 'shard'), may hold values from 0 to 1
- owner: int32 [8, 256, 128], P('ves', 'shard'), may hold values from 0 to 31, as said below
- cell: int32 [8, 256, 128], P('ves', 'shard'), may hold values from 0 to 131071
- populations: float32 [64, 19, 256, 256], P(('ves', 'shard')), may hold values from 0 to 1, as said below
Outputs:
- membrane_force: float32 [3, 8, 256, 128], P(None, 'ves', 'shard')
- force_field: float32 [64, 3, 256, 256], P(('ves', 'shard'))
- new_populations: float32 [64, 19, 256, 256], P(('ves', 'shard'))
The draws below stay inside these ranges and needn't reach their ends.
Inputs may be any that keep to these rules, and one draw needn't show every extreme that they name: The points of one device name any one owner at most 512 times, and some owner is named exactly 512 times by the points of every device. `populations`: entries are positive.
All inputs are finite; a program needn't handle non-finite values.
Results may differ from the reference program's by a relative error of at most 0.0061.
Values sent between devices are 32-bit elements; how exact they have to be, the bound alone decides.
A program may use at most 128 MiB of HBM per device.

```python
import math
import jax
import jax.numpy as jnp
from jax import lax

NXY = 256
SLAB = 2
LAT = 256
LON = 128
VES_GRP = 2
NVES = 8
NZ = 64
N_VES = 4
N_SHARD = 8


lattice_weights = [1.0 / 18, 1.0 / 36, 1.0 / 36, 1.0 / 36, 1.0 / 36, 1.0 / 18, 1.0 / 36, 1.0 / 36, 1.0 / 36, 1.0 / 36, 1.0 / 3, 1.0 / 18, 1.0 / 18, 1.0 / 18, 1.0 / 18, 1.0 / 36, 1.0 / 36, 1.0 / 36, 1.0 / 36]


def draw_populations(key, part):
    shape = (NZ, 19, NXY, NXY)
    table = jnp.array(lattice_weights, jnp.float32).reshape(1, 19, 1, 1)
    level = jax.random.uniform(key, shape, jnp.float32, 0.5, 1.5)
    return (level * table).astype(jnp.float32)


def draw_owner(key, part):
    device_count = N_VES * N_SHARD
    row_count = LAT // N_SHARD
    point_count = VES_GRP * row_count * LON
    capacity = 2 * point_count // device_count
    slot_count = device_count * capacity
    hottest = jax.random.randint(jax.random.fold_in(key, 1), (), 0, device_count)
    extra_load = jax.random.randint(jax.random.fold_in(key, 2), (device_count,), 0, 4) * 1024
    extra_load = jnp.where(jnp.arange(device_count) == hottest, 8192, extra_load)
    slot_dest = jnp.arange(slot_count, dtype=jnp.int32) // capacity

    def one_block(block_number):
        jitter = jax.random.randint(jax.random.fold_in(jax.random.fold_in(key, 3), block_number), (slot_count,), 0, 4096)
        ranking = (jitter + extra_load[slot_dest]) * slot_count + jnp.arange(slot_count, dtype=jnp.int32)
        picked_slots = jax.lax.top_k(ranking, point_count)[1]
        chosen = slot_dest[picked_slots]
        mixer = jax.random.permutation(jax.random.fold_in(jax.random.fold_in(key, 4), block_number), point_count)
        return chosen[mixer]
    blocks = jax.vmap(one_block)(jnp.arange(device_count))
    blocks = blocks.reshape(N_VES, N_SHARD, VES_GRP, row_count, LON)
    return blocks.transpose(0, 2, 1, 3, 4).reshape(N_VES * VES_GRP, LAT, LON).astype(jnp.int32)


def set_ends(entries, key, smallest, high):
    spot = [jax.random.randint(jax.random.fold_in(key, axis), (), 0, length) for axis, length in enumerate(entries.shape)]
    widest = entries.shape.index(max(entries.shape))
    beside = spot[:widest] + [(spot[widest] + 1) % entries.shape[widest]] + spot[widest + 1:]
    return entries.at[tuple(spot)].set(smallest).at[tuple(beside)].set(high)


def levels(key, extent, split, smallest, high):
    level = 1.0
    for dim, parts in split:
        draws = jax.random.uniform(jax.random.fold_in(jax.random.fold_in(key, 6), dim), (parts,), jnp.float32, smallest / len(split), high / len(split))
        level = level * jnp.repeat(jnp.exp(draws), extent[dim] // parts).reshape((-1,) + (1,) * (len(extent) - 1 - dim))
    return level


def scatter_about(stream_key, dims, deviation, limit, split=(), held_as=jnp.bfloat16):
    values = deviation * jax.random.normal(stream_key, dims, jnp.float32)
    if split:
        values = values * levels(stream_key, dims, split, -0.22, 0.18)
    return jnp.clip(values, -limit, limit).astype(held_as)


def setup_inputs(seed: int = 0) -> dict:
    seeds = jax.random.split(jax.random.key(seed), 8)
    displacement = scatter_about(seeds[0], (3, NVES, LAT, LON), 1.0, 6.0, ((1, 4), (2, 8)), jnp.float32)
    tension = jnp.clip(jnp.exp(math.log(8.0) - 1.3862944 * jax.random.uniform(seeds[1], (NVES,), jnp.float32) ** levels(seeds[1], (NVES,), ((0, 4),), -0.2, 0.2)), 2.0, 8.0)
    bending = jnp.clip(jnp.exp(math.log(0.8) - 1.3862944 * jax.random.uniform(seeds[2], (NVES,), jnp.float32) ** levels(seeds[2], (NVES,), ((0, 4),), -0.2, 0.2)), 0.2, 0.8)
    offset = jnp.clip(1.0 * jax.random.uniform(seeds[3], (3, NVES, LAT, LON), jnp.float32) ** levels(seeds[3], (3, NVES, LAT, LON), ((1, 4), (2, 8)), -0.2, 0.2), 0.0, 1.0)
    owner = draw_owner(jax.random.fold_in(seeds[7], 71), 0)
    cell = set_ends(jax.random.randint(seeds[5], (NVES, LAT, LON), 0, SLAB * NXY * NXY), jax.random.fold_in(seeds[5], 1), 0, (SLAB * NXY * NXY) - 1).astype(jnp.int32)
    populations = draw_populations(jax.random.fold_in(seeds[7], 71), 0)
    return {"displacement": displacement, "tension": tension, "bending": bending, "offset": offset, "owner": owner, "cell": cell, "populations": populations}


relax_time = 0.8
velocity_x = [0, 1, -1, 0, 0, 0, 1, -1, 0, 0, 0, 1, -1, 0, 0, 1, 1, -1, -1]
velocity_y = [0, 0, 0, 1, -1, 0, 0, 0, 1, -1, 0, 0, 0, 1, -1, 1, -1, 1, -1]
velocity_z = [1, 1, 1, 1, 1, -1, -1, -1, -1, -1, 0, 0, 0, 0, 0, 0, 0, 0, 0]
lattice_weights = [1.0 / 18, 1.0 / 36, 1.0 / 36, 1.0 / 36, 1.0 / 36, 1.0 / 18, 1.0 / 36, 1.0 / 36, 1.0 / 36, 1.0 / 36, 1.0 / 3, 1.0 / 18, 1.0 / 18, 1.0 / 18, 1.0 / 18, 1.0 / 36, 1.0 / 36, 1.0 / 36, 1.0 / 36]


def kernel_weight(distance):
    return 0.25 * (1.0 + jnp.cos(0.5 * math.pi * distance))


def surface_laplacian(field):
    padded = jnp.pad(field, ((0, 0), (0, 0), (1, 1), (0, 0)))
    center = padded[:, :, 1:-1]
    return padded[:, :, 2:] + padded[:, :, :-2] + jnp.roll(center, 1, 3) + jnp.roll(center, -1, 3) - 4.0 * center


def reference(displacement, tension, bending, offset, owner, cell, populations):
    first = surface_laplacian(displacement)
    second = surface_laplacian(first)
    membrane_force = tension[None, :, None, None] * first - bending[None, :, None, None] * second
    forces = membrane_force.reshape(3, -1)
    fraction = offset.reshape(3, -1)
    owner_flat = owner.reshape(-1).astype(jnp.int32)
    cell_flat = cell.reshape(-1).astype(jnp.int32)
    plane = cell_flat // (NXY * NXY)
    column_x = (cell_flat // NXY) % NXY
    column_y = cell_flat % NXY
    base_z = owner_flat * SLAB + plane
    coords = jnp.arange(3, dtype=jnp.int32)
    field = jnp.zeros((NZ, 3, NXY, NXY), jnp.float32)
    for reach_z in range(-1, 3):
        scaled = forces * kernel_weight(fraction[2] - reach_z)[None, :]
        plane_z = (base_z + reach_z) % NZ
        for reach_x in range(-1, 3):
            left = (scaled * kernel_weight(fraction[0] - reach_x)[None, :]).astype(jnp.bfloat16)
            left = lax.optimization_barrier(left).astype(jnp.float32)
            place_x = (column_x + reach_x) % NXY
            for reach_y in range(-1, 3):
                right = kernel_weight(fraction[1] - reach_y).astype(jnp.bfloat16)
                right = lax.optimization_barrier(right).astype(jnp.float32)
                place_y = (column_y + reach_y) % NXY
                term = left * right[None, :]
                field = field.at[plane_z[:, None], coords[None, :], place_x[:, None], place_y[:, None]].add(term.T)
    density = jnp.sum(populations, 1)
    moment_x = jnp.zeros_like(density)
    moment_y = jnp.zeros_like(density)
    moment_z = jnp.zeros_like(density)
    for item in range(19):
        moment_x = moment_x + velocity_x[item] * populations[:, item]
        moment_y = moment_y + velocity_y[item] * populations[:, item]
        moment_z = moment_z + velocity_z[item] * populations[:, item]
    flow_x = (moment_x + 0.5 * field[:, 0]) / density
    flow_y = (moment_y + 0.5 * field[:, 1]) / density
    flow_z = (moment_z + 0.5 * field[:, 2]) / density
    speed_sq = flow_x * flow_x + flow_y * flow_y + flow_z * flow_z
    moved = []
    for item in range(19):
        ex, ey, ez = velocity_x[item], velocity_y[item], velocity_z[item]
        weight = lattice_weights[item]
        along = ex * flow_x + ey * flow_y + ez * flow_z
        equilibrium = weight * density * (1.0 + 3.0 * along + 4.5 * along * along - 1.5 * speed_sq)
        push = (ex - flow_x) * field[:, 0] + (ey - flow_y) * field[:, 1] + (ez - flow_z) * field[:, 2]
        facing = ex * field[:, 0] + ey * field[:, 1] + ez * field[:, 2]
        source = weight * (3.0 * push + 9.0 * along * facing)
        current = populations[:, item]
        post = current - (current - equilibrium) / relax_time + (1.0 - 0.5 / relax_time) * source
        moved.append(jnp.roll(post, (ez, ex, ey), (0, 1, 2)))
    return membrane_force, field, jnp.stack(moved, 1)
```

```python
import math

import jax
import jax.numpy as jnp
from jax import lax
from jax.experimental import pallas as pl
from jax.experimental.pallas import tpu as pltpu
from jax.sharding import PartitionSpec as P


relax_time = 0.8
velocity_x = [0, 1, -1, 0, 0, 0, 1, -1, 0, 0, 0, 1, -1, 0, 0, 1, 1, -1, -1]
velocity_y = [0, 0, 0, 1, -1, 0, 0, 0, 1, -1, 0, 0, 0, 1, -1, 1, -1, 1, -1]
velocity_z = [1, 1, 1, 1, 1, -1, -1, -1, -1, -1, 0, 0, 0, 0, 0, 0, 0, 0, 0]
lattice_weights = [
    1.0 / 18,
    1.0 / 36,
    1.0 / 36,
    1.0 / 36,
    1.0 / 36,
    1.0 / 18,
    1.0 / 36,
    1.0 / 36,
    1.0 / 36,
    1.0 / 36,
    1.0 / 3,
    1.0 / 18,
    1.0 / 18,
    1.0 / 18,
    1.0 / 18,
    1.0 / 36,
    1.0 / 36,
    1.0 / 36,
    1.0 / 36,
]


def passed_along(value, axis, steps):
    count = lax.axis_size(axis)
    pairs = [(source, (source + steps) % count) for source in range(count)]
    return lax.ppermute(value, axis, pairs)


def with_halo(x, axis, dim, width):
    devices, length = (lax.axis_size(axis), x.shape[dim])
    up = [(i, i + 1) for i in range(devices - 1)]
    down = [(j, i) for i, j in up]
    last = lax.slice_in_dim(x, length - width, length, axis=dim)
    initial = lax.slice_in_dim(x, 0, width, axis=dim)
    before = lax.ppermute(last, axis, up)
    after = lax.ppermute(initial, axis, down)
    return jnp.concatenate([before, x, after], axis=dim)


def laplacian(padded):
    center = padded[:, :, 1:-1]
    return (
        padded[:, :, 2:]
        + padded[:, :, :-2]
        + jnp.roll(center, 1, 3)
        + jnp.roll(center, -1, 3)
        - 4.0 * center
    )


def membrane(displacement, tension, bending):
    padded = with_halo(displacement, "shard", 2, 2)
    wide_first = laplacian(padded)
    rows = wide_first.shape[2]
    place = lax.broadcasted_iota(jnp.int32, (1, 1, rows, 1), 2)
    index = lax.axis_index("shard")
    outside = ((place == 0) & (index == 0)) | (
        (place == rows - 1) & (index == lax.axis_size("shard") - 1)
    )
    wide_first = jnp.where(outside, 0.0, wide_first)
    second = laplacian(wide_first)
    first = wide_first[:, :, 1:-1]
    return tension[None, :, None, None] * first - bending[None, :, None, None] * second


WINDOW = 16
ROWS = 24
BLOCK = 256


HALF_PI = 0.5 * math.pi
COSINE = [(-1.0) ** n * HALF_PI ** (2 * n) / math.factorial(2 * n) for n in range(8)]
SINE = [(-1.0) ** n * HALF_PI ** (2 * n + 1) / math.factorial(2 * n + 1) for n in range(8)]


def weights(fraction):
    square = fraction * fraction
    c = jnp.full_like(square, COSINE[-1])
    s = jnp.full_like(square, SINE[-1])
    for n in range(6, -1, -1):
        c = c * square + COSINE[n]
        s = s * square + SINE[n]
    s = s * fraction
    return [0.25 * (1.0 - s), 0.25 * (1.0 + c), 0.25 * (1.0 + s), 0.25 * (1.0 - c)]


def bits(count):
    return (count - 1).bit_length()


def spread_list(starts, list_ref, acc, shift, planes, slab, ranges):
    width = acc.shape[2]
    row_id = lax.broadcasted_iota(jnp.int32, (ROWS, BLOCK), 0)
    y_id = lax.broadcasted_iota(jnp.int32, (width, BLOCK), 0)

    def pick(rel, parts):
        result = jnp.zeros(rel.shape, jnp.float32)
        for k in range(4):
            result = jnp.where(rel == k, parts[k], result)
        return result

    def window(w, offset):
        begin = starts[w] // BLOCK
        end = (starts[w + 1] + (BLOCK - 1)) // BLOCK
        base = w * WINDOW
        at_row = (w + offset) * WINDOW

        @pl.loop(begin, end)
        def _(b):
            at = pl.ds(pl.multiple_of(b * BLOCK, BLOCK), BLOCK)
            phi = weights(list_ref[3:6, at])
            key = list_ref[6:7, at].astype(jnp.int32)
            y = key & ((1 << bits(width)) - 1)
            plane = (key >> bits(width)) & ((1 << bits(slab)) - 1)
            x = (key >> (bits(width) + bits(slab))) - base
            x = jnp.where((x >= 0) & (x < WINDOW), x, 4 * ROWS)
            weight_x = pick(row_id - x, [phi[k][0:1] for k in range(4)])
            right = pick((y_id - (y - 1)) & (width - 1), [phi[k][1:2] for k in range(4)])
            lefts = []
            for q in planes:
                weight_z = pick(q + 1 + shift - plane, [phi[k][2:3] for k in range(4)])
                for c in range(3):
                    lefts.append((list_ref[c : c + 1, at] * weight_z) * weight_x)
            product = lax.dot_general(
                jnp.concatenate(lefts, 0).astype(jnp.bfloat16),
                right.astype(jnp.bfloat16),
                (((1,), (1,)), ((), ())),
                preferred_element_type=jnp.float32,
            )
            rows = pl.ds(pl.multiple_of(at_row, 8), ROWS)
            for n, q in enumerate(planes):
                for c in range(3):
                    i = n * 3 + c
                    acc[q * 3 + c, rows, :] += product[i * ROWS : (i + 1) * ROWS]

    for first, last, offset in ranges:

        @pl.loop(first, last)
        def _(w):
            window(w, offset)


VMEM = pl.BlockSpec(memory_space=pltpu.VMEM)
SMEM = pl.BlockSpec(memory_space=pltpu.SMEM)


def cost(flops):
    return pl.CostEstimate(flops=flops, bytes_accessed=4_000_000, transcendentals=0)


def starts_of(listed, windows):
    return listed[7, : windows + 1].astype(jnp.int32)


def spread_own(listed, slab, width):
    windows = width // WINDOW

    def kernel(starts, list_ref, acc):
        acc[...] = jnp.zeros_like(acc)
        spread_list(starts, list_ref, acc, 0, range(slab), slab, [(0, windows, 0)])

    return pl.pallas_call(
        kernel,
        out_shape=jax.ShapeDtypeStruct((slab * 3, width + ROWS - WINDOW, width), jnp.float32),
        in_specs=[SMEM, VMEM],
        out_specs=VMEM,
        name="spread_own",
        cost_estimate=cost(20_000_000_000),
    )(starts_of(listed, windows), listed)


ANY = pl.BlockSpec(memory_space=pl.ANY)
MIB = 1 << 20
LAG = 7
KEEP = 1.0 - 1.0 / relax_time
FORCING = 1.0 - 0.5 / relax_time


def collided(f, force, items):
    def along(vector, item, start=None):
        total = start
        for e, v in zip((velocity_x[item], velocity_y[item], velocity_z[item]), vector):
            if e == 0:
                continue
            if total is None:
                total = v if e > 0 else -v
            else:
                total = total + v if e > 0 else total - v
        return total

    def tree(values):
        while len(values) > 1:
            values = [
                values[i] + values[i + 1] if i + 1 < len(values) else values[i]
                for i in range(0, len(values), 2)
            ]
        return values[0]

    density = tree(list(f))
    inverse = 1.0 / density
    flow = []
    for axis, table in enumerate((velocity_x, velocity_y, velocity_z)):
        plus = tree([f[i] for i in range(19) if table[i] > 0])
        minus = tree([f[i] for i in range(19) if table[i] < 0])
        flow.append(((plus - minus) + 0.5 * force[axis]) * inverse)
    speed_sq = flow[0] * flow[0] + flow[1] * flow[1] + flow[2] * flow[2]
    work = flow[0] * force[0] + flow[1] * force[1] + flow[2] * force[2]
    scaled = density * (1.0 / relax_time)
    base = scaled - (1.5 * scaled) * speed_sq - (3.0 * FORCING) * work
    linear = 3.0 * scaled
    square = 4.5 * scaled
    pushed = [3.0 * FORCING * v for v in force]
    result = {}
    for item in items:
        cu = along(flow, item)
        if cu is None:
            bracket = base
        else:
            facing = along(pushed, item)
            bracket = base + facing + cu * (linear + square * cu + 3.0 * facing)
        result[item] = KEEP * f[item] + lattice_weights[item] * bracket
    return result


def spread_chunk(lists, total, carry, head, populations, field, first, last):
    below, above = lists
    slab, width = (populations.shape[0], populations.shape[2])
    windows = width // WINDOW
    opening, closing = (first == 0, last == windows)
    begin = 0 if opening else (first - 1) * WINDOW
    end = width if closing else (last - 1) * WINDOW
    n = end - begin
    span = n + ROWS
    planes = (slab - 1, 0)

    def kernel(s0, l0, s1, l1, total_ref, carry_ref, head_ref, pop_ref, field_in, *rest):
        low, high, carry_out, field_out, acc, pop, post, sems = rest
        del field_in
        copies = []

        def fetch(source, target):
            copy = pltpu.make_async_copy(source, target, sems.at[len(copies)])
            copy.start()
            copies.append(copy)

        got = 0
        if not opening:
            fetch(carry_ref, acc.at[:, 0:ROWS, :])
            got = ROWS
        stop = min(span, width + ROWS - WINDOW - begin)
        fetch(total_ref.at[:, begin + got : begin + stop, :], acc.at[:, got:stop, :])
        early = len(copies)
        for n_plane, plane in enumerate(planes):
            for x in range(0, 3):
                source, target, size = (
                    ((begin - 8) % width, 0, 8),
                    (begin, 8, n),
                    (end % width, n + 8, 8),
                )[x]
                fetch(
                    pop_ref.at[plane, :, source : source + size, :],
                    pop.at[n_plane, :, target : target + size, :],
                )
        for copy in copies[:early]:
            copy.wait()
        if closing:
            acc[:, stop:span, :] = jnp.zeros((slab * 3, span - stop, width), jnp.float32)
        moves = (first, last, 0 if opening else 1 - first)
        spread_list(s0, l0, acc, slab, (0, 1), slab, [moves])
        spread_list(s1, l1, acc, -slab, (slab - 1,), slab, [moves])
        if closing:
            acc[:, n : n + 16, :] += head_ref[:, 0:16, :]
        if opening:
            carry_out[:, ROWS : 2 * ROWS, :] = acc[:, 0:ROWS, :]
            carry_out[:, 0:ROWS, :] = acc[:, n : n + ROWS, :]
        elif not closing:
            carry_out[:, 0:ROWS, :] = acc[:, n : n + ROWS, :]
        else:
            carry_out[...] = jnp.zeros_like(carry_out)
        written = [
            pltpu.make_async_copy(
                acc.at[i, 8 : 8 + n, :],
                field_out.at[i // 3, i % 3, begin:end, :],
                sems.at[len(copies) + i],
            )
            for i in range(slab * 3)
        ]
        for copy in written:
            copy.start()
        for copy in copies[early:]:
            copy.wait()

        @pl.loop(0, (n + 16) // 8)
        def _(t):
            rows = pl.ds(pl.multiple_of(t * 8, 8), 8)
            for n_plane, plane in enumerate(planes):
                f = [pop[n_plane, i, rows, :] for i in range(19)]
                force = [acc[plane * 3 + c, rows, :] for c in range(3)]
                items = range(n_plane * 5, n_plane * 5 + 5)
                for i, value in collided(f, force, items).items():
                    post[i, rows, :] = value

        for target, begin_item in ((low, 0), (high, 5)):
            for i in range(5):
                item = begin_item + i
                at = 8 - velocity_x[item]
                value = post[item, at : at + n, :]
                if velocity_y[item]:
                    value = pltpu.roll(value, velocity_y[item] % width, 1)
                target[i] = value
        for copy in written:
            copy.wait()

    shape = jax.ShapeDtypeStruct
    return pl.pallas_call(
        kernel,
        out_shape=(
            shape((5, n, width), jnp.float32),
            shape((5, n, width), jnp.float32),
            shape((slab * 3, 2 * ROWS, width), jnp.float32),
            shape((slab, 3, width, width), jnp.float32),
        ),
        in_specs=[SMEM, VMEM, SMEM, VMEM, ANY, ANY, VMEM, ANY, ANY],
        out_specs=(VMEM, VMEM, VMEM, ANY),
        scratch_shapes=[
            pltpu.VMEM((slab * 3, span, width), jnp.float32),
            pltpu.VMEM((2, 19, n + 16, width), jnp.float32),
            pltpu.VMEM((10, n + 16, width), jnp.float32),
            pltpu.SemaphoreType.DMA((8 + slab * 3,)),
        ],
        input_output_aliases={} if field is None else {8: 3},
        compiler_params=pltpu.CompilerParams(vmem_limit_bytes=20 * MIB),
        cost_estimate=cost(8_000_000_000),
    )(
        starts_of(below, windows),
        below,
        starts_of(above, windows),
        above,
        total,
        jnp.zeros((slab * 3, ROWS, width), jnp.float32) if carry is None else carry[:, :ROWS],
        jnp.zeros((slab * 3, ROWS, width), jnp.float32) if head is None else head,
        populations,
        jnp.zeros((8, 128), jnp.float32) if field is None else field,
    )


def interior(populations, field):
    slab, width = (populations.shape[0], populations.shape[2])
    pieces = 4
    step = width // pieces

    def kernel(pop_ref, field_ref, out_ref, pop, force, post, out, in_sems, out_sems):
        def fetch(k):
            rows = pl.ds(k * step, step)
            return (
                pltpu.make_async_copy(pop_ref.at[:, :, rows, :], pop.at[:, :, rows, :], in_sems.at[0, k]),
                pltpu.make_async_copy(field_ref.at[:, :, rows, :], force.at[:, :, rows, :], in_sems.at[1, k]),
            )

        for k in range(pieces):
            for copy in fetch(k):
                copy.start()

        ranges = []
        for p in range(slab):
            if p > 0:
                ranges.append((p, 0, 5))
            if p < slab - 1:
                ranges.append((p, 5, 19))
            else:
                ranges.append((p, 10, 19))

        def kept(p):
            return [i for i in range(19) if 0 <= p + velocity_z[i] < slab]

        started = []

        def emit(k, low, high):
            @pl.loop(low // 8, high // 8)
            def _(t):
                for p in range(slab):
                    for i in kept(p):
                        x = velocity_x[i]
                        if x == 0:
                            continue
                        q = p + velocity_z[i]
                        near = pl.ds(pl.multiple_of(t * 8 + (0 if x > 0 else 8), 8), 16)
                        value = post[q, i, near, :]
                        value = value[7:15] if x > 0 else value[1:9]
                        out[q, i, pl.ds(pl.multiple_of(t * 8, 8), 8), :] = value

            for r, (p, begin, end) in enumerate(ranges):
                copy = pltpu.make_async_copy(
                    out.at[p, begin:end, low:high, :],
                    out_ref.at[p, begin:end, low:high, :],
                    out_sems.at[r, k],
                )
                copy.start()
                started.append(copy)

        for k in range(pieces):
            for copy in fetch(k):
                copy.wait()

            @pl.loop(k * step // 8, (k + 1) * step // 8)
            def _(t):
                rows = pl.ds(pl.multiple_of(t * 8, 8), 8)
                padded = pl.ds(pl.multiple_of(t * 8 + 8, 8), 8)
                for p in range(slab):
                    f = [pop[p, i, rows, :] for i in range(19)]
                    moved = collided(f, [force[p, c, rows, :] for c in range(3)], kept(p))
                    for i, value in moved.items():
                        if velocity_y[i]:
                            value = pltpu.roll(value, velocity_y[i] % width, 1)
                        q = p + velocity_z[i]
                        if velocity_x[i]:
                            post[q, i, padded, :] = value
                        else:
                            out[q, i, rows, :] = value

            if k < pieces - 1:
                emit(k, 8 if k == 0 else k * step - 8, (k + 1) * step - 8)
        for p in range(slab):
            for i in kept(p):
                q = p + velocity_z[i]
                if velocity_x[i] > 0:
                    post[q, i, 0:8, :] = post[q, i, width : width + 8, :]
                elif velocity_x[i] < 0:
                    post[q, i, width + 8 : width + 16, :] = post[q, i, 8:16, :]
        emit(pieces - 1, (pieces - 1) * step - 8, width)
        emit(pieces, 0, 8)
        for copy in started:
            copy.wait()

    return pl.pallas_call(
        kernel,
        out_shape=jax.ShapeDtypeStruct(populations.shape, jnp.float32),
        in_specs=[ANY, ANY],
        out_specs=ANY,
        scratch_shapes=[
            pltpu.VMEM(populations.shape, jnp.float32),
            pltpu.VMEM(field.shape, jnp.float32),
            pltpu.VMEM((slab, 19, width + 16, width), jnp.float32),
            pltpu.VMEM(populations.shape, jnp.float32),
            pltpu.SemaphoreType.DMA((2, pieces)),
            pltpu.SemaphoreType.DMA((2 * slab, pieces + 1)),
        ],
        compiler_params=pltpu.CompilerParams(vmem_limit_bytes=36 * MIB),
        name="interior",
        cost_estimate=pl.CostEstimate(flops=0, bytes_accessed=25_000_000, transcendentals=0),
    )(populations, field)


def arrivals(new_populations, lows, highs, edges):
    slab = new_populations.shape[0]
    count = len(lows)

    def kernel(*refs):
        parts, out_ref, sems = (refs[1 : 1 + 2 * count], refs[-2], refs[-1])
        copies = []
        for k, (begin, end) in enumerate(edges):
            for s, (part, plane, item) in enumerate(
                ((parts[k], 0, 0), (parts[count + k], slab - 1, 5))
            ):
                copies.append(
                    pltpu.make_async_copy(
                        part, out_ref.at[plane, item : item + 5, begin:end, :], sems.at[s, k]
                    )
                )
        for copy in copies:
            copy.start()
        for copy in copies:
            copy.wait()

    return pl.pallas_call(
        kernel,
        out_shape=jax.ShapeDtypeStruct(new_populations.shape, jnp.float32),
        in_specs=[ANY] + [VMEM] * (2 * count),
        out_specs=ANY,
        scratch_shapes=[pltpu.SemaphoreType.DMA((2, count))],
        input_output_aliases={0: 0},
        compiler_params=pltpu.CompilerParams(vmem_limit_bytes=8 * MIB),
        name="arrivals",
    )(new_populations, *lows, *highs)


def dispatched(membrane_force, offset, owner, cell, device_count, cells):
    point_count = owner.size
    capacity = 2 * point_count // device_count
    slot_total = device_count * capacity
    owner = owner.reshape(point_count)
    cell = cell.reshape(point_count)
    devices = jnp.arange(device_count, dtype=jnp.int32)
    counts = jnp.sum((owner[None, :] == devices[:, None]).astype(jnp.int32), 1)
    filler_ends = jnp.cumsum(capacity - counts)
    filler = jnp.arange(slot_total - point_count, dtype=jnp.int32)
    filler_owner = jnp.sum((filler[None, :] >= filler_ends[:, None]).astype(jnp.int32), 0)
    span = 2 * cells
    key = jnp.concatenate([owner * span + cell, filler_owner * span + cells])
    payload = jnp.concatenate(
        [membrane_force.reshape(3, point_count), offset.reshape(3, point_count)], 0
    )
    payload = jnp.pad(payload, ((0, 0), (0, slot_total - point_count)))
    ordered = lax.sort(
        (key,) + tuple(payload[i] for i in range(6)), num_keys=1, is_stable=False
    )
    tag = (ordered[0] % span).astype(jnp.float32)
    send = jnp.stack(
        [v.reshape(device_count, capacity) for v in list(ordered[1:]) + [tag]], 1
    )
    got = lax.all_to_all(send, ("ves", "shard"), split_axis=0, concat_axis=0, tiled=True)
    return got.transpose(1, 0, 2).reshape(7, slot_total)


CUTS = (0, 4, 8, 12, 16)


def one_step(displacement, tension, bending, offset, owner, cell, populations):
    membrane_force = membrane(displacement, tension, bending)
    device_count = lax.axis_size("ves") * lax.axis_size("shard")
    slab, width = (populations.shape[0], populations.shape[2])
    cells = slab * width * width
    windows = width // WINDOW
    got = dispatched(membrane_force, offset, owner, cell, device_count, cells)
    tag = got[6].astype(jnp.int32)
    plane, x, y = (tag // (width * width), tag // width % width, tag % width)
    x = (x + LAG) & (width - 1)
    x_bit = bits(slab) + bits(width)
    key = jnp.where(tag >= cells, width << x_bit, (x << x_bit) | (plane << bits(width)) | y)
    bounds = jnp.arange(windows + 1, dtype=jnp.int32) * (WINDOW << x_bit)
    starts = jnp.sum((key[None, :] < bounds[:, None]).astype(jnp.float32), 1)
    ordered = lax.sort(
        (key,) + tuple(got[i] for i in range(6)), num_keys=1, is_stable=False
    )
    listed = jnp.stack(
        list(ordered[1:])
        + [ordered[0].astype(jnp.float32), jnp.pad(starts, (0, key.size - windows - 1))],
        0,
    )
    below = passed_along(listed, ("ves", "shard"), 1)
    above = passed_along(listed, ("ves", "shard"), -1)
    total = spread_own(listed, slab, width)

    cuts = [cut * windows // CUTS[-1] for cut in CUTS]
    field = carry = head = None
    lows, highs, edges = ([], [], [])
    begin = 0
    for j, (first, last) in enumerate(zip(cuts[:-1], cuts[1:])):
        low, high, carry, field = spread_chunk(
            (below, above), total, carry, head if last == windows else None,
            populations, field, first, last,
        )
        if j == 0:
            head = carry[:, ROWS:]
        edges.append((begin, begin + low.shape[1]))
        begin += low.shape[1]
        lows.append(passed_along(low, ("ves", "shard"), 1))
        highs.append(passed_along(high, ("ves", "shard"), -1))
    new_populations = interior(populations, field)
    new_populations = arrivals(new_populations, lows, highs, edges)
    return (membrane_force, field, new_populations)


def solution(mesh):
    return jax.shard_map(
        one_step,
        mesh=mesh,
        in_specs=(
            P(None, "ves", "shard", None),
            P("ves"),
            P("ves"),
            P(None, "ves", "shard", None),
            P("ves", "shard", None),
            P("ves", "shard", None),
            P(("ves", "shard"), None, None, None),
        ),
        out_specs=(
            P(None, "ves", "shard", None),
            P(("ves", "shard"), None, None, None),
            P(("ves", "shard"), None, None, None),
        ),
        check_vma=False,
    )
```

```python
import math

import jax
import jax.numpy as jnp
from jax import lax
from jax.experimental import pallas as pl
from jax.experimental.pallas import tpu as pltpu
from jax.sharding import PartitionSpec as P


relax_time = 0.8
velocity_x = [0, 1, -1, 0, 0, 0, 1, -1, 0, 0, 0, 1, -1, 0, 0, 1, 1, -1, -1]
velocity_y = [0, 0, 0, 1, -1, 0, 0, 0, 1, -1, 0, 0, 0, 1, -1, 1, -1, 1, -1]
velocity_z = [1, 1, 1, 1, 1, -1, -1, -1, -1, -1, 0, 0, 0, 0, 0, 0, 0, 0, 0]
lattice_weights = [
    1.0 / 18,
    1.0 / 36,
    1.0 / 36,
    1.0 / 36,
    1.0 / 36,
    1.0 / 18,
    1.0 / 36,
    1.0 / 36,
    1.0 / 36,
    1.0 / 36,
    1.0 / 3,
    1.0 / 18,
    1.0 / 18,
    1.0 / 18,
    1.0 / 18,
    1.0 / 36,
    1.0 / 36,
    1.0 / 36,
    1.0 / 36,
]


def passed_along(value, axis, steps):
    count = lax.axis_size(axis)
    pairs = [(source, (source + steps) % count) for source in range(count)]
    return lax.ppermute(value, axis, pairs)


def with_halo(x, axis, dim, width):
    devices, length = (lax.axis_size(axis), x.shape[dim])
    up = [(i, i + 1) for i in range(devices - 1)]
    down = [(j, i) for i, j in up]
    last = lax.slice_in_dim(x, length - width, length, axis=dim)
    initial = lax.slice_in_dim(x, 0, width, axis=dim)
    before = lax.ppermute(last, axis, up)
    after = lax.ppermute(initial, axis, down)
    return jnp.concatenate([before, x, after], axis=dim)


def laplacian(padded):
    center = padded[:, :, 1:-1]
    return (
        padded[:, :, 2:]
        + padded[:, :, :-2]
        + jnp.roll(center, 1, 3)
        + jnp.roll(center, -1, 3)
        - 4.0 * center
    )


def membrane(displacement, tension, bending):
    padded = with_halo(displacement, "shard", 2, 2)
    wide_first = laplacian(padded)
    rows = wide_first.shape[2]
    place = lax.broadcasted_iota(jnp.int32, (1, 1, rows, 1), 2)
    index = lax.axis_index("shard")
    outside = ((place == 0) & (index == 0)) | (
        (place == rows - 1) & (index == lax.axis_size("shard") - 1)
    )
    wide_first = jnp.where(outside, 0.0, wide_first)
    second = laplacian(wide_first)
    first = wide_first[:, :, 1:-1]
    return tension[None, :, None, None] * first - bending[None, :, None, None] * second


WINDOW = 16
ROWS = 24
BLOCK = 256


HALF_PI = 0.5 * math.pi
COSINE = [(-1.0) ** n * HALF_PI ** (2 * n) / math.factorial(2 * n) for n in range(8)]
SINE = [(-1.0) ** n * HALF_PI ** (2 * n + 1) / math.factorial(2 * n + 1) for n in range(8)]


def weights(fraction):
    square = fraction * fraction
    c = jnp.full_like(square, COSINE[-1])
    s = jnp.full_like(square, SINE[-1])
    for n in range(6, -1, -1):
        c = c * square + COSINE[n]
        s = s * square + SINE[n]
    s = s * fraction
    return [0.25 * (1.0 - s), 0.25 * (1.0 + c), 0.25 * (1.0 + s), 0.25 * (1.0 - c)]


def bits(count):
    return (count - 1).bit_length()


LANES = 128
MIB = 1 << 20


def rows_of(planes):
    return 13 + 3 * len(planes)


def spread_list(starts, list_ref, acc, table, shift, planes, slab, ranges):
    width = acc.shape[2]
    count = table.shape[1]
    row_id = lax.broadcasted_iota(jnp.int32, (ROWS, LANES), 0).astype(jnp.float32)
    y_id = lax.broadcasted_iota(jnp.int32, (width, LANES), 0).astype(jnp.bfloat16)

    def prepare(t):
        at = pl.ds(pl.multiple_of(t * 8, 8), 8)
        part = [list_ref[pl.ds(pl.multiple_of(c * count + t * 8, 8), 8), :] for c in range(7)]
        key = part[6].astype(jnp.int32)
        y = key & (width - 1)
        plane = (key >> bits(width)) & (slab - 1)
        table[0, at, :] = (key >> (bits(width) + bits(slab))).astype(jnp.float32)
        phi_x, phi_y, phi_z = (weights(part[c]) for c in (3, 4, 5))
        for k in range(4):
            table[1 + k, at, :] = phi_x[k]
            table[5 + k, at, :] = phi_y[k]
            table[9 + k, at, :] = ((y + (k - 1)) & (width - 1)).astype(jnp.float32)
        for n, q in enumerate(planes):
            rel = q + 1 + shift - plane
            weight = jnp.zeros_like(part[0])
            for k in range(4):
                weight = jnp.where(rel == k, phi_z[k], weight)
            for c in range(3):
                table[13 + n * 3 + c, at, :] = part[c] * weight

    def half(r, base):
        def row(i, like):
            return jnp.broadcast_to(table[i, pl.ds(r, 1), :], like.shape)

        def narrow(i):
            return jnp.broadcast_to(table[i, pl.ds(r, 1), :].astype(jnp.bfloat16), y_id.shape)

        right = jnp.zeros(y_id.shape, jnp.bfloat16)
        for k in range(4):
            right = jnp.where(y_id == narrow(9 + k), narrow(5 + k), right)
        x = table[0, pl.ds(r, 1), :] - base
        x = jnp.where((x >= 0.0) & (x < WINDOW), x, 4.0 * ROWS)
        rel = row_id - x
        weight_x = jnp.zeros(row_id.shape, jnp.float32)
        for k in range(4):
            weight_x = jnp.where(rel == k, row(1 + k, row_id), weight_x)
        lefts = [row(13 + i, row_id) * weight_x for i in range(3 * len(planes))]
        return jnp.concatenate(lefts, 0).astype(jnp.bfloat16), right

    def window(w, offset):
        begin = starts[w] // BLOCK
        end = (starts[w + 1] + (BLOCK - 1)) // BLOCK
        base = (w * WINDOW).astype(jnp.float32)
        at_row = (w + offset) * WINDOW

        @pl.loop(begin, end)
        def _(b):
            parts = [half(b * (BLOCK // LANES) + h, base) for h in range(BLOCK // LANES)]
            product = lax.dot_general(
                jnp.concatenate([p[0] for p in parts], 1),
                jnp.concatenate([p[1] for p in parts], 1),
                (((1,), (1,)), ((), ())),
                preferred_element_type=jnp.float32,
            )
            rows = pl.ds(pl.multiple_of(at_row, 8), ROWS)
            for n, q in enumerate(planes):
                for c in range(3):
                    i = n * 3 + c
                    acc[q * 3 + c, rows, :] += product[i * ROWS : (i + 1) * ROWS]

    for first, last, offset in ranges:
        unit = 8 * LANES
        low = starts[first] // BLOCK * BLOCK // unit
        high = (starts[last] + (BLOCK - 1)) // BLOCK * BLOCK

        @pl.loop(low, (high + (unit - 1)) // unit)
        def _(t):
            prepare(t)

        @pl.loop(first, last)
        def _(w):
            window(w, offset)


VMEM = pl.BlockSpec(memory_space=pltpu.VMEM)
SMEM = pl.BlockSpec(memory_space=pltpu.SMEM)


def cost(flops):
    return pl.CostEstimate(flops=flops, bytes_accessed=4_000_000, transcendentals=0)


def starts_of(listed, windows):
    return listed[-8, : windows + 1].astype(jnp.int32)


def spread_own(listed, slab, width):
    windows = width // WINDOW

    count = (listed.shape[0] - 8) // 7
    assert count % 8 == 0

    def kernel(starts, list_ref, acc, table):
        acc[...] = jnp.zeros_like(acc)
        spread_list(starts, list_ref, acc, table, 0, range(slab), slab, [(0, windows, 0)])

    return pl.pallas_call(
        kernel,
        out_shape=jax.ShapeDtypeStruct((slab * 3, width + ROWS - WINDOW, width), jnp.float32),
        in_specs=[SMEM, VMEM],
        out_specs=VMEM,
        scratch_shapes=[pltpu.VMEM((rows_of(range(slab)), count, LANES), jnp.float32)],
        compiler_params=pltpu.CompilerParams(vmem_limit_bytes=12 * MIB),
        name="spread_own",
        cost_estimate=cost(20_000_000_000),
    )(starts_of(listed, windows), listed)


ANY = pl.BlockSpec(memory_space=pl.ANY)
HBM = pl.BlockSpec(memory_space=pltpu.HBM)
LAG = 7
KEEP = 1.0 - 1.0 / relax_time
FORCING = 1.0 - 0.5 / relax_time


def collided(f, force, items):
    def along(vector, item, start=None):
        total = start
        for e, v in zip((velocity_x[item], velocity_y[item], velocity_z[item]), vector):
            if e == 0:
                continue
            if total is None:
                total = v if e > 0 else -v
            else:
                total = total + v if e > 0 else total - v
        return total

    def tree(values):
        while len(values) > 1:
            values = [
                values[i] + values[i + 1] if i + 1 < len(values) else values[i]
                for i in range(0, len(values), 2)
            ]
        return values[0]

    density = tree(list(f))
    inverse = 1.0 / density
    flow = []
    for axis, table in enumerate((velocity_x, velocity_y, velocity_z)):
        plus = tree([f[i] for i in range(19) if table[i] > 0])
        minus = tree([f[i] for i in range(19) if table[i] < 0])
        flow.append(((plus - minus) + 0.5 * force[axis]) * inverse)
    speed_sq = flow[0] * flow[0] + flow[1] * flow[1] + flow[2] * flow[2]
    work = flow[0] * force[0] + flow[1] * force[1] + flow[2] * force[2]
    scaled = density * (1.0 / relax_time)
    base = scaled - (1.5 * scaled) * speed_sq - (3.0 * FORCING) * work
    linear = 3.0 * scaled
    square = 4.5 * scaled
    pushed = [3.0 * FORCING * v for v in force]
    result = {}
    for item in items:
        cu = along(flow, item)
        if cu is None:
            bracket = base
        else:
            facing = along(pushed, item)
            bracket = base + facing + cu * (linear + square * cu + 3.0 * facing)
        result[item] = KEEP * f[item] + lattice_weights[item] * bracket
    return result


def spread_chunk(lists, total, carry, head, populations, field, first, last):
    below, above = lists
    slab, width = (populations.shape[0], populations.shape[2])
    windows = width // WINDOW
    opening, closing = (first == 0, last == windows)
    begin = 0 if opening else (first - 1) * WINDOW
    end = width if closing else (last - 1) * WINDOW
    n = end - begin
    span = n + ROWS
    planes = (slab - 1, 0)

    def kernel(s0, l0, s1, l1, total_ref, carry_ref, head_ref, pop_ref, field_in, *rest):
        low, high, carry_out, field_out, acc, pop, post, table, sems = rest
        del field_in
        copies = []

        def fetch(source, target):
            copy = pltpu.make_async_copy(source, target, sems.at[len(copies)])
            copy.start()
            copies.append(copy)

        got = 0
        if not opening:
            fetch(carry_ref, acc.at[:, 0:ROWS, :])
            got = ROWS
        stop = min(span, width + ROWS - WINDOW - begin)
        fetch(total_ref.at[:, begin + got : begin + stop, :], acc.at[:, got:stop, :])
        early = len(copies)
        for n_plane, plane in enumerate(planes):
            for x in range(0, 3):
                source, target, size = (
                    ((begin - 8) % width, 0, 8),
                    (begin, 8, n),
                    (end % width, n + 8, 8),
                )[x]
                fetch(
                    pop_ref.at[plane, :, source : source + size, :],
                    pop.at[n_plane, :, target : target + size, :],
                )
        for copy in copies[:early]:
            copy.wait()
        if closing:
            acc[:, stop:span, :] = jnp.zeros((slab * 3, span - stop, width), jnp.float32)
        moves = (first, last, 0 if opening else 1 - first)
        spread_list(s0, l0, acc, table, slab, (0, 1), slab, [moves])
        spread_list(s1, l1, acc, table, -slab, (slab - 1,), slab, [moves])
        if closing:
            acc[:, n : n + 16, :] += head_ref[:, 0:16, :]
        if opening:
            carry_out[:, ROWS : 2 * ROWS, :] = acc[:, 0:ROWS, :]
            carry_out[:, 0:ROWS, :] = acc[:, n : n + ROWS, :]
        elif not closing:
            carry_out[:, 0:ROWS, :] = acc[:, n : n + ROWS, :]
        else:
            carry_out[...] = jnp.zeros_like(carry_out)
        written = [
            pltpu.make_async_copy(
                acc.at[i, 8 : 8 + n, :],
                field_out.at[i // 3, i % 3, begin:end, :],
                sems.at[len(copies) + i],
            )
            for i in range(slab * 3)
        ]
        for copy in written:
            copy.start()
        for copy in copies[early:]:
            copy.wait()

        @pl.loop(0, (n + 16) // 8)
        def _(t):
            rows = pl.ds(pl.multiple_of(t * 8, 8), 8)
            for n_plane, plane in enumerate(planes):
                f = [pop[n_plane, i, rows, :] for i in range(19)]
                force = [acc[plane * 3 + c, rows, :] for c in range(3)]
                items = range(n_plane * 5, n_plane * 5 + 5)
                for i, value in collided(f, force, items).items():
                    post[i, rows, :] = value

        for target, begin_item in ((low, 0), (high, 5)):
            for i in range(5):
                item = begin_item + i
                at = 8 - velocity_x[item]
                value = post[item, at : at + n, :]
                if velocity_y[item]:
                    value = pltpu.roll(value, velocity_y[item] % width, 1)
                target[i] = value
        for copy in written:
            copy.wait()

    shape = jax.ShapeDtypeStruct
    return pl.pallas_call(
        kernel,
        out_shape=(
            shape((5, n, width), jnp.float32),
            shape((5, n, width), jnp.float32),
            shape((slab * 3, 2 * ROWS, width), jnp.float32),
            shape((slab, 3, width, width), jnp.float32),
        ),
        in_specs=[SMEM, VMEM, SMEM, VMEM, HBM, ANY, VMEM, HBM, HBM],
        out_specs=(VMEM, VMEM, VMEM, HBM),
        scratch_shapes=[
            pltpu.VMEM((slab * 3, span, width), jnp.float32),
            pltpu.VMEM((2, 19, n + 16, width), jnp.float32),
            pltpu.VMEM((10, n + 16, width), jnp.float32),
            pltpu.VMEM((rows_of((0, 1)), (below.shape[0] - 8) // 7, LANES), jnp.float32),
            pltpu.SemaphoreType.DMA((8 + slab * 3,)),
        ],
        input_output_aliases={} if field is None else {8: 3},
        compiler_params=pltpu.CompilerParams(vmem_limit_bytes=20 * MIB),
        cost_estimate=cost(8_000_000_000),
    )(
        starts_of(below, windows),
        below,
        starts_of(above, windows),
        above,
        total,
        jnp.zeros((slab * 3, ROWS, width), jnp.float32) if carry is None else carry[:, :ROWS],
        jnp.zeros((slab * 3, ROWS, width), jnp.float32) if head is None else head,
        populations,
        jnp.zeros((8, 128), jnp.float32) if field is None else field,
    )


def interior(populations, field):
    slab, width = (populations.shape[0], populations.shape[2])
    pieces = 4
    step = width // pieces

    def kernel(pop_ref, field_ref, out_ref, pop, force, post, out, in_sems, out_sems):
        def fetch(k):
            rows = pl.ds(k * step, step)
            return (
                pltpu.make_async_copy(pop_ref.at[:, :, rows, :], pop.at[:, :, rows, :], in_sems.at[0, k]),
                pltpu.make_async_copy(field_ref.at[:, :, rows, :], force.at[:, :, rows, :], in_sems.at[1, k]),
            )

        for k in range(pieces):
            for copy in fetch(k):
                copy.start()

        ranges = []
        for p in range(slab):
            if p > 0:
                ranges.append((p, 0, 5))
            if p < slab - 1:
                ranges.append((p, 5, 19))
            else:
                ranges.append((p, 10, 19))

        def kept(p):
            return [i for i in range(19) if 0 <= p + velocity_z[i] < slab]

        started = []

        def emit(k, low, high):
            @pl.loop(low // 8, high // 8)
            def _(t):
                for p in range(slab):
                    for i in kept(p):
                        x = velocity_x[i]
                        if x == 0:
                            continue
                        q = p + velocity_z[i]
                        near = pl.ds(pl.multiple_of(t * 8 + (0 if x > 0 else 8), 8), 16)
                        value = post[q, i, near, :]
                        value = value[7:15] if x > 0 else value[1:9]
                        out[q, i, pl.ds(pl.multiple_of(t * 8, 8), 8), :] = value

            for r, (p, begin, end) in enumerate(ranges):
                copy = pltpu.make_async_copy(
                    out.at[p, begin:end, low:high, :],
                    out_ref.at[p, begin:end, low:high, :],
                    out_sems.at[r, k],
                )
                copy.start()
                started.append(copy)

        for k in range(pieces):
            for copy in fetch(k):
                copy.wait()

            @pl.loop(k * step // 8, (k + 1) * step // 8)
            def _(t):
                rows = pl.ds(pl.multiple_of(t * 8, 8), 8)
                padded = pl.ds(pl.multiple_of(t * 8 + 8, 8), 8)
                for p in range(slab):
                    f = [pop[p, i, rows, :] for i in range(19)]
                    moved = collided(f, [force[p, c, rows, :] for c in range(3)], kept(p))
                    for i, value in moved.items():
                        if velocity_y[i]:
                            value = pltpu.roll(value, velocity_y[i] % width, 1)
                        q = p + velocity_z[i]
                        if velocity_x[i]:
                            post[q, i, padded, :] = value
                        else:
                            out[q, i, rows, :] = value

            if k < pieces - 1:
                emit(k, 8 if k == 0 else k * step - 8, (k + 1) * step - 8)
        for p in range(slab):
            for i in kept(p):
                q = p + velocity_z[i]
                if velocity_x[i] > 0:
                    post[q, i, 0:8, :] = post[q, i, width : width + 8, :]
                elif velocity_x[i] < 0:
                    post[q, i, width + 8 : width + 16, :] = post[q, i, 8:16, :]
        emit(pieces - 1, (pieces - 1) * step - 8, width)
        emit(pieces, 0, 8)
        for copy in started:
            copy.wait()

    return pl.pallas_call(
        kernel,
        out_shape=jax.ShapeDtypeStruct(populations.shape, jnp.float32),
        in_specs=[HBM, HBM],
        out_specs=HBM,
        scratch_shapes=[
            pltpu.VMEM(populations.shape, jnp.float32),
            pltpu.VMEM(field.shape, jnp.float32),
            pltpu.VMEM((slab, 19, width + 16, width), jnp.float32),
            pltpu.VMEM(populations.shape, jnp.float32),
            pltpu.SemaphoreType.DMA((2, pieces)),
            pltpu.SemaphoreType.DMA((2 * slab, pieces + 1)),
        ],
        compiler_params=pltpu.CompilerParams(vmem_limit_bytes=36 * MIB),
        name="interior",
        cost_estimate=pl.CostEstimate(flops=0, bytes_accessed=25_000_000, transcendentals=0),
    )(populations, field)


def arrivals(new_populations, lows, highs, edges):
    slab = new_populations.shape[0]
    count = len(lows)

    def kernel(*refs):
        parts, out_ref, sems = (refs[1 : 1 + 2 * count], refs[-2], refs[-1])
        copies = []
        for k, (begin, end) in enumerate(edges):
            for s, (part, plane, item) in enumerate(
                ((parts[k], 0, 0), (parts[count + k], slab - 1, 5))
            ):
                copies.append(
                    pltpu.make_async_copy(
                        part, out_ref.at[plane, item : item + 5, begin:end, :], sems.at[s, k]
                    )
                )
        for copy in copies:
            copy.start()
        for copy in copies:
            copy.wait()

    return pl.pallas_call(
        kernel,
        out_shape=jax.ShapeDtypeStruct(new_populations.shape, jnp.float32),
        in_specs=[HBM] + [VMEM] * (2 * count),
        out_specs=HBM,
        scratch_shapes=[pltpu.SemaphoreType.DMA((2, count))],
        input_output_aliases={0: 0},
        compiler_params=pltpu.CompilerParams(vmem_limit_bytes=8 * MIB),
        name="arrivals",
    )(new_populations, *lows, *highs)


def dispatched(membrane_force, offset, owner, cell, device_count, cells):
    point_count = owner.size
    capacity = 2 * point_count // device_count
    slot_total = device_count * capacity
    owner = owner.reshape(point_count)
    cell = cell.reshape(point_count)
    devices = jnp.arange(device_count, dtype=jnp.int32)
    counts = jnp.sum((owner[None, :] == devices[:, None]).astype(jnp.int32), 1)
    filler_ends = jnp.cumsum(capacity - counts)
    filler = jnp.arange(slot_total - point_count, dtype=jnp.int32)
    filler_owner = jnp.sum((filler[None, :] >= filler_ends[:, None]).astype(jnp.int32), 0)
    span = 2 * cells
    key = jnp.concatenate([owner * span + cell, filler_owner * span + cells])
    payload = jnp.concatenate(
        [membrane_force.reshape(3, point_count), offset.reshape(3, point_count)], 0
    )
    payload = jnp.pad(payload, ((0, 0), (0, slot_total - point_count)))
    ordered = lax.sort(
        (key,) + tuple(payload[i] for i in range(6)), num_keys=1, is_stable=False
    )
    tag = (ordered[0] % span).astype(jnp.float32)
    send = jnp.stack(
        [v.reshape(device_count, capacity) for v in list(ordered[1:]) + [tag]], 1
    )
    got = lax.all_to_all(send, ("ves", "shard"), split_axis=0, concat_axis=0, tiled=True)
    return got.transpose(1, 0, 2).reshape(7, slot_total)


CUTS = (0, 4, 8, 12, 16)


def one_step(displacement, tension, bending, offset, owner, cell, populations):
    membrane_force = membrane(displacement, tension, bending)
    device_count = lax.axis_size("ves") * lax.axis_size("shard")
    slab, width = (populations.shape[0], populations.shape[2])
    cells = slab * width * width
    windows = width // WINDOW
    got = dispatched(membrane_force, offset, owner, cell, device_count, cells)
    tag = got[6].astype(jnp.int32)
    plane, x, y = (tag // (width * width), tag // width % width, tag % width)
    x = (x + LAG) & (width - 1)
    x_bit = bits(slab) + bits(width)
    key = jnp.where(tag >= cells, width << x_bit, (x << x_bit) | (plane << bits(width)) | y)
    bounds = jnp.arange(windows + 1, dtype=jnp.int32) * (WINDOW << x_bit)
    starts = jnp.sum((key[None, :] < bounds[:, None]).astype(jnp.float32), 1)
    ordered = lax.sort(
        (key,) + tuple(got[i] for i in range(6)), num_keys=1, is_stable=False
    )
    columns = list(ordered[1:]) + [ordered[0].astype(jnp.float32)]
    starts = jnp.pad(starts, (0, LANES - windows - 1))
    listed = jnp.concatenate(
        [v.reshape(-1, LANES) for v in columns]
        + [jnp.broadcast_to(starts[None, :], (8, LANES))],
        0,
    )
    below = passed_along(listed, ("ves", "shard"), 1)
    above = passed_along(listed, ("ves", "shard"), -1)
    total = spread_own(listed, slab, width)

    cuts = [cut * windows // CUTS[-1] for cut in CUTS]
    field = carry = head = None
    lows, highs, edges = ([], [], [])
    begin = 0
    for j, (first, last) in enumerate(zip(cuts[:-1], cuts[1:])):
        low, high, carry, field = spread_chunk(
            (below, above), total, carry, head if last == windows else None,
            populations, field, first, last,
        )
        if j == 0:
            head = carry[:, ROWS:]
        edges.append((begin, begin + low.shape[1]))
        begin += low.shape[1]
        lows.append(passed_along(low, ("ves", "shard"), 1))
        highs.append(passed_along(high, ("ves", "shard"), -1))
    new_populations = interior(populations, field)
    new_populations = arrivals(new_populations, lows, highs, edges)
    return (membrane_force, field, new_populations)


def solution(mesh):
    return jax.shard_map(
        one_step,
        mesh=mesh,
        in_specs=(
            P(None, "ves", "shard", None),
            P("ves"),
            P("ves"),
            P(None, "ves", "shard", None),
            P("ves", "shard", None),
            P("ves", "shard", None),
            P(("ves", "shard"), None, None, None),
        ),
        out_specs=(
            P(None, "ves", "shard", None),
            P(("ves", "shard"), None, None, None),
            P(("ves", "shard"), None, None, None),
        ),
        check_vma=False,
    )
```

```python
import math

import jax
import jax.numpy as jnp
from jax import lax
from jax.experimental import pallas as pl
from jax.experimental.pallas import tpu as pltpu
from jax.sharding import PartitionSpec as P


relax_time = 0.8
velocity_x = [0, 1, -1, 0, 0, 0, 1, -1, 0, 0, 0, 1, -1, 0, 0, 1, 1, -1, -1]
velocity_y = [0, 0, 0, 1, -1, 0, 0, 0, 1, -1, 0, 0, 0, 1, -1, 1, -1, 1, -1]
velocity_z = [1, 1, 1, 1, 1, -1, -1, -1, -1, -1, 0, 0, 0, 0, 0, 0, 0, 0, 0]
lattice_weights = [
    1.0 / 18,
    1.0 / 36,
    1.0 / 36,
    1.0 / 36,
    1.0 / 36,
    1.0 / 18,
    1.0 / 36,
    1.0 / 36,
    1.0 / 36,
    1.0 / 36,
    1.0 / 3,
    1.0 / 18,
    1.0 / 18,
    1.0 / 18,
    1.0 / 18,
    1.0 / 36,
    1.0 / 36,
    1.0 / 36,
    1.0 / 36,
]


def passed_along(value, axis, steps):
    count = lax.axis_size(axis)
    pairs = [(source, (source + steps) % count) for source in range(count)]
    return lax.ppermute(value, axis, pairs)


def halos(x, axis, dim, width):
    devices, length = (lax.axis_size(axis), x.shape[dim])
    up = [(i, i + 1) for i in range(devices - 1)]
    down = [(j, i) for i, j in up]
    last = lax.slice_in_dim(x, length - width, length, axis=dim)
    initial = lax.slice_in_dim(x, 0, width, axis=dim)
    return lax.ppermute(last, axis, up), lax.ppermute(initial, axis, down)


WINDOW = 16
ROWS = 24
BLOCK = 256


HALF_PI = 0.5 * math.pi
COSINE = [(-1.0) ** n * HALF_PI ** (2 * n) / math.factorial(2 * n) for n in range(8)]
SINE = [(-1.0) ** n * HALF_PI ** (2 * n + 1) / math.factorial(2 * n + 1) for n in range(8)]


def weights(fraction):
    square = fraction * fraction
    c = jnp.full_like(square, COSINE[-1])
    s = jnp.full_like(square, SINE[-1])
    for n in range(6, -1, -1):
        c = c * square + COSINE[n]
        s = s * square + SINE[n]
    s = s * fraction
    return [0.25 * (1.0 - s), 0.25 * (1.0 + c), 0.25 * (1.0 + s), 0.25 * (1.0 - c)]


def bits(count):
    return (count - 1).bit_length()


LANES = 128
MIB = 1 << 20


def rows_of(planes):
    return 13 + 3 * len(planes)


def spread_list(starts, list_ref, acc, table, shift, planes, slab, ranges):
    width = acc.shape[2]
    count = table.shape[1]
    row_id = lax.broadcasted_iota(jnp.int32, (ROWS, LANES), 0).astype(jnp.float32)
    y_id = lax.broadcasted_iota(jnp.int32, (width, LANES), 0).astype(jnp.bfloat16)

    def prepare(t):
        at = pl.ds(pl.multiple_of(t * 8, 8), 8)
        part = [list_ref[pl.ds(pl.multiple_of(c * count + t * 8, 8), 8), :] for c in range(7)]
        key = part[6].astype(jnp.int32)
        y = key & (width - 1)
        plane = (key >> bits(width)) & (slab - 1)
        table[0, at, :] = (key >> (bits(width) + bits(slab))).astype(jnp.float32)
        phi_x, phi_y, phi_z = (weights(part[c]) for c in (3, 4, 5))
        for k in range(4):
            table[1 + k, at, :] = phi_x[k]
            table[5 + k, at, :] = phi_y[k]
            table[9 + k, at, :] = ((y + (k - 1)) & (width - 1)).astype(jnp.float32)
        for n, q in enumerate(planes):
            rel = q + 1 + shift - plane
            weight = jnp.zeros_like(part[0])
            for k in range(4):
                weight = jnp.where(rel == k, phi_z[k], weight)
            for c in range(3):
                table[13 + n * 3 + c, at, :] = part[c] * weight

    def half(r, base):
        def row(i, like):
            return jnp.broadcast_to(table[i, pl.ds(r, 1), :], like.shape)

        def narrow(i):
            return jnp.broadcast_to(table[i, pl.ds(r, 1), :].astype(jnp.bfloat16), y_id.shape)

        right = jnp.zeros(y_id.shape, jnp.bfloat16)
        for k in range(4):
            right = jnp.where(y_id == narrow(9 + k), narrow(5 + k), right)
        x = table[0, pl.ds(r, 1), :] - base
        x = jnp.where((x >= 0.0) & (x < WINDOW), x, 4.0 * ROWS)
        rel = row_id - x
        weight_x = jnp.zeros(row_id.shape, jnp.float32)
        for k in range(4):
            weight_x = jnp.where(rel == k, row(1 + k, row_id), weight_x)
        lefts = [row(13 + i, row_id) * weight_x for i in range(3 * len(planes))]
        return jnp.concatenate(lefts, 0).astype(jnp.bfloat16), right

    def window(w, offset):
        begin = starts[w] // BLOCK
        end = (starts[w + 1] + (BLOCK - 1)) // BLOCK
        base = (w * WINDOW).astype(jnp.float32)
        at_row = (w + offset) * WINDOW

        @pl.loop(begin, end)
        def _(b):
            parts = [half(b * (BLOCK // LANES) + h, base) for h in range(BLOCK // LANES)]
            product = lax.dot_general(
                jnp.concatenate([p[0] for p in parts], 1),
                jnp.concatenate([p[1] for p in parts], 1),
                (((1,), (1,)), ((), ())),
                preferred_element_type=jnp.float32,
            )
            rows = pl.ds(pl.multiple_of(at_row, 8), ROWS)
            for n, q in enumerate(planes):
                for c in range(3):
                    i = n * 3 + c
                    acc[q * 3 + c, rows, :] += product[i * ROWS : (i + 1) * ROWS]

    for first, last, offset in ranges:
        unit = 8 * LANES
        low = starts[first] // BLOCK * BLOCK // unit
        high = (starts[last] + (BLOCK - 1)) // BLOCK * BLOCK

        @pl.loop(low, (high + (unit - 1)) // unit)
        def _(t):
            prepare(t)

        @pl.loop(first, last)
        def _(w):
            window(w, offset)


VMEM = pl.BlockSpec(memory_space=pltpu.VMEM)
SMEM = pl.BlockSpec(memory_space=pltpu.SMEM)


def cost(flops):
    return pl.CostEstimate(flops=flops, bytes_accessed=4_000_000, transcendentals=0)


def starts_of(listed, windows):
    return listed[-8, : windows + 1].astype(jnp.int32)


def spread_own(listed, slab, width):
    windows = width // WINDOW

    count = (listed.shape[0] - 8) // 7
    assert count % 8 == 0

    def kernel(starts, list_ref, acc, table):
        acc[...] = jnp.zeros_like(acc)
        spread_list(starts, list_ref, acc, table, 0, range(slab), slab, [(0, windows, 0)])

    return pl.pallas_call(
        kernel,
        out_shape=jax.ShapeDtypeStruct((slab * 3, width + ROWS - WINDOW, width), jnp.float32),
        in_specs=[SMEM, VMEM],
        out_specs=VMEM,
        scratch_shapes=[pltpu.VMEM((rows_of(range(slab)), count, LANES), jnp.float32)],
        compiler_params=pltpu.CompilerParams(vmem_limit_bytes=12 * MIB),
        name="spread_own",
        cost_estimate=cost(20_000_000_000),
    )(starts_of(listed, windows), listed)


ANY = pl.BlockSpec(memory_space=pl.ANY)
HBM = pl.BlockSpec(memory_space=pltpu.HBM)
LAG = 7
KEEP = 1.0 - 1.0 / relax_time
FORCING = 1.0 - 0.5 / relax_time


def collided(f, force, items):
    def along(vector, item, start=None):
        total = start
        for e, v in zip((velocity_x[item], velocity_y[item], velocity_z[item]), vector):
            if e == 0:
                continue
            if total is None:
                total = v if e > 0 else -v
            else:
                total = total + v if e > 0 else total - v
        return total

    def tree(values):
        while len(values) > 1:
            values = [
                values[i] + values[i + 1] if i + 1 < len(values) else values[i]
                for i in range(0, len(values), 2)
            ]
        return values[0]

    density = tree(list(f))
    inverse = 1.0 / density
    flow = []
    for axis, table in enumerate((velocity_x, velocity_y, velocity_z)):
        plus = tree([f[i] for i in range(19) if table[i] > 0])
        minus = tree([f[i] for i in range(19) if table[i] < 0])
        flow.append(((plus - minus) + 0.5 * force[axis]) * inverse)
    speed_sq = flow[0] * flow[0] + flow[1] * flow[1] + flow[2] * flow[2]
    work = flow[0] * force[0] + flow[1] * force[1] + flow[2] * force[2]
    scaled = density * (1.0 / relax_time)
    base = scaled - (1.5 * scaled) * speed_sq - (3.0 * FORCING) * work
    linear = 3.0 * scaled
    square = 4.5 * scaled
    pushed = [3.0 * FORCING * v for v in force]
    result = {}
    for item in items:
        cu = along(flow, item)
        if cu is None:
            bracket = base
        else:
            facing = along(pushed, item)
            bracket = base + facing + cu * (linear + square * cu + 3.0 * facing)
        result[item] = KEEP * f[item] + lattice_weights[item] * bracket
    return result


def spread_chunk(lists, total, carry, head, populations, field, first, last):
    below, above = lists
    slab, width = (populations.shape[0], populations.shape[2])
    windows = width // WINDOW
    opening, closing = (first == 0, last == windows)
    begin = 0 if opening else (first - 1) * WINDOW
    end = width if closing else (last - 1) * WINDOW
    n = end - begin
    span = n + ROWS
    planes = (slab - 1, 0)

    def kernel(s0, l0, s1, l1, total_ref, carry_ref, head_ref, pop_ref, field_in, *rest):
        low, high, carry_out, field_out, acc, pop, post, table, sems = rest
        del field_in
        copies = []

        def fetch(source, target):
            copy = pltpu.make_async_copy(source, target, sems.at[len(copies)])
            copy.start()
            copies.append(copy)

        got = 0
        if not opening:
            fetch(carry_ref, acc.at[:, 0:ROWS, :])
            got = ROWS
        stop = min(span, width + ROWS - WINDOW - begin)
        fetch(total_ref.at[:, begin + got : begin + stop, :], acc.at[:, got:stop, :])
        early = len(copies)
        for n_plane, plane in enumerate(planes):
            for x in range(0, 3):
                source, target, size = (
                    ((begin - 8) % width, 0, 8),
                    (begin, 8, n),
                    (end % width, n + 8, 8),
                )[x]
                fetch(
                    pop_ref.at[plane, :, source : source + size, :],
                    pop.at[n_plane, :, target : target + size, :],
                )
        for copy in copies[:early]:
            copy.wait()
        if closing:
            acc[:, stop:span, :] = jnp.zeros((slab * 3, span - stop, width), jnp.float32)
        moves = (first, last, 0 if opening else 1 - first)
        spread_list(s0, l0, acc, table, slab, (0, 1), slab, [moves])
        spread_list(s1, l1, acc, table, -slab, (slab - 1,), slab, [moves])
        if closing:
            acc[:, n : n + 16, :] += head_ref[:, 0:16, :]
        if opening:
            carry_out[:, ROWS : 2 * ROWS, :] = acc[:, 0:ROWS, :]
            carry_out[:, 0:ROWS, :] = acc[:, n : n + ROWS, :]
        elif not closing:
            carry_out[:, 0:ROWS, :] = acc[:, n : n + ROWS, :]
        else:
            carry_out[...] = jnp.zeros_like(carry_out)
        written = [
            pltpu.make_async_copy(
                acc.at[i, 8 : 8 + n, :],
                field_out.at[i // 3, i % 3, begin:end, :],
                sems.at[len(copies) + i],
            )
            for i in range(slab * 3)
        ]
        for copy in written:
            copy.start()
        for copy in copies[early:]:
            copy.wait()

        @pl.loop(0, (n + 16) // 8)
        def _(t):
            rows = pl.ds(pl.multiple_of(t * 8, 8), 8)
            for n_plane, plane in enumerate(planes):
                f = [pop[n_plane, i, rows, :] for i in range(19)]
                force = [acc[plane * 3 + c, rows, :] for c in range(3)]
                items = range(n_plane * 5, n_plane * 5 + 5)
                for i, value in collided(f, force, items).items():
                    post[i, rows, :] = value

        for target, begin_item in ((low, 0), (high, 5)):
            for i in range(5):
                item = begin_item + i
                at = 8 - velocity_x[item]
                value = post[item, at : at + n, :]
                if velocity_y[item]:
                    value = pltpu.roll(value, velocity_y[item] % width, 1)
                target[i] = value
        for copy in written:
            copy.wait()

    shape = jax.ShapeDtypeStruct
    return pl.pallas_call(
        kernel,
        out_shape=(
            shape((5, n, width), jnp.float32),
            shape((5, n, width), jnp.float32),
            shape((slab * 3, 2 * ROWS, width), jnp.float32),
            shape((slab, 3, width, width), jnp.float32),
        ),
        in_specs=[SMEM, VMEM, SMEM, VMEM, HBM, ANY, VMEM, HBM, HBM],
        out_specs=(VMEM, VMEM, VMEM, HBM),
        scratch_shapes=[
            pltpu.VMEM((slab * 3, span, width), jnp.float32),
            pltpu.VMEM((2, 19, n + 16, width), jnp.float32),
            pltpu.VMEM((10, n + 16, width), jnp.float32),
            pltpu.VMEM((rows_of((0, 1)), (below.shape[0] - 8) // 7, LANES), jnp.float32),
            pltpu.SemaphoreType.DMA((8 + slab * 3,)),
        ],
        input_output_aliases={} if field is None else {8: 3},
        compiler_params=pltpu.CompilerParams(vmem_limit_bytes=20 * MIB),
        cost_estimate=cost(8_000_000_000),
    )(
        starts_of(below, windows),
        below,
        starts_of(above, windows),
        above,
        total,
        jnp.zeros((slab * 3, ROWS, width), jnp.float32) if carry is None else carry[:, :ROWS],
        jnp.zeros((slab * 3, ROWS, width), jnp.float32) if head is None else head,
        populations,
        jnp.zeros((8, 128), jnp.float32) if field is None else field,
    )


def interior(populations, field):
    slab, width = (populations.shape[0], populations.shape[2])
    pieces = 4
    step = width // pieces

    def kernel(pop_ref, field_ref, out_ref, pop, force, post, out, in_sems, out_sems):
        def fetch(k):
            rows = pl.ds(k * step, step)
            return (
                pltpu.make_async_copy(pop_ref.at[:, :, rows, :], pop.at[:, :, rows, :], in_sems.at[0, k]),
                pltpu.make_async_copy(field_ref.at[:, :, rows, :], force.at[:, :, rows, :], in_sems.at[1, k]),
            )

        for k in range(pieces):
            for copy in fetch(k):
                copy.start()

        ranges = []
        for p in range(slab):
            if p > 0:
                ranges.append((p, 0, 5))
            if p < slab - 1:
                ranges.append((p, 5, 19))
            else:
                ranges.append((p, 10, 19))

        def kept(p):
            return [i for i in range(19) if 0 <= p + velocity_z[i] < slab]

        started = []

        def emit(k, low, high):
            @pl.loop(low // 8, high // 8)
            def _(t):
                for p in range(slab):
                    for i in kept(p):
                        x = velocity_x[i]
                        if x == 0:
                            continue
                        q = p + velocity_z[i]
                        near = pl.ds(pl.multiple_of(t * 8 + (0 if x > 0 else 8), 8), 16)
                        value = post[q, i, near, :]
                        value = value[7:15] if x > 0 else value[1:9]
                        out[q, i, pl.ds(pl.multiple_of(t * 8, 8), 8), :] = value

            for r, (p, begin, end) in enumerate(ranges):
                copy = pltpu.make_async_copy(
                    out.at[p, begin:end, low:high, :],
                    out_ref.at[p, begin:end, low:high, :],
                    out_sems.at[r, k],
                )
                copy.start()
                started.append(copy)

        for k in range(pieces):
            for copy in fetch(k):
                copy.wait()

            @pl.loop(k * step // 8, (k + 1) * step // 8)
            def _(t):
                rows = pl.ds(pl.multiple_of(t * 8, 8), 8)
                padded = pl.ds(pl.multiple_of(t * 8 + 8, 8), 8)
                for p in range(slab):
                    f = [pop[p, i, rows, :] for i in range(19)]
                    moved = collided(f, [force[p, c, rows, :] for c in range(3)], kept(p))
                    for i, value in moved.items():
                        if velocity_y[i]:
                            value = pltpu.roll(value, velocity_y[i] % width, 1)
                        q = p + velocity_z[i]
                        if velocity_x[i]:
                            post[q, i, padded, :] = value
                        else:
                            out[q, i, rows, :] = value

            if k < pieces - 1:
                emit(k, 8 if k == 0 else k * step - 8, (k + 1) * step - 8)
        for p in range(slab):
            for i in kept(p):
                q = p + velocity_z[i]
                if velocity_x[i] > 0:
                    post[q, i, 0:8, :] = post[q, i, width : width + 8, :]
                elif velocity_x[i] < 0:
                    post[q, i, width + 8 : width + 16, :] = post[q, i, 8:16, :]
        emit(pieces - 1, (pieces - 1) * step - 8, width)
        emit(pieces, 0, 8)
        for copy in started:
            copy.wait()

    return pl.pallas_call(
        kernel,
        out_shape=jax.ShapeDtypeStruct(populations.shape, jnp.float32),
        in_specs=[HBM, HBM],
        out_specs=HBM,
        scratch_shapes=[
            pltpu.VMEM(populations.shape, jnp.float32),
            pltpu.VMEM(field.shape, jnp.float32),
            pltpu.VMEM((slab, 19, width + 16, width), jnp.float32),
            pltpu.VMEM(populations.shape, jnp.float32),
            pltpu.SemaphoreType.DMA((2, pieces)),
            pltpu.SemaphoreType.DMA((2 * slab, pieces + 1)),
        ],
        compiler_params=pltpu.CompilerParams(vmem_limit_bytes=36 * MIB),
        name="interior",
        cost_estimate=pl.CostEstimate(flops=0, bytes_accessed=25_000_000, transcendentals=0),
    )(populations, field)


def arrivals(new_populations, lows, highs, edges):
    slab = new_populations.shape[0]
    count = len(lows)

    def kernel(*refs):
        parts, out_ref, sems = (refs[1 : 1 + 2 * count], refs[-2], refs[-1])
        copies = []
        for k, (begin, end) in enumerate(edges):
            for s, (part, plane, item) in enumerate(
                ((parts[k], 0, 0), (parts[count + k], slab - 1, 5))
            ):
                copies.append(
                    pltpu.make_async_copy(
                        part, out_ref.at[plane, item : item + 5, begin:end, :], sems.at[s, k]
                    )
                )
        for copy in copies:
            copy.start()
        for copy in copies:
            copy.wait()

    return pl.pallas_call(
        kernel,
        out_shape=jax.ShapeDtypeStruct(new_populations.shape, jnp.float32),
        in_specs=[HBM] + [VMEM] * (2 * count),
        out_specs=HBM,
        scratch_shapes=[pltpu.SemaphoreType.DMA((2, count))],
        input_output_aliases={0: 0},
        compiler_params=pltpu.CompilerParams(vmem_limit_bytes=8 * MIB),
        name="arrivals",
    )(new_populations, *lows, *highs)


def prepared(displacement, tension, bending, offset, owner, cell, cells, width):
    before, after = halos(displacement, "shard", 2, 2)
    _, vesicles, rows, lanes = displacement.shape
    assert lanes == LANES
    index = lax.axis_index("shard")
    outside = jnp.stack(
        [
            jnp.where(index == 0, 0, -1),
            jnp.where(index == lax.axis_size("shard") - 1, rows + 1, -1),
        ]
    ).astype(jnp.int32)
    slab_bits = bits(cells // (width * width))

    def kernel(edge, t_ref, b_ref, x_ref, before_ref, after_ref, o_ref, own_ref, cell_ref, *rest):
        force_ref, key_ref = rest[:2]
        values, (padded, wide_ref) = (rest[2:8], rest[8:])
        place = lax.broadcasted_iota(jnp.int32, (rows + 2, lanes), 0)

        def laplacian(ref, begin, count):
            center = ref[begin : begin + count, :]
            return (
                ref[begin + 1 : begin + count + 1, :]
                + ref[begin - 1 : begin + count - 1, :]
                + pltpu.roll(center, 1, 1)
                + pltpu.roll(center, lanes - 1, 1)
                - 4.0 * center
            )

        for v in range(vesicles):
            at = slice(v * rows, (v + 1) * rows)
            code = cell_ref[v]
            plane, x, y = (
                code >> (2 * bits(width)),
                (code >> bits(width)) & (width - 1),
                code & (width - 1),
            )
            x = (x + LAG) & (width - 1)
            key_ref[at, :] = own_ref[v] * cells + (
                (x << (bits(width) + slab_bits)) | (plane << bits(width)) | y
            )
            for c in range(3):
                values[3 + c][at, :] = o_ref[c, v]
                padded[6:8, :] = before_ref[c, v]
                padded[8 : 8 + rows, :] = x_ref[c, v]
                padded[8 + rows : 10 + rows, :] = after_ref[c, v]
                wide = laplacian(padded, 7, rows + 2)
                hidden = (place == edge[0]) | (place == edge[1])
                wide_ref[7 : 9 + rows, :] = jnp.where(hidden, 0.0, wide)
                second = laplacian(wide_ref, 8, rows)
                force = t_ref[v] * wide_ref[8 : 8 + rows, :] - b_ref[v] * second
                force_ref[c, v] = force
                values[c][at, :] = force

    shape = jax.ShapeDtypeStruct
    flat = (vesicles * rows, lanes)
    out = pl.pallas_call(
        kernel,
        out_shape=(shape(displacement.shape, jnp.float32), shape(flat, jnp.int32))
        + (shape(flat, jnp.float32),) * 6,
        in_specs=[SMEM] * 3 + [VMEM] * 6,
        out_specs=(VMEM,) * 8,
        scratch_shapes=[pltpu.VMEM((rows + 16, lanes), jnp.float32)] * 2,
        compiler_params=pltpu.CompilerParams(vmem_limit_bytes=8 * MIB),
        name="prepared",
    )(outside, tension, bending, displacement, before, after, offset, owner, cell)
    return out[0], out[1], out[2:]


def packed(starts, columns, device_count, capacity, cells):
    count = columns[0].shape[0]
    lanes = min(capacity, LANES)
    tiles = capacity // lanes

    def kernel(start_ref, *refs):
        columns, out, table = (refs[:7], refs[7], refs[8])
        for i in range(7):
            table[0:count, i, :] = columns[i][...].astype(jnp.float32)
        field = lax.broadcasted_iota(jnp.int32, (7, LANES), 0)
        lane = lax.broadcasted_iota(jnp.int32, (7, LANES), 1)
        for r in range(tiles + 1):
            table[count + r] = jnp.where(field == 0, float(device_count * cells), 0.0)

        @pl.loop(0, device_count)
        def _(d):
            row, shift = (start_ref[d] // LANES, start_ref[d] % LANES)
            turned = [
                pltpu.roll(table[row + j], (LANES - shift) % LANES, 1) for j in range(tiles + 1)
            ]
            before = (d * cells).astype(jnp.float32)
            for j in range(tiles):
                value = jnp.where(lane < LANES - shift, turned[j], turned[j + 1])
                tag = jnp.minimum(value - before, float(cells))
                out[d, j] = jnp.where(field == 0, tag, value)[:, :lanes]

    return pl.pallas_call(
        kernel,
        out_shape=jax.ShapeDtypeStruct((device_count, tiles, 7, lanes), jnp.float32),
        in_specs=[SMEM] + [VMEM] * 7,
        out_specs=VMEM,
        scratch_shapes=[pltpu.VMEM((count + tiles + 1, 7, LANES), jnp.float32)],
        compiler_params=pltpu.CompilerParams(vmem_limit_bytes=8 * MIB),
        name="packed",
    )(starts, *columns)


def dispatched(key, values, owner, device_count, cells):
    capacity = 2 * owner.size // device_count
    devices = jnp.arange(device_count, dtype=jnp.int32)
    starts = jnp.sum((owner.reshape(-1)[None, :] < devices[:, None]).astype(jnp.int32), 1)
    ordered = lax.sort(
        (key.reshape(-1),) + tuple(v.reshape(-1) for v in values), num_keys=1, is_stable=False
    )
    send = packed(
        starts, [v.reshape(-1, LANES) for v in ordered], device_count, capacity, cells
    )
    return lax.all_to_all(send, ("ves", "shard"), split_axis=0, concat_axis=0, tiled=True)


CUTS = (0, 4, 8, 12, 16)


def one_step(displacement, tension, bending, offset, owner, cell, populations):
    device_count = lax.axis_size("ves") * lax.axis_size("shard")
    slab, width = (populations.shape[0], populations.shape[2])
    cells = slab * width * width
    windows = width // WINDOW
    x_bit = bits(slab) + bits(width)
    membrane_force, key, values = prepared(
        displacement, tension, bending, offset, owner, cell, cells, width
    )
    got = dispatched(key, values, owner, device_count, cells)
    got = [got[:, :, i, :].reshape(-1) for i in range(7)]
    key = got[0].astype(jnp.int32)
    bounds = jnp.arange(windows + 1, dtype=jnp.int32) * (WINDOW << x_bit)
    starts = jnp.sum((key[None, :] < bounds[:, None]).astype(jnp.float32), 1)
    ordered = lax.sort(
        (key,) + tuple(got[1:]), num_keys=1, is_stable=False
    )
    columns = list(ordered[1:]) + [ordered[0].astype(jnp.float32)]
    starts = jnp.pad(starts, (0, LANES - windows - 1))
    listed = jnp.concatenate(
        [v.reshape(-1, LANES) for v in columns]
        + [jnp.broadcast_to(starts[None, :], (8, LANES))],
        0,
    )
    below = passed_along(listed, ("ves", "shard"), 1)
    above = passed_along(listed, ("ves", "shard"), -1)
    total = spread_own(listed, slab, width)

    cuts = [cut * windows // CUTS[-1] for cut in CUTS]
    field = carry = head = None
    lows, highs, edges = ([], [], [])
    begin = 0
    for j, (first, last) in enumerate(zip(cuts[:-1], cuts[1:])):
        low, high, carry, field = spread_chunk(
            (below, above), total, carry, head if last == windows else None,
            populations, field, first, last,
        )
        if j == 0:
            head = carry[:, ROWS:]
        edges.append((begin, begin + low.shape[1]))
        begin += low.shape[1]
        lows.append(passed_along(low, ("ves", "shard"), 1))
        highs.append(passed_along(high, ("ves", "shard"), -1))
    new_populations = interior(populations, field)
    new_populations = arrivals(new_populations, lows, highs, edges)
    return (membrane_force, field, new_populations)


def solution(mesh):
    return jax.shard_map(
        one_step,
        mesh=mesh,
        in_specs=(
            P(None, "ves", "shard", None),
            P("ves"),
            P("ves"),
            P(None, "ves", "shard", None),
            P("ves", "shard", None),
            P("ves", "shard", None),
            P(("ves", "shard"), None, None, None),
        ),
        out_specs=(
            P(None, "ves", "shard", None),
            P(("ves", "shard"), None, None, None),
            P(("ves", "shard"), None, None, None),
        ),
        check_vma=False,
    )
```

```python
import math

import jax
import jax.numpy as jnp
from jax import lax
from jax.experimental import pallas as pl
from jax.experimental.pallas import tpu as pltpu
from jax.sharding import PartitionSpec as P


relax_time = 0.8
velocity_x = [0, 1, -1, 0, 0, 0, 1, -1, 0, 0, 0, 1, -1, 0, 0, 1, 1, -1, -1]
velocity_y = [0, 0, 0, 1, -1, 0, 0, 0, 1, -1, 0, 0, 0, 1, -1, 1, -1, 1, -1]
velocity_z = [1, 1, 1, 1, 1, -1, -1, -1, -1, -1, 0, 0, 0, 0, 0, 0, 0, 0, 0]
lattice_weights = [
    1.0 / 18,
    1.0 / 36,
    1.0 / 36,
    1.0 / 36,
    1.0 / 36,
    1.0 / 18,
    1.0 / 36,
    1.0 / 36,
    1.0 / 36,
    1.0 / 36,
    1.0 / 3,
    1.0 / 18,
    1.0 / 18,
    1.0 / 18,
    1.0 / 18,
    1.0 / 36,
    1.0 / 36,
    1.0 / 36,
    1.0 / 36,
]


def passed_along(value, axis, steps):
    count = lax.axis_size(axis)
    pairs = [(source, (source + steps) % count) for source in range(count)]
    return lax.ppermute(value, axis, pairs)


def halos(x, axis, dim, width):
    devices, length = (lax.axis_size(axis), x.shape[dim])
    up = [(i, i + 1) for i in range(devices - 1)]
    down = [(j, i) for i, j in up]
    last = lax.slice_in_dim(x, length - width, length, axis=dim)
    initial = lax.slice_in_dim(x, 0, width, axis=dim)
    return lax.ppermute(last, axis, up), lax.ppermute(initial, axis, down)


WINDOW = 16
ROWS = 24
BLOCK = 256


HALF_PI = 0.5 * math.pi
COSINE = [(-1.0) ** n * HALF_PI ** (2 * n) / math.factorial(2 * n) for n in range(8)]
SINE = [(-1.0) ** n * HALF_PI ** (2 * n + 1) / math.factorial(2 * n + 1) for n in range(8)]


def weights(fraction):
    square = fraction * fraction
    c = jnp.full_like(square, COSINE[-1])
    s = jnp.full_like(square, SINE[-1])
    for n in range(6, -1, -1):
        c = c * square + COSINE[n]
        s = s * square + SINE[n]
    s = s * fraction
    return [0.25 * (1.0 - s), 0.25 * (1.0 + c), 0.25 * (1.0 + s), 0.25 * (1.0 - c)]


def bits(count):
    return (count - 1).bit_length()


LANES = 128
MIB = 1 << 20


def rows_of(planes):
    return 13 + 3 * len(planes)


def spread_list(starts, list_ref, acc, table, shift, planes, slab, ranges):
    width = acc.shape[2]
    count = table.shape[1]
    row_id = lax.broadcasted_iota(jnp.int32, (ROWS, LANES), 0).astype(jnp.float32)
    y_id = lax.broadcasted_iota(jnp.int32, (width, LANES), 0).astype(jnp.bfloat16)

    def prepare(t):
        at = pl.ds(pl.multiple_of(t * 8, 8), 8)
        part = [list_ref[pl.ds(pl.multiple_of(c * count + t * 8, 8), 8), :] for c in range(7)]
        key = part[6].astype(jnp.int32)
        y = key & (width - 1)
        plane = (key >> bits(width)) & (slab - 1)
        table[0, at, :] = (key >> (bits(width) + bits(slab))).astype(jnp.float32)
        phi_x, phi_y, phi_z = (weights(part[c]) for c in (3, 4, 5))
        for k in range(4):
            table[1 + k, at, :] = phi_x[k]
            table[5 + k, at, :] = phi_y[k]
            table[9 + k, at, :] = ((y + (k - 1)) & (width - 1)).astype(jnp.float32)
        for n, q in enumerate(planes):
            rel = q + 1 + shift - plane
            weight = jnp.zeros_like(part[0])
            for k in range(4):
                weight = jnp.where(rel == k, phi_z[k], weight)
            for c in range(3):
                table[13 + n * 3 + c, at, :] = part[c] * weight

    def half(r, base):
        def row(i, like):
            return jnp.broadcast_to(table[i, pl.ds(r, 1), :], like.shape)

        def narrow(i):
            return jnp.broadcast_to(table[i, pl.ds(r, 1), :].astype(jnp.bfloat16), y_id.shape)

        right = jnp.zeros(y_id.shape, jnp.bfloat16)
        for k in range(4):
            right = jnp.where(y_id == narrow(9 + k), narrow(5 + k), right)
        x = table[0, pl.ds(r, 1), :] - base
        x = jnp.where((x >= 0.0) & (x < WINDOW), x, 4.0 * ROWS)
        rel = row_id - x
        weight_x = jnp.zeros(row_id.shape, jnp.float32)
        for k in range(4):
            weight_x = jnp.where(rel == k, row(1 + k, row_id), weight_x)
        lefts = [row(13 + i, row_id) * weight_x for i in range(3 * len(planes))]
        return jnp.concatenate(lefts, 0).astype(jnp.bfloat16), right

    def window(w, offset):
        begin = starts[w] // BLOCK
        end = (starts[w + 1] + (BLOCK - 1)) // BLOCK
        base = (w * WINDOW).astype(jnp.float32)
        at_row = (w + offset) * WINDOW

        @pl.loop(begin, end)
        def _(b):
            parts = [half(b * (BLOCK // LANES) + h, base) for h in range(BLOCK // LANES)]
            product = lax.dot_general(
                jnp.concatenate([p[0] for p in parts], 1),
                jnp.concatenate([p[1] for p in parts], 1),
                (((1,), (1,)), ((), ())),
                preferred_element_type=jnp.float32,
            )
            rows = pl.ds(pl.multiple_of(at_row, 8), ROWS)
            for n, q in enumerate(planes):
                for c in range(3):
                    i = n * 3 + c
                    acc[q * 3 + c, rows, :] += product[i * ROWS : (i + 1) * ROWS]

    for first, last, offset in ranges:
        unit = 8 * LANES
        low = starts[first] // BLOCK * BLOCK // unit
        high = (starts[last] + (BLOCK - 1)) // BLOCK * BLOCK

        @pl.loop(low, (high + (unit - 1)) // unit)
        def _(t):
            prepare(t)

        @pl.loop(first, last)
        def _(w):
            window(w, offset)


VMEM = pl.BlockSpec(memory_space=pltpu.VMEM)
SMEM = pl.BlockSpec(memory_space=pltpu.SMEM)


def cost(flops):
    return pl.CostEstimate(flops=flops, bytes_accessed=4_000_000, transcendentals=0)


def starts_of(listed, windows):
    return listed[-8, : windows + 1].astype(jnp.int32)


def spread_own(listed, slab, width):
    windows = width // WINDOW

    count = (listed.shape[0] - 8) // 7
    assert count % 8 == 0

    def kernel(starts, list_ref, acc, table):
        acc[...] = jnp.zeros_like(acc)
        spread_list(starts, list_ref, acc, table, 0, range(slab), slab, [(0, windows, 0)])

    return pl.pallas_call(
        kernel,
        out_shape=jax.ShapeDtypeStruct((slab * 3, width + ROWS - WINDOW, width), jnp.float32),
        in_specs=[SMEM, VMEM],
        out_specs=VMEM,
        scratch_shapes=[pltpu.VMEM((rows_of(range(slab)), count, LANES), jnp.float32)],
        compiler_params=pltpu.CompilerParams(vmem_limit_bytes=12 * MIB),
        name="spread_own",
        cost_estimate=cost(20_000_000_000),
    )(starts_of(listed, windows), listed)


ANY = pl.BlockSpec(memory_space=pl.ANY)
HBM = pl.BlockSpec(memory_space=pltpu.HBM)
LAG = 7
KEEP = 1.0 - 1.0 / relax_time
FORCING = 1.0 - 0.5 / relax_time


def collided(f, force, items):
    def along(vector, item, start=None):
        total = start
        for e, v in zip((velocity_x[item], velocity_y[item], velocity_z[item]), vector):
            if e == 0:
                continue
            if total is None:
                total = v if e > 0 else -v
            else:
                total = total + v if e > 0 else total - v
        return total

    def tree(values):
        while len(values) > 1:
            values = [
                values[i] + values[i + 1] if i + 1 < len(values) else values[i]
                for i in range(0, len(values), 2)
            ]
        return values[0]

    density = tree(list(f))
    inverse = 1.0 / density
    flow = []
    for axis, table in enumerate((velocity_x, velocity_y, velocity_z)):
        plus = tree([f[i] for i in range(19) if table[i] > 0])
        minus = tree([f[i] for i in range(19) if table[i] < 0])
        flow.append(((plus - minus) + 0.5 * force[axis]) * inverse)
    speed_sq = flow[0] * flow[0] + flow[1] * flow[1] + flow[2] * flow[2]
    work = flow[0] * force[0] + flow[1] * force[1] + flow[2] * force[2]
    scaled = density * (1.0 / relax_time)
    base = scaled - (1.5 * scaled) * speed_sq - (3.0 * FORCING) * work
    linear = 3.0 * scaled
    square = 4.5 * scaled
    pushed = [3.0 * FORCING * v for v in force]
    result = {}
    for item in items:
        cu = along(flow, item)
        if cu is None:
            bracket = base
        else:
            facing = along(pushed, item)
            bracket = base + facing + cu * (linear + square * cu + 3.0 * facing)
        result[item] = KEEP * f[item] + lattice_weights[item] * bracket
    return result


def spread_chunk(lists, total, carry, head, populations, field, first, last):
    below, above = lists
    slab, width = (populations.shape[0], populations.shape[2])
    windows = width // WINDOW
    opening, closing = (first == 0, last == windows)
    begin = 0 if opening else (first - 1) * WINDOW
    end = width if closing else (last - 1) * WINDOW
    n = end - begin
    span = n + ROWS
    planes = (slab - 1, 0)

    def kernel(s0, l0, s1, l1, total_ref, carry_ref, head_ref, pop_ref, field_in, *rest):
        low, high, carry_out, field_out, acc, pop, post, table, sems = rest
        del field_in
        copies = []

        def fetch(source, target):
            copy = pltpu.make_async_copy(source, target, sems.at[len(copies)])
            copy.start()
            copies.append(copy)

        got = 0
        if not opening:
            fetch(carry_ref, acc.at[:, 0:ROWS, :])
            got = ROWS
        stop = min(span, width + ROWS - WINDOW - begin)
        fetch(total_ref.at[:, begin + got : begin + stop, :], acc.at[:, got:stop, :])
        early = len(copies)
        for n_plane, plane in enumerate(planes):
            for x in range(0, 3):
                source, target, size = (
                    ((begin - 8) % width, 0, 8),
                    (begin, 8, n),
                    (end % width, n + 8, 8),
                )[x]
                fetch(
                    pop_ref.at[plane, :, source : source + size, :],
                    pop.at[n_plane, :, target : target + size, :],
                )
        for copy in copies[:early]:
            copy.wait()
        if closing:
            acc[:, stop:span, :] = jnp.zeros((slab * 3, span - stop, width), jnp.float32)
        moves = (first, last, 0 if opening else 1 - first)
        spread_list(s0, l0, acc, table, slab, (0, 1), slab, [moves])
        spread_list(s1, l1, acc, table, -slab, (slab - 1,), slab, [moves])
        if closing:
            acc[:, n : n + 16, :] += head_ref[:, 0:16, :]
        if opening:
            carry_out[:, ROWS : 2 * ROWS, :] = acc[:, 0:ROWS, :]
            carry_out[:, 0:ROWS, :] = acc[:, n : n + ROWS, :]
        elif not closing:
            carry_out[:, 0:ROWS, :] = acc[:, n : n + ROWS, :]
        else:
            carry_out[...] = jnp.zeros_like(carry_out)
        written = [
            pltpu.make_async_copy(
                acc.at[i, 8 : 8 + n, :],
                field_out.at[i // 3, i % 3, begin:end, :],
                sems.at[len(copies) + i],
            )
            for i in range(slab * 3)
        ]
        for copy in written:
            copy.start()
        for copy in copies[early:]:
            copy.wait()

        @pl.loop(0, (n + 16) // 8)
        def _(t):
            rows = pl.ds(pl.multiple_of(t * 8, 8), 8)
            for n_plane, plane in enumerate(planes):
                f = [pop[n_plane, i, rows, :] for i in range(19)]
                force = [acc[plane * 3 + c, rows, :] for c in range(3)]
                items = range(n_plane * 5, n_plane * 5 + 5)
                for i, value in collided(f, force, items).items():
                    post[i, rows, :] = value

        for target, begin_item in ((low, 0), (high, 5)):
            for i in range(5):
                item = begin_item + i
                at = 8 - velocity_x[item]
                value = post[item, at : at + n, :]
                if velocity_y[item]:
                    value = pltpu.roll(value, velocity_y[item] % width, 1)
                target[i] = value
        for copy in written:
            copy.wait()

    shape = jax.ShapeDtypeStruct
    return pl.pallas_call(
        kernel,
        out_shape=(
            shape((5, n, width), jnp.float32),
            shape((5, n, width), jnp.float32),
            shape((slab * 3, 2 * ROWS, width), jnp.float32),
            shape((slab, 3, width, width), jnp.float32),
        ),
        in_specs=[SMEM, VMEM, SMEM, VMEM, HBM, ANY, VMEM, HBM, HBM],
        out_specs=(VMEM, VMEM, VMEM, HBM),
        scratch_shapes=[
            pltpu.VMEM((slab * 3, span, width), jnp.float32),
            pltpu.VMEM((2, 19, n + 16, width), jnp.float32),
            pltpu.VMEM((10, n + 16, width), jnp.float32),
            pltpu.VMEM((rows_of((0, 1)), (below.shape[0] - 8) // 7, LANES), jnp.float32),
            pltpu.SemaphoreType.DMA((8 + slab * 3,)),
        ],
        input_output_aliases={} if field is None else {8: 3},
        compiler_params=pltpu.CompilerParams(vmem_limit_bytes=20 * MIB),
        cost_estimate=cost(8_000_000_000),
    )(
        starts_of(below, windows),
        below,
        starts_of(above, windows),
        above,
        total,
        jnp.zeros((slab * 3, ROWS, width), jnp.float32) if carry is None else carry[:, :ROWS],
        jnp.zeros((slab * 3, ROWS, width), jnp.float32) if head is None else head,
        populations,
        jnp.zeros((8, 128), jnp.float32) if field is None else field,
    )


def interior(populations, field):
    slab, width = (populations.shape[0], populations.shape[2])
    pieces = 4
    step = width // pieces

    def kernel(pop_ref, field_ref, out_ref, pop, force, post, out, in_sems, out_sems):
        def fetch(k):
            rows = pl.ds(k * step, step)
            return (
                pltpu.make_async_copy(pop_ref.at[:, :, rows, :], pop.at[:, :, rows, :], in_sems.at[0, k]),
                pltpu.make_async_copy(field_ref.at[:, :, rows, :], force.at[:, :, rows, :], in_sems.at[1, k]),
            )

        for k in range(pieces):
            for copy in fetch(k):
                copy.start()

        ranges = []
        for p in range(slab):
            if p > 0:
                ranges.append((p, 0, 5))
            if p < slab - 1:
                ranges.append((p, 5, 19))
            else:
                ranges.append((p, 10, 19))

        def kept(p):
            return [i for i in range(19) if 0 <= p + velocity_z[i] < slab]

        started = []

        def emit(k, low, high):
            @pl.loop(low // 8, high // 8)
            def _(t):
                for p in range(slab):
                    for i in kept(p):
                        x = velocity_x[i]
                        if x == 0:
                            continue
                        q = p + velocity_z[i]
                        near = pl.ds(pl.multiple_of(t * 8 + (0 if x > 0 else 8), 8), 16)
                        value = post[q, i, near, :]
                        value = value[7:15] if x > 0 else value[1:9]
                        out[q, i, pl.ds(pl.multiple_of(t * 8, 8), 8), :] = value

            for r, (p, begin, end) in enumerate(ranges):
                copy = pltpu.make_async_copy(
                    out.at[p, begin:end, low:high, :],
                    out_ref.at[p, begin:end, low:high, :],
                    out_sems.at[r, k],
                )
                copy.start()
                started.append(copy)

        for k in range(pieces):
            for copy in fetch(k):
                copy.wait()

            @pl.loop(k * step // 8, (k + 1) * step // 8)
            def _(t):
                rows = pl.ds(pl.multiple_of(t * 8, 8), 8)
                padded = pl.ds(pl.multiple_of(t * 8 + 8, 8), 8)
                for p in range(slab):
                    f = [pop[p, i, rows, :] for i in range(19)]
                    moved = collided(f, [force[p, c, rows, :] for c in range(3)], kept(p))
                    for i, value in moved.items():
                        if velocity_y[i]:
                            value = pltpu.roll(value, velocity_y[i] % width, 1)
                        q = p + velocity_z[i]
                        if velocity_x[i]:
                            post[q, i, padded, :] = value
                        else:
                            out[q, i, rows, :] = value

            if k < pieces - 1:
                emit(k, 8 if k == 0 else k * step - 8, (k + 1) * step - 8)
        for p in range(slab):
            for i in kept(p):
                q = p + velocity_z[i]
                if velocity_x[i] > 0:
                    post[q, i, 0:8, :] = post[q, i, width : width + 8, :]
                elif velocity_x[i] < 0:
                    post[q, i, width + 8 : width + 16, :] = post[q, i, 8:16, :]
        emit(pieces - 1, (pieces - 1) * step - 8, width)
        emit(pieces, 0, 8)
        for copy in started:
            copy.wait()

    return pl.pallas_call(
        kernel,
        out_shape=jax.ShapeDtypeStruct(populations.shape, jnp.float32),
        in_specs=[HBM, HBM],
        out_specs=HBM,
        scratch_shapes=[
            pltpu.VMEM(populations.shape, jnp.float32),
            pltpu.VMEM(field.shape, jnp.float32),
            pltpu.VMEM((slab, 19, width + 16, width), jnp.float32),
            pltpu.VMEM(populations.shape, jnp.float32),
            pltpu.SemaphoreType.DMA((2, pieces)),
            pltpu.SemaphoreType.DMA((2 * slab, pieces + 1)),
        ],
        compiler_params=pltpu.CompilerParams(vmem_limit_bytes=36 * MIB),
        name="interior",
        cost_estimate=pl.CostEstimate(flops=0, bytes_accessed=25_000_000, transcendentals=0),
    )(populations, field)


def arrivals(new_populations, lows, highs, edges):
    slab = new_populations.shape[0]
    count = len(lows)

    def kernel(*refs):
        parts, out_ref, sems = (refs[1 : 1 + 2 * count], refs[-2], refs[-1])
        copies = []
        for k, (begin, end) in enumerate(edges):
            for s, (part, plane, item) in enumerate(
                ((parts[k], 0, 0), (parts[count + k], slab - 1, 5))
            ):
                copies.append(
                    pltpu.make_async_copy(
                        part, out_ref.at[plane, item : item + 5, begin:end, :], sems.at[s, k]
                    )
                )
        for copy in copies:
            copy.start()
        for copy in copies:
            copy.wait()

    return pl.pallas_call(
        kernel,
        out_shape=jax.ShapeDtypeStruct(new_populations.shape, jnp.float32),
        in_specs=[HBM] + [VMEM] * (2 * count),
        out_specs=HBM,
        scratch_shapes=[pltpu.SemaphoreType.DMA((2, count))],
        input_output_aliases={0: 0},
        compiler_params=pltpu.CompilerParams(vmem_limit_bytes=8 * MIB),
        name="arrivals",
    )(new_populations, *lows, *highs)


def prepared(displacement, tension, bending, offset, owner, cell, cells, width):
    before, after = halos(displacement, "shard", 2, 2)
    _, vesicles, rows, lanes = displacement.shape
    assert lanes == LANES
    index = lax.axis_index("shard")
    outside = jnp.stack(
        [
            jnp.where(index == 0, 0, -1),
            jnp.where(index == lax.axis_size("shard") - 1, rows + 1, -1),
        ]
    ).astype(jnp.int32)
    slab_bits = bits(cells // (width * width))

    def kernel(edge, t_ref, b_ref, x_ref, before_ref, after_ref, o_ref, own_ref, cell_ref, *rest):
        force_ref, key_ref = rest[:2]
        values, (padded, wide_ref) = (rest[2:8], rest[8:])
        place = lax.broadcasted_iota(jnp.int32, (rows + 2, lanes), 0)

        def laplacian(ref, begin, count):
            center = ref[begin : begin + count, :]
            return (
                ref[begin + 1 : begin + count + 1, :]
                + ref[begin - 1 : begin + count - 1, :]
                + pltpu.roll(center, 1, 1)
                + pltpu.roll(center, lanes - 1, 1)
                - 4.0 * center
            )

        for v in range(vesicles):
            at = slice(v * rows, (v + 1) * rows)
            code = cell_ref[v]
            plane, x, y = (
                code >> (2 * bits(width)),
                (code >> bits(width)) & (width - 1),
                code & (width - 1),
            )
            x = (x + LAG) & (width - 1)
            key_ref[at, :] = own_ref[v] * cells + (
                (x << (bits(width) + slab_bits)) | (plane << bits(width)) | y
            )
            for c in range(3):
                values[3 + c][at, :] = o_ref[c, v]
                padded[6:8, :] = before_ref[c, v]
                padded[8 : 8 + rows, :] = x_ref[c, v]
                padded[8 + rows : 10 + rows, :] = after_ref[c, v]
                wide = laplacian(padded, 7, rows + 2)
                hidden = (place == edge[0]) | (place == edge[1])
                wide_ref[7 : 9 + rows, :] = jnp.where(hidden, 0.0, wide)
                second = laplacian(wide_ref, 8, rows)
                force = t_ref[v] * wide_ref[8 : 8 + rows, :] - b_ref[v] * second
                force_ref[c, v] = force
                values[c][at, :] = force

    shape = jax.ShapeDtypeStruct
    flat = (vesicles * rows, lanes)
    out = pl.pallas_call(
        kernel,
        out_shape=(shape(displacement.shape, jnp.float32), shape(flat, jnp.int32))
        + (shape(flat, jnp.float32),) * 6,
        in_specs=[SMEM] * 3 + [VMEM] * 6,
        out_specs=(VMEM,) * 8,
        scratch_shapes=[pltpu.VMEM((rows + 16, lanes), jnp.float32)] * 2,
        name="prepared",
    )(outside, tension, bending, displacement, before, after, offset, owner, cell)
    return out[0], out[1], out[2:]


def packed(starts, columns, device_count, capacity, cells):
    count = columns[0].shape[0]
    lanes = min(capacity, LANES)
    tiles = capacity // lanes

    def kernel(start_ref, *refs):
        columns, out, table = (refs[:7], refs[7], refs[8])
        for i in range(7):
            table[0:count, i, :] = columns[i][...].astype(jnp.float32)
        field = lax.broadcasted_iota(jnp.int32, (7, LANES), 0)
        lane = lax.broadcasted_iota(jnp.int32, (7, LANES), 1)
        for r in range(tiles + 1):
            table[count + r] = jnp.where(field == 0, float(device_count * cells), 0.0)

        @pl.loop(0, device_count, unroll=4)
        def _(d):
            row, shift = (start_ref[d] // LANES, start_ref[d] % LANES)
            turned = [
                pltpu.roll(table[row + j], (LANES - shift) % LANES, 1) for j in range(tiles + 1)
            ]
            before = (d * cells).astype(jnp.float32)
            for j in range(tiles):
                value = jnp.where(lane < LANES - shift, turned[j], turned[j + 1])
                tag = jnp.minimum(value - before, float(cells))
                out[d, :, j, :] = jnp.where(field == 0, tag, value)[:, :lanes]

    return pl.pallas_call(
        kernel,
        out_shape=jax.ShapeDtypeStruct((device_count, 7, tiles, lanes), jnp.float32),
        in_specs=[SMEM] + [VMEM] * 7,
        out_specs=VMEM,
        scratch_shapes=[pltpu.VMEM((count + tiles + 1, 7, LANES), jnp.float32)],
        compiler_params=pltpu.CompilerParams(vmem_limit_bytes=8 * MIB),
        name="packed",
    )(starts, *columns)


def dispatched(key, values, owner, device_count, cells):
    capacity = 2 * owner.size // device_count
    devices = jnp.arange(device_count, dtype=jnp.int32)
    starts = jnp.sum((owner.reshape(-1)[None, :] < devices[:, None]).astype(jnp.int32), 1)
    ordered = lax.sort(
        (key.reshape(-1),) + tuple(v.reshape(-1) for v in values), num_keys=1, is_stable=False
    )
    send = packed(
        starts, [v.reshape(-1, LANES) for v in ordered], device_count, capacity, cells
    )
    return lax.all_to_all(send, ("ves", "shard"), split_axis=0, concat_axis=0, tiled=True)


CUTS = (0, 3, 6, 11, 16)


def one_step(displacement, tension, bending, offset, owner, cell, populations):
    device_count = lax.axis_size("ves") * lax.axis_size("shard")
    slab, width = (populations.shape[0], populations.shape[2])
    cells = slab * width * width
    windows = width // WINDOW
    x_bit = bits(slab) + bits(width)
    membrane_force, key, values = prepared(
        displacement, tension, bending, offset, owner, cell, cells, width
    )
    got = dispatched(key, values, owner, device_count, cells)
    got = [got[:, i].reshape(-1) for i in range(7)]
    key = got[0].astype(jnp.int32)
    bounds = jnp.arange(windows + 1, dtype=jnp.int32) * (WINDOW << x_bit)
    starts = jnp.sum((key[None, :] < bounds[:, None]).astype(jnp.float32), 1)
    ordered = lax.sort(
        (key,) + tuple(got[1:]), num_keys=1, is_stable=False
    )
    columns = list(ordered[1:]) + [ordered[0].astype(jnp.float32)]
    starts = jnp.pad(starts, (0, LANES - windows - 1))
    listed = jnp.concatenate(
        [v.reshape(-1, LANES) for v in columns]
        + [jnp.broadcast_to(starts[None, :], (8, LANES))],
        0,
    )
    below = passed_along(listed, ("ves", "shard"), 1)
    above = passed_along(listed, ("ves", "shard"), -1)
    total = spread_own(listed, slab, width)

    cuts = [cut * windows // CUTS[-1] for cut in CUTS]
    field = carry = head = None
    lows, highs, edges = ([], [], [])
    begin = 0
    for j, (first, last) in enumerate(zip(cuts[:-1], cuts[1:])):
        low, high, carry, field = spread_chunk(
            (below, above), total, carry, head if last == windows else None,
            populations, field, first, last,
        )
        if j == 0:
            head = carry[:, ROWS:]
        edges.append((begin, begin + low.shape[1]))
        begin += low.shape[1]
        lows.append(passed_along(low, ("ves", "shard"), 1))
        highs.append(passed_along(high, ("ves", "shard"), -1))
    new_populations = interior(populations, field)
    new_populations = arrivals(new_populations, lows, highs, edges)
    return (membrane_force, field, new_populations)


def solution(mesh):
    return jax.shard_map(
        one_step,
        mesh=mesh,
        in_specs=(
            P(None, "ves", "shard", None),
            P("ves"),
            P("ves"),
            P(None, "ves", "shard", None),
            P("ves", "shard", None),
            P("ves", "shard", None),
            P(("ves", "shard"), None, None, None),
        ),
        out_specs=(
            P(None, "ves", "shard", None),
            P(("ves", "shard"), None, None, None),
            P(("ves", "shard"), None, None, None),
        ),
        check_vma=False,
    )
```

```python
import math

import jax
import jax.numpy as jnp
from jax import lax
from jax.experimental import pallas as pl
from jax.experimental.pallas import tpu as pltpu
from jax.sharding import PartitionSpec as P


relax_time = 0.8
velocity_x = [0, 1, -1, 0, 0, 0, 1, -1, 0, 0, 0, 1, -1, 0, 0, 1, 1, -1, -1]
velocity_y = [0, 0, 0, 1, -1, 0, 0, 0, 1, -1, 0, 0, 0, 1, -1, 1, -1, 1, -1]
velocity_z = [1, 1, 1, 1, 1, -1, -1, -1, -1, -1, 0, 0, 0, 0, 0, 0, 0, 0, 0]
lattice_weights = [
    1.0 / 18,
    1.0 / 36,
    1.0 / 36,
    1.0 / 36,
    1.0 / 36,
    1.0 / 18,
    1.0 / 36,
    1.0 / 36,
    1.0 / 36,
    1.0 / 36,
    1.0 / 3,
    1.0 / 18,
    1.0 / 18,
    1.0 / 18,
    1.0 / 18,
    1.0 / 36,
    1.0 / 36,
    1.0 / 36,
    1.0 / 36,
]


def passed_along(value, axis, steps):
    count = lax.axis_size(axis)
    pairs = [(source, (source + steps) % count) for source in range(count)]
    return lax.ppermute(value, axis, pairs)


def halos(x, axis, dim, width):
    devices, length = (lax.axis_size(axis), x.shape[dim])
    up = [(i, i + 1) for i in range(devices - 1)]
    down = [(j, i) for i, j in up]
    last = lax.slice_in_dim(x, length - width, length, axis=dim)
    initial = lax.slice_in_dim(x, 0, width, axis=dim)
    return lax.ppermute(last, axis, up), lax.ppermute(initial, axis, down)


WINDOW = 16
ROWS = 24
BLOCK = 256


HALF_PI = 0.5 * math.pi
COSINE = [(-1.0) ** n * HALF_PI ** (2 * n) / math.factorial(2 * n) for n in range(8)]
SINE = [(-1.0) ** n * HALF_PI ** (2 * n + 1) / math.factorial(2 * n + 1) for n in range(8)]


def weights(fraction):
    square = fraction * fraction
    c = jnp.full_like(square, COSINE[-1])
    s = jnp.full_like(square, SINE[-1])
    for n in range(6, -1, -1):
        c = c * square + COSINE[n]
        s = s * square + SINE[n]
    s = s * fraction
    return [0.25 * (1.0 - s), 0.25 * (1.0 + c), 0.25 * (1.0 + s), 0.25 * (1.0 - c)]


def bits(count):
    return (count - 1).bit_length()


LANES = 128
MIB = 1 << 20


def rows_of(planes):
    return 13 + 3 * len(planes)


def spread_list(starts, list_ref, acc, table, shift, planes, slab, ranges):
    width = acc.shape[2]
    count = table.shape[1]
    row_id = lax.broadcasted_iota(jnp.int32, (ROWS, LANES), 0).astype(jnp.float32)
    y_id = lax.broadcasted_iota(jnp.int32, (width, LANES), 0).astype(jnp.bfloat16)

    def prepare(t):
        at = pl.ds(pl.multiple_of(t * 8, 8), 8)
        part = [list_ref[pl.ds(pl.multiple_of(c * count + t * 8, 8), 8), :] for c in range(7)]
        key = part[6].astype(jnp.int32)
        y = key & (width - 1)
        plane = (key >> bits(width)) & (slab - 1)
        table[0, at, :] = (key >> (bits(width) + bits(slab))).astype(jnp.float32)
        phi_x, phi_y, phi_z = (weights(part[c]) for c in (3, 4, 5))
        for k in range(4):
            table[1 + k, at, :] = phi_x[k]
            table[5 + k, at, :] = phi_y[k]
            table[9 + k, at, :] = ((y + (k - 1)) & (width - 1)).astype(jnp.float32)
        for n, q in enumerate(planes):
            rel = q + 1 + shift - plane
            weight = jnp.zeros_like(part[0])
            for k in range(4):
                weight = jnp.where(rel == k, phi_z[k], weight)
            for c in range(3):
                table[13 + n * 3 + c, at, :] = part[c] * weight

    def half(r, base):
        def row(i, like):
            return jnp.broadcast_to(table[i, pl.ds(r, 1), :], like.shape)

        def narrow(i):
            return jnp.broadcast_to(table[i, pl.ds(r, 1), :].astype(jnp.bfloat16), y_id.shape)

        right = jnp.zeros(y_id.shape, jnp.bfloat16)
        for k in range(4):
            right = jnp.where(y_id == narrow(9 + k), narrow(5 + k), right)
        x = table[0, pl.ds(r, 1), :] - base
        x = jnp.where((x >= 0.0) & (x < WINDOW), x, 4.0 * ROWS)
        rel = row_id - x
        weight_x = jnp.zeros(row_id.shape, jnp.float32)
        for k in range(4):
            weight_x = jnp.where(rel == k, row(1 + k, row_id), weight_x)
        lefts = [row(13 + i, row_id) * weight_x for i in range(3 * len(planes))]
        return jnp.concatenate(lefts, 0).astype(jnp.bfloat16), right

    def window(w, offset):
        begin = starts[w] // BLOCK
        end = (starts[w + 1] + (BLOCK - 1)) // BLOCK
        base = (w * WINDOW).astype(jnp.float32)
        at_row = (w + offset) * WINDOW

        @pl.loop(begin, end)
        def _(b):
            parts = [half(b * (BLOCK // LANES) + h, base) for h in range(BLOCK // LANES)]
            product = lax.dot_general(
                jnp.concatenate([p[0] for p in parts], 1),
                jnp.concatenate([p[1] for p in parts], 1),
                (((1,), (1,)), ((), ())),
                preferred_element_type=jnp.float32,
            )
            rows = pl.ds(pl.multiple_of(at_row, 8), ROWS)
            for n, q in enumerate(planes):
                for c in range(3):
                    i = n * 3 + c
                    acc[q * 3 + c, rows, :] += product[i * ROWS : (i + 1) * ROWS]

    for first, last, offset in ranges:
        unit = 8 * LANES
        low = starts[first] // BLOCK * BLOCK // unit
        high = (starts[last] + (BLOCK - 1)) // BLOCK * BLOCK

        @pl.loop(low, (high + (unit - 1)) // unit)
        def _(t):
            prepare(t)

        @pl.loop(first, last)
        def _(w):
            window(w, offset)


VMEM = pl.BlockSpec(memory_space=pltpu.VMEM)
SMEM = pl.BlockSpec(memory_space=pltpu.SMEM)


def cost(flops):
    return pl.CostEstimate(flops=flops, bytes_accessed=4_000_000, transcendentals=0)


def starts_of(listed, windows):
    return listed[-8, : windows + 1].astype(jnp.int32)


def spread_own(listed, slab, width):
    windows = width // WINDOW

    count = (listed.shape[0] - 8) // 7
    assert count % 8 == 0

    def kernel(starts, list_ref, acc, table):
        acc[...] = jnp.zeros_like(acc)
        spread_list(starts, list_ref, acc, table, 0, range(slab), slab, [(0, windows, 0)])

    return pl.pallas_call(
        kernel,
        out_shape=jax.ShapeDtypeStruct((slab * 3, width + ROWS - WINDOW, width), jnp.float32),
        in_specs=[SMEM, VMEM],
        out_specs=VMEM,
        scratch_shapes=[pltpu.VMEM((rows_of(range(slab)), count, LANES), jnp.float32)],
        compiler_params=pltpu.CompilerParams(vmem_limit_bytes=12 * MIB),
        name="spread_own",
        cost_estimate=cost(20_000_000_000),
    )(starts_of(listed, windows), listed)


ANY = pl.BlockSpec(memory_space=pl.ANY)
HBM = pl.BlockSpec(memory_space=pltpu.HBM)
LAG = 7
KEEP = 1.0 - 1.0 / relax_time
FORCING = 1.0 - 0.5 / relax_time


def collided(f, force, items):
    def along(vector, item, start=None):
        total = start
        for e, v in zip((velocity_x[item], velocity_y[item], velocity_z[item]), vector):
            if e == 0:
                continue
            if total is None:
                total = v if e > 0 else -v
            else:
                total = total + v if e > 0 else total - v
        return total

    def tree(values):
        while len(values) > 1:
            values = [
                values[i] + values[i + 1] if i + 1 < len(values) else values[i]
                for i in range(0, len(values), 2)
            ]
        return values[0]

    density = tree(list(f))
    inverse = 1.0 / density
    flow = []
    for axis, table in enumerate((velocity_x, velocity_y, velocity_z)):
        plus = tree([f[i] for i in range(19) if table[i] > 0])
        minus = tree([f[i] for i in range(19) if table[i] < 0])
        flow.append(((plus - minus) + 0.5 * force[axis]) * inverse)
    speed_sq = flow[0] * flow[0] + flow[1] * flow[1] + flow[2] * flow[2]
    work = flow[0] * force[0] + flow[1] * force[1] + flow[2] * force[2]
    scaled = density * (1.0 / relax_time)
    base = scaled - (1.5 * scaled) * speed_sq - (3.0 * FORCING) * work
    linear = 3.0 * scaled
    square = 4.5 * scaled
    pushed = [3.0 * FORCING * v for v in force]
    result = {}
    for item in items:
        cu = along(flow, item)
        if cu is None:
            bracket = base
        else:
            facing = along(pushed, item)
            bracket = base + facing + cu * (linear + square * cu + 3.0 * facing)
        result[item] = KEEP * f[item] + lattice_weights[item] * bracket
    return result


def spread_chunk(lists, total, carry, head, populations, field, first, last):
    below, above = lists
    slab, width = (populations.shape[0], populations.shape[2])
    windows = width // WINDOW
    opening, closing = (first == 0, last == windows)
    begin = 0 if opening else (first - 1) * WINDOW
    end = width if closing else (last - 1) * WINDOW
    n = end - begin
    span = n + ROWS
    planes = (slab - 1, 0)

    def kernel(s0, l0, s1, l1, total_ref, carry_ref, head_ref, pop_ref, field_in, *rest):
        low, high, carry_out, field_out, acc, pop, post, table, sems = rest
        del field_in
        copies = []

        def fetch(source, target):
            copy = pltpu.make_async_copy(source, target, sems.at[len(copies)])
            copy.start()
            copies.append(copy)

        got = 0
        if not opening:
            fetch(carry_ref, acc.at[:, 0:ROWS, :])
            got = ROWS
        stop = min(span, width + ROWS - WINDOW - begin)
        fetch(total_ref.at[:, begin + got : begin + stop, :], acc.at[:, got:stop, :])
        early = len(copies)
        for n_plane, plane in enumerate(planes):
            for x in range(0, 3):
                source, target, size = (
                    ((begin - 8) % width, 0, 8),
                    (begin, 8, n),
                    (end % width, n + 8, 8),
                )[x]
                fetch(
                    pop_ref.at[plane, :, source : source + size, :],
                    pop.at[n_plane, :, target : target + size, :],
                )
        for copy in copies[:early]:
            copy.wait()
        if closing:
            acc[:, stop:span, :] = jnp.zeros((slab * 3, span - stop, width), jnp.float32)
        moves = (first, last, 0 if opening else 1 - first)
        spread_list(s0, l0, acc, table, slab, (0, 1), slab, [moves])
        spread_list(s1, l1, acc, table, -slab, (slab - 1,), slab, [moves])
        if closing:
            acc[:, n : n + 16, :] += head_ref[:, 0:16, :]
        if opening:
            carry_out[:, ROWS : 2 * ROWS, :] = acc[:, 0:ROWS, :]
            carry_out[:, 0:ROWS, :] = acc[:, n : n + ROWS, :]
        elif not closing:
            carry_out[:, 0:ROWS, :] = acc[:, n : n + ROWS, :]
        else:
            carry_out[...] = jnp.zeros_like(carry_out)
        written = [
            pltpu.make_async_copy(
                acc.at[i, 8 : 8 + n, :],
                field_out.at[i // 3, i % 3, begin:end, :],
                sems.at[len(copies) + i],
            )
            for i in range(slab * 3)
        ]
        for copy in written:
            copy.start()
        for copy in copies[early:]:
            copy.wait()

        @pl.loop(0, (n + 16) // 8)
        def _(t):
            rows = pl.ds(pl.multiple_of(t * 8, 8), 8)
            for n_plane, plane in enumerate(planes):
                f = [pop[n_plane, i, rows, :] for i in range(19)]
                force = [acc[plane * 3 + c, rows, :] for c in range(3)]
                items = range(n_plane * 5, n_plane * 5 + 5)
                for i, value in collided(f, force, items).items():
                    post[i, rows, :] = value

        for target, begin_item in ((low, 0), (high, 5)):
            for i in range(5):
                item = begin_item + i
                at = 8 - velocity_x[item]
                value = post[item, at : at + n, :]
                if velocity_y[item]:
                    value = pltpu.roll(value, velocity_y[item] % width, 1)
                target[i] = value
        for copy in written:
            copy.wait()

    shape = jax.ShapeDtypeStruct
    return pl.pallas_call(
        kernel,
        out_shape=(
            shape((5, n, width), jnp.float32),
            shape((5, n, width), jnp.float32),
            shape((slab * 3, 2 * ROWS, width), jnp.float32),
            shape((slab, 3, width, width), jnp.float32),
        ),
        in_specs=[SMEM, VMEM, SMEM, VMEM, HBM, ANY, VMEM, HBM, HBM],
        out_specs=(VMEM, VMEM, VMEM, HBM),
        scratch_shapes=[
            pltpu.VMEM((slab * 3, span, width), jnp.float32),
            pltpu.VMEM((2, 19, n + 16, width), jnp.float32),
            pltpu.VMEM((10, n + 16, width), jnp.float32),
            pltpu.VMEM((rows_of((0, 1)), (below.shape[0] - 8) // 7, LANES), jnp.float32),
            pltpu.SemaphoreType.DMA((8 + slab * 3,)),
        ],
        input_output_aliases={} if field is None else {8: 3},
        compiler_params=pltpu.CompilerParams(vmem_limit_bytes=20 * MIB),
        cost_estimate=cost(8_000_000_000),
    )(
        starts_of(below, windows),
        below,
        starts_of(above, windows),
        above,
        total,
        jnp.zeros((slab * 3, ROWS, width), jnp.float32) if carry is None else carry[:, :ROWS],
        jnp.zeros((slab * 3, ROWS, width), jnp.float32) if head is None else head,
        populations,
        jnp.zeros((8, 128), jnp.float32) if field is None else field,
    )


def interior(populations, field):
    slab, width = (populations.shape[0], populations.shape[2])
    pieces = 4
    step = width // pieces

    def kernel(pop_ref, field_ref, out_ref, pop, force, post, out, in_sems, out_sems):
        def fetch(k):
            rows = pl.ds(k * step, step)
            return (
                pltpu.make_async_copy(pop_ref.at[:, :, rows, :], pop.at[:, :, rows, :], in_sems.at[0, k]),
                pltpu.make_async_copy(field_ref.at[:, :, rows, :], force.at[:, :, rows, :], in_sems.at[1, k]),
            )

        for k in range(pieces):
            for copy in fetch(k):
                copy.start()

        ranges = []
        for p in range(slab):
            if p > 0:
                ranges.append((p, 0, 5))
            if p < slab - 1:
                ranges.append((p, 5, 19))
            else:
                ranges.append((p, 10, 19))

        def kept(p):
            return [i for i in range(19) if 0 <= p + velocity_z[i] < slab]

        started = []

        def emit(k, low, high):
            @pl.loop(low // 8, high // 8)
            def _(t):
                for p in range(slab):
                    for i in kept(p):
                        x = velocity_x[i]
                        if x == 0:
                            continue
                        q = p + velocity_z[i]
                        near = pl.ds(pl.multiple_of(t * 8 + (0 if x > 0 else 8), 8), 16)
                        value = post[q, i, near, :]
                        value = value[7:15] if x > 0 else value[1:9]
                        out[q, i, pl.ds(pl.multiple_of(t * 8, 8), 8), :] = value

            for r, (p, begin, end) in enumerate(ranges):
                copy = pltpu.make_async_copy(
                    out.at[p, begin:end, low:high, :],
                    out_ref.at[p, begin:end, low:high, :],
                    out_sems.at[r, k],
                )
                copy.start()
                started.append(copy)

        for k in range(pieces):
            for copy in fetch(k):
                copy.wait()

            @pl.loop(k * step // 8, (k + 1) * step // 8)
            def _(t):
                rows = pl.ds(pl.multiple_of(t * 8, 8), 8)
                padded = pl.ds(pl.multiple_of(t * 8 + 8, 8), 8)
                for p in range(slab):
                    f = [pop[p, i, rows, :] for i in range(19)]
                    moved = collided(f, [force[p, c, rows, :] for c in range(3)], kept(p))
                    for i, value in moved.items():
                        if velocity_y[i]:
                            value = pltpu.roll(value, velocity_y[i] % width, 1)
                        q = p + velocity_z[i]
                        if velocity_x[i]:
                            post[q, i, padded, :] = value
                        else:
                            out[q, i, rows, :] = value

            if k < pieces - 1:
                emit(k, 8 if k == 0 else k * step - 8, (k + 1) * step - 8)
        for p in range(slab):
            for i in kept(p):
                q = p + velocity_z[i]
                if velocity_x[i] > 0:
                    post[q, i, 0:8, :] = post[q, i, width : width + 8, :]
                elif velocity_x[i] < 0:
                    post[q, i, width + 8 : width + 16, :] = post[q, i, 8:16, :]
        emit(pieces - 1, (pieces - 1) * step - 8, width)
        emit(pieces, 0, 8)
        for copy in started:
            copy.wait()

    return pl.pallas_call(
        kernel,
        out_shape=jax.ShapeDtypeStruct(populations.shape, jnp.float32),
        in_specs=[HBM, HBM],
        out_specs=HBM,
        scratch_shapes=[
            pltpu.VMEM(populations.shape, jnp.float32),
            pltpu.VMEM(field.shape, jnp.float32),
            pltpu.VMEM((slab, 19, width + 16, width), jnp.float32),
            pltpu.VMEM(populations.shape, jnp.float32),
            pltpu.SemaphoreType.DMA((2, pieces)),
            pltpu.SemaphoreType.DMA((2 * slab, pieces + 1)),
        ],
        compiler_params=pltpu.CompilerParams(vmem_limit_bytes=36 * MIB),
        name="interior",
        cost_estimate=pl.CostEstimate(flops=0, bytes_accessed=25_000_000, transcendentals=0),
    )(populations, field)


def arrivals(new_populations, lows, highs, edges):
    slab = new_populations.shape[0]
    count = len(lows)

    def kernel(*refs):
        parts, out_ref, sems = (refs[1 : 1 + 2 * count], refs[-2], refs[-1])
        copies = []
        for k, (begin, end) in enumerate(edges):
            for s, (part, plane, item) in enumerate(
                ((parts[k], 0, 0), (parts[count + k], slab - 1, 5))
            ):
                copies.append(
                    pltpu.make_async_copy(
                        part, out_ref.at[plane, item : item + 5, begin:end, :], sems.at[s, k]
                    )
                )
        for copy in copies:
            copy.start()
        for copy in copies:
            copy.wait()

    return pl.pallas_call(
        kernel,
        out_shape=jax.ShapeDtypeStruct(new_populations.shape, jnp.float32),
        in_specs=[HBM] + [VMEM] * (2 * count),
        out_specs=HBM,
        scratch_shapes=[pltpu.SemaphoreType.DMA((2, count))],
        input_output_aliases={0: 0},
        compiler_params=pltpu.CompilerParams(vmem_limit_bytes=8 * MIB),
        name="arrivals",
    )(new_populations, *lows, *highs)


def prepared(displacement, tension, bending, offset, owner, cell, cells, width):
    before, after = halos(displacement, "shard", 2, 2)
    _, vesicles, rows, lanes = displacement.shape
    assert lanes == LANES
    index = lax.axis_index("shard")
    outside = jnp.stack(
        [
            jnp.where(index == 0, 0, -1),
            jnp.where(index == lax.axis_size("shard") - 1, rows + 1, -1),
        ]
    ).astype(jnp.int32)
    slab_bits = bits(cells // (width * width))

    def kernel(edge, t_ref, b_ref, x_ref, before_ref, after_ref, o_ref, own_ref, cell_ref, *rest):
        force_ref, key_ref = rest[:2]
        values, (padded, wide_ref) = (rest[2:8], rest[8:])
        place = lax.broadcasted_iota(jnp.int32, (rows + 2, lanes), 0)

        def laplacian(ref, begin, count):
            center = ref[begin : begin + count, :]
            return (
                ref[begin + 1 : begin + count + 1, :]
                + ref[begin - 1 : begin + count - 1, :]
                + pltpu.roll(center, 1, 1)
                + pltpu.roll(center, lanes - 1, 1)
                - 4.0 * center
            )

        for v in range(vesicles):
            at = slice(v * rows, (v + 1) * rows)
            code = cell_ref[v]
            plane, x, y = (
                code >> (2 * bits(width)),
                (code >> bits(width)) & (width - 1),
                code & (width - 1),
            )
            x = (x + LAG) & (width - 1)
            key_ref[at, :] = own_ref[v] * cells + (
                (x << (bits(width) + slab_bits)) | (plane << bits(width)) | y
            )
            for c in range(3):
                values[3 + c][at, :] = o_ref[c, v]
                padded[6:8, :] = before_ref[c, v]
                padded[8 : 8 + rows, :] = x_ref[c, v]
                padded[8 + rows : 10 + rows, :] = after_ref[c, v]
                wide = laplacian(padded, 7, rows + 2)
                hidden = (place == edge[0]) | (place == edge[1])
                wide_ref[7 : 9 + rows, :] = jnp.where(hidden, 0.0, wide)
                second = laplacian(wide_ref, 8, rows)
                force = t_ref[v] * wide_ref[8 : 8 + rows, :] - b_ref[v] * second
                force_ref[c, v] = force
                values[c][at, :] = force

    shape = jax.ShapeDtypeStruct
    flat = (vesicles * rows, lanes)
    out = pl.pallas_call(
        kernel,
        out_shape=(shape(displacement.shape, jnp.float32), shape(flat, jnp.int32))
        + (shape(flat, jnp.float32),) * 6,
        in_specs=[SMEM] * 3 + [VMEM] * 6,
        out_specs=(VMEM,) * 8,
        scratch_shapes=[pltpu.VMEM((rows + 16, lanes), jnp.float32)] * 2,
        name="prepared",
    )(outside, tension, bending, displacement, before, after, offset, owner, cell)
    return out[0], out[1], out[2:]


def packed(starts, columns, device_count, capacity, cells):
    count = columns[0].shape[0]
    lanes = min(capacity, LANES)
    tiles = capacity // lanes

    def kernel(start_ref, *refs):
        columns, out, table = (refs[:7], refs[7], refs[8])
        for i in range(7):
            table[0:count, i, :] = columns[i][...].astype(jnp.float32)
        field = lax.broadcasted_iota(jnp.int32, (7, LANES), 0)
        lane = lax.broadcasted_iota(jnp.int32, (7, LANES), 1)
        for r in range(tiles + 1):
            table[count + r] = jnp.where(field == 0, float(device_count * cells), 0.0)

        @pl.loop(0, device_count, unroll=4)
        def _(d):
            row, shift = (start_ref[d] // LANES, start_ref[d] % LANES)
            turned = [
                pltpu.roll(table[row + j], (LANES - shift) % LANES, 1) for j in range(tiles + 1)
            ]
            before = (d * cells).astype(jnp.float32)
            for j in range(tiles):
                value = jnp.where(lane < LANES - shift, turned[j], turned[j + 1])
                tag = jnp.minimum(value - before, float(cells))
                out[d, :, j, :] = jnp.where(field == 0, tag, value)[:, :lanes]

    return pl.pallas_call(
        kernel,
        out_shape=jax.ShapeDtypeStruct((device_count, 7, tiles, lanes), jnp.float32),
        in_specs=[SMEM] + [VMEM] * 7,
        out_specs=VMEM,
        scratch_shapes=[pltpu.VMEM((count + tiles + 1, 7, LANES), jnp.float32)],
        compiler_params=pltpu.CompilerParams(vmem_limit_bytes=8 * MIB),
        name="packed",
    )(starts, *columns)


def exchanged(send):
    groups, members = (lax.axis_size("ves"), lax.axis_size("shard"))
    count = groups * members

    def kernel(send_ref, got_ref, own_sem, send_sems, got_sems):
        group, member = (lax.axis_index("ves"), lax.axis_index("shard"))
        me = group * members + member
        barrier = pltpu.get_barrier_semaphore()

        def other(k):
            peer = lax.rem(me + k, count)
            return peer, (peer // members, lax.rem(peer, members))

        def greet(k, carry):
            pl.semaphore_signal(
                barrier, inc=1, device_id=other(k)[1], device_id_type=pl.DeviceIdType.MESH
            )
            return carry

        lax.fori_loop(1, count, greet, 0)
        own = pltpu.make_async_copy(send_ref.at[me], got_ref.at[me], own_sem)
        own.start()
        pl.semaphore_wait(barrier, count - 1)

        def copy(k):
            peer, place = other(k)
            return pltpu.make_async_remote_copy(
                src_ref=send_ref.at[peer],
                dst_ref=got_ref.at[me],
                send_sem=send_sems.at[k],
                recv_sem=got_sems.at[k],
                device_id=place,
                device_id_type=pl.DeviceIdType.MESH,
            )

        def begin(k, carry):
            copy(k).start()
            return carry

        def finish(k, carry):
            copy(k).wait()
            return carry

        lax.fori_loop(1, count, begin, 0)
        own.wait()
        lax.fori_loop(1, count, finish, 0)

    return pl.pallas_call(
        kernel,
        out_shape=jax.ShapeDtypeStruct(send.shape, send.dtype),
        in_specs=[ANY],
        out_specs=ANY,
        scratch_shapes=[
            pltpu.SemaphoreType.DMA,
            pltpu.SemaphoreType.DMA((count,)),
            pltpu.SemaphoreType.DMA((count,)),
        ],
        compiler_params=pltpu.CompilerParams(
            collective_id=0, has_side_effects=True, vmem_limit_bytes=4 * MIB
        ),
        name="exchanged",
    )(send)


def dispatched(key, values, owner, device_count, cells):
    capacity = 2 * owner.size // device_count
    devices = jnp.arange(device_count, dtype=jnp.int32)
    starts = jnp.sum((owner.reshape(-1)[None, :] < devices[:, None]).astype(jnp.int32), 1)
    ordered = lax.sort(
        (key.reshape(-1),) + tuple(v.reshape(-1) for v in values), num_keys=1, is_stable=False
    )
    send = packed(
        starts, [v.reshape(-1, LANES) for v in ordered], device_count, capacity, cells
    )
    return exchanged(send)


CUTS = (0, 3, 6, 11, 16)


def one_step(displacement, tension, bending, offset, owner, cell, populations):
    device_count = lax.axis_size("ves") * lax.axis_size("shard")
    slab, width = (populations.shape[0], populations.shape[2])
    cells = slab * width * width
    windows = width // WINDOW
    x_bit = bits(slab) + bits(width)
    membrane_force, key, values = prepared(
        displacement, tension, bending, offset, owner, cell, cells, width
    )
    got = dispatched(key, values, owner, device_count, cells)
    got = [got[:, i].reshape(-1) for i in range(7)]
    key = got[0].astype(jnp.int32)
    bounds = jnp.arange(windows + 1, dtype=jnp.int32) * (WINDOW << x_bit)
    starts = jnp.sum((key[None, :] < bounds[:, None]).astype(jnp.float32), 1)
    ordered = lax.sort(
        (key,) + tuple(got[1:]), num_keys=1, is_stable=False
    )
    columns = list(ordered[1:]) + [ordered[0].astype(jnp.float32)]
    starts = jnp.pad(starts, (0, LANES - windows - 1))
    listed = jnp.concatenate(
        [v.reshape(-1, LANES) for v in columns]
        + [jnp.broadcast_to(starts[None, :], (8, LANES))],
        0,
    )
    below = passed_along(listed, ("ves", "shard"), 1)
    above = passed_along(listed, ("ves", "shard"), -1)
    total = spread_own(listed, slab, width)

    cuts = [cut * windows // CUTS[-1] for cut in CUTS]
    field = carry = head = None
    lows, highs, edges = ([], [], [])
    begin = 0
    for j, (first, last) in enumerate(zip(cuts[:-1], cuts[1:])):
        low, high, carry, field = spread_chunk(
            (below, above), total, carry, head if last == windows else None,
            populations, field, first, last,
        )
        if j == 0:
            head = carry[:, ROWS:]
        edges.append((begin, begin + low.shape[1]))
        begin += low.shape[1]
        lows.append(passed_along(low, ("ves", "shard"), 1))
        highs.append(passed_along(high, ("ves", "shard"), -1))
    new_populations = interior(populations, field)
    new_populations = arrivals(new_populations, lows, highs, edges)
    return (membrane_force, field, new_populations)


def solution(mesh):
    return jax.shard_map(
        one_step,
        mesh=mesh,
        in_specs=(
            P(None, "ves", "shard", None),
            P("ves"),
            P("ves"),
            P(None, "ves", "shard", None),
            P("ves", "shard", None),
            P("ves", "shard", None),
            P(("ves", "shard"), None, None, None),
        ),
        out_specs=(
            P(None, "ves", "shard", None),
            P(("ves", "shard"), None, None, None),
            P(("ves", "shard"), None, None, None),
        ),
        check_vma=False,
    )
```

```python
import math

import jax
import jax.numpy as jnp
from jax import lax
from jax.experimental import pallas as pl
from jax.experimental.pallas import tpu as pltpu
from jax.sharding import PartitionSpec as P


relax_time = 0.8
velocity_x = [0, 1, -1, 0, 0, 0, 1, -1, 0, 0, 0, 1, -1, 0, 0, 1, 1, -1, -1]
velocity_y = [0, 0, 0, 1, -1, 0, 0, 0, 1, -1, 0, 0, 0, 1, -1, 1, -1, 1, -1]
velocity_z = [1, 1, 1, 1, 1, -1, -1, -1, -1, -1, 0, 0, 0, 0, 0, 0, 0, 0, 0]
lattice_weights = [
    1.0 / 18,
    1.0 / 36,
    1.0 / 36,
    1.0 / 36,
    1.0 / 36,
    1.0 / 18,
    1.0 / 36,
    1.0 / 36,
    1.0 / 36,
    1.0 / 36,
    1.0 / 3,
    1.0 / 18,
    1.0 / 18,
    1.0 / 18,
    1.0 / 18,
    1.0 / 36,
    1.0 / 36,
    1.0 / 36,
    1.0 / 36,
]


def passed_along(value, axis, steps):
    count = lax.axis_size(axis)
    pairs = [(source, (source + steps) % count) for source in range(count)]
    return lax.ppermute(value, axis, pairs)


def halos(x, axis, dim, width):
    devices, length = (lax.axis_size(axis), x.shape[dim])
    up = [(i, i + 1) for i in range(devices - 1)]
    down = [(j, i) for i, j in up]
    last = lax.slice_in_dim(x, length - width, length, axis=dim)
    initial = lax.slice_in_dim(x, 0, width, axis=dim)
    return lax.ppermute(last, axis, up), lax.ppermute(initial, axis, down)


WINDOW = 16
ROWS = 24
BLOCK = 256


HALF_PI = 0.5 * math.pi
COSINE = [(-1.0) ** n * HALF_PI ** (2 * n) / math.factorial(2 * n) for n in range(8)]
SINE = [(-1.0) ** n * HALF_PI ** (2 * n + 1) / math.factorial(2 * n + 1) for n in range(8)]


def weights(fraction):
    square = fraction * fraction
    c = jnp.full_like(square, COSINE[-1])
    s = jnp.full_like(square, SINE[-1])
    for n in range(6, -1, -1):
        c = c * square + COSINE[n]
        s = s * square + SINE[n]
    s = s * fraction
    return [0.25 * (1.0 - s), 0.25 * (1.0 + c), 0.25 * (1.0 + s), 0.25 * (1.0 - c)]


def bits(count):
    return (count - 1).bit_length()


LANES = 128
MIB = 1 << 20


def rows_of(planes):
    return 13 + 3 * len(planes)


def spread_list(starts, list_ref, acc, table, shift, planes, slab, ranges):
    width = acc.shape[2]
    count = table.shape[1]
    row_id = lax.broadcasted_iota(jnp.int32, (ROWS, LANES), 0).astype(jnp.float32)
    y_id = lax.broadcasted_iota(jnp.int32, (width, LANES), 0).astype(jnp.bfloat16)

    def prepare(t):
        at = pl.ds(pl.multiple_of(t * 8, 8), 8)
        part = [list_ref[pl.ds(pl.multiple_of(c * count + t * 8, 8), 8), :] for c in range(7)]
        key = part[6].astype(jnp.int32)
        y = key & (width - 1)
        plane = (key >> bits(width)) & (slab - 1)
        table[0, at, :] = (key >> (bits(width) + bits(slab))).astype(jnp.float32)
        phi_x, phi_y, phi_z = (weights(part[c]) for c in (3, 4, 5))
        for k in range(4):
            table[1 + k, at, :] = phi_x[k]
            table[5 + k, at, :] = phi_y[k]
            table[9 + k, at, :] = ((y + (k - 1)) & (width - 1)).astype(jnp.float32)
        for n, q in enumerate(planes):
            rel = q + 1 + shift - plane
            weight = jnp.zeros_like(part[0])
            for k in range(4):
                weight = jnp.where(rel == k, phi_z[k], weight)
            for c in range(3):
                table[13 + n * 3 + c, at, :] = part[c] * weight

    def half(r, base):
        def row(i, like):
            return jnp.broadcast_to(table[i, pl.ds(r, 1), :], like.shape)

        def narrow(i):
            return jnp.broadcast_to(table[i, pl.ds(r, 1), :].astype(jnp.bfloat16), y_id.shape)

        right = jnp.zeros(y_id.shape, jnp.bfloat16)
        for k in range(4):
            right = jnp.where(y_id == narrow(9 + k), narrow(5 + k), right)
        x = table[0, pl.ds(r, 1), :] - base
        x = jnp.where((x >= 0.0) & (x < WINDOW), x, 4.0 * ROWS)
        rel = row_id - x
        weight_x = jnp.zeros(row_id.shape, jnp.float32)
        for k in range(4):
            weight_x = jnp.where(rel == k, row(1 + k, row_id), weight_x)
        lefts = [row(13 + i, row_id) * weight_x for i in range(3 * len(planes))]
        return jnp.concatenate(lefts, 0).astype(jnp.bfloat16), right

    def window(w, offset):
        begin = starts[w] // BLOCK
        end = (starts[w + 1] + (BLOCK - 1)) // BLOCK
        base = (w * WINDOW).astype(jnp.float32)
        at_row = (w + offset) * WINDOW

        @pl.loop(0, (end - begin + 1) // 2)
        def _(pair):
            b = begin + 2 * pair
            more = b + 1 < end
            parts = []
            for block, shifted in (
                (b, base),
                (jnp.where(more, b + 1, b), jnp.where(more, base, -4.0 * ROWS * WINDOW * LANES)),
            ):
                for h in range(BLOCK // LANES):
                    parts.append(half(block * (BLOCK // LANES) + h, shifted))
            product = lax.dot_general(
                jnp.concatenate([p[0] for p in parts], 1),
                jnp.concatenate([p[1] for p in parts], 1),
                (((1,), (1,)), ((), ())),
                preferred_element_type=jnp.float32,
            )
            rows = pl.ds(pl.multiple_of(at_row, 8), ROWS)
            for n, q in enumerate(planes):
                for c in range(3):
                    i = n * 3 + c
                    acc[q * 3 + c, rows, :] += product[i * ROWS : (i + 1) * ROWS]

    for first, last, offset in ranges:
        unit = 8 * LANES
        low = starts[first] // BLOCK * BLOCK // unit
        high = (starts[last] + (BLOCK - 1)) // BLOCK * BLOCK

        @pl.loop(low, (high + (unit - 1)) // unit)
        def _(t):
            prepare(t)

        @pl.loop(first, last)
        def _(w):
            window(w, offset)


VMEM = pl.BlockSpec(memory_space=pltpu.VMEM)
SMEM = pl.BlockSpec(memory_space=pltpu.SMEM)


def cost(flops):
    return pl.CostEstimate(flops=flops, bytes_accessed=4_000_000, transcendentals=0)


def starts_of(listed, windows):
    return listed[-8, : windows + 1].astype(jnp.int32)


def spread_own(listed, slab, width):
    windows = width // WINDOW

    count = (listed.shape[0] - 8) // 7
    assert count % 8 == 0

    def kernel(starts, list_ref, acc, table):
        acc[...] = jnp.zeros_like(acc)
        spread_list(starts, list_ref, acc, table, 0, range(slab), slab, [(0, windows, 0)])

    return pl.pallas_call(
        kernel,
        out_shape=jax.ShapeDtypeStruct((slab * 3, width + ROWS - WINDOW, width), jnp.float32),
        in_specs=[SMEM, VMEM],
        out_specs=VMEM,
        scratch_shapes=[pltpu.VMEM((rows_of(range(slab)), count, LANES), jnp.float32)],
        compiler_params=pltpu.CompilerParams(vmem_limit_bytes=12 * MIB),
        name="spread_own",
        cost_estimate=cost(20_000_000_000),
    )(starts_of(listed, windows), listed)


ANY = pl.BlockSpec(memory_space=pl.ANY)
HBM = pl.BlockSpec(memory_space=pltpu.HBM)
LAG = 7
KEEP = 1.0 - 1.0 / relax_time
FORCING = 1.0 - 0.5 / relax_time


def collided(f, force, items):
    def along(vector, item, start=None):
        total = start
        for e, v in zip((velocity_x[item], velocity_y[item], velocity_z[item]), vector):
            if e == 0:
                continue
            if total is None:
                total = v if e > 0 else -v
            else:
                total = total + v if e > 0 else total - v
        return total

    def tree(values):
        while len(values) > 1:
            values = [
                values[i] + values[i + 1] if i + 1 < len(values) else values[i]
                for i in range(0, len(values), 2)
            ]
        return values[0]

    density = tree(list(f))
    inverse = 1.0 / density
    flow = []
    for axis, table in enumerate((velocity_x, velocity_y, velocity_z)):
        plus = tree([f[i] for i in range(19) if table[i] > 0])
        minus = tree([f[i] for i in range(19) if table[i] < 0])
        flow.append(((plus - minus) + 0.5 * force[axis]) * inverse)
    speed_sq = flow[0] * flow[0] + flow[1] * flow[1] + flow[2] * flow[2]
    work = flow[0] * force[0] + flow[1] * force[1] + flow[2] * force[2]
    scaled = density * (1.0 / relax_time)
    base = scaled - (1.5 * scaled) * speed_sq - (3.0 * FORCING) * work
    linear = 3.0 * scaled
    square = 4.5 * scaled
    pushed = [3.0 * FORCING * v for v in force]
    result = {}
    for item in items:
        cu = along(flow, item)
        if cu is None:
            bracket = base
        else:
            facing = along(pushed, item)
            bracket = base + facing + cu * (linear + square * cu + 3.0 * facing)
        result[item] = KEEP * f[item] + lattice_weights[item] * bracket
    return result


def spread_chunk(lists, total, carry, head, populations, field, first, last):
    below, above = lists
    slab, width = (populations.shape[0], populations.shape[2])
    windows = width // WINDOW
    opening, closing = (first == 0, last == windows)
    begin = 0 if opening else (first - 1) * WINDOW
    end = width if closing else (last - 1) * WINDOW
    n = end - begin
    span = n + ROWS
    planes = (slab - 1, 0)

    def kernel(s0, l0, s1, l1, total_ref, carry_ref, head_ref, pop_ref, field_in, *rest):
        low, high, carry_out, field_out, acc, pop, post, table, sems = rest
        del field_in
        copies = []

        def fetch(source, target):
            copy = pltpu.make_async_copy(source, target, sems.at[len(copies)])
            copy.start()
            copies.append(copy)

        got = 0
        if not opening:
            fetch(carry_ref, acc.at[:, 0:ROWS, :])
            got = ROWS
        stop = min(span, width + ROWS - WINDOW - begin)
        fetch(total_ref.at[:, begin + got : begin + stop, :], acc.at[:, got:stop, :])
        early = len(copies)
        for n_plane, plane in enumerate(planes):
            for x in range(0, 3):
                source, target, size = (
                    ((begin - 8) % width, 0, 8),
                    (begin, 8, n),
                    (end % width, n + 8, 8),
                )[x]
                fetch(
                    pop_ref.at[plane, :, source : source + size, :],
                    pop.at[n_plane, :, target : target + size, :],
                )
        for copy in copies[:early]:
            copy.wait()
        if closing:
            acc[:, stop:span, :] = jnp.zeros((slab * 3, span - stop, width), jnp.float32)
        moves = (first, last, 0 if opening else 1 - first)
        spread_list(s0, l0, acc, table, slab, (0, 1), slab, [moves])
        spread_list(s1, l1, acc, table, -slab, (slab - 1,), slab, [moves])
        if closing:
            acc[:, n : n + 16, :] += head_ref[:, 0:16, :]
        if opening:
            carry_out[:, ROWS : 2 * ROWS, :] = acc[:, 0:ROWS, :]
            carry_out[:, 0:ROWS, :] = acc[:, n : n + ROWS, :]
        elif not closing:
            carry_out[:, 0:ROWS, :] = acc[:, n : n + ROWS, :]
        else:
            carry_out[...] = jnp.zeros_like(carry_out)
        written = [
            pltpu.make_async_copy(
                acc.at[i, 8 : 8 + n, :],
                field_out.at[i // 3, i % 3, begin:end, :],
                sems.at[len(copies) + i],
            )
            for i in range(slab * 3)
        ]
        for copy in written:
            copy.start()
        for copy in copies[early:]:
            copy.wait()

        @pl.loop(0, (n + 16) // 8)
        def _(t):
            rows = pl.ds(pl.multiple_of(t * 8, 8), 8)
            for n_plane, plane in enumerate(planes):
                f = [pop[n_plane, i, rows, :] for i in range(19)]
                force = [acc[plane * 3 + c, rows, :] for c in range(3)]
                items = range(n_plane * 5, n_plane * 5 + 5)
                for i, value in collided(f, force, items).items():
                    post[i, rows, :] = value

        for target, begin_item in ((low, 0), (high, 5)):
            for i in range(5):
                item = begin_item + i
                at = 8 - velocity_x[item]
                value = post[item, at : at + n, :]
                if velocity_y[item]:
                    value = pltpu.roll(value, velocity_y[item] % width, 1)
                target[i] = value
        for copy in written:
            copy.wait()

    shape = jax.ShapeDtypeStruct
    return pl.pallas_call(
        kernel,
        out_shape=(
            shape((5, n, width), jnp.float32),
            shape((5, n, width), jnp.float32),
            shape((slab * 3, 2 * ROWS, width), jnp.float32),
            shape((slab, 3, width, width), jnp.float32),
        ),
        in_specs=[SMEM, VMEM, SMEM, VMEM, HBM, ANY, VMEM, HBM, HBM],
        out_specs=(VMEM, VMEM, VMEM, HBM),
        scratch_shapes=[
            pltpu.VMEM((slab * 3, span, width), jnp.float32),
            pltpu.VMEM((2, 19, n + 16, width), jnp.float32),
            pltpu.VMEM((10, n + 16, width), jnp.float32),
            pltpu.VMEM((rows_of((0, 1)), (below.shape[0] - 8) // 7, LANES), jnp.float32),
            pltpu.SemaphoreType.DMA((8 + slab * 3,)),
        ],
        input_output_aliases={} if field is None else {8: 3},
        compiler_params=pltpu.CompilerParams(vmem_limit_bytes=20 * MIB),
        cost_estimate=cost(8_000_000_000),
    )(
        starts_of(below, windows),
        below,
        starts_of(above, windows),
        above,
        total,
        jnp.zeros((slab * 3, ROWS, width), jnp.float32) if carry is None else carry[:, :ROWS],
        jnp.zeros((slab * 3, ROWS, width), jnp.float32) if head is None else head,
        populations,
        jnp.zeros((8, 128), jnp.float32) if field is None else field,
    )


def interior(populations, field):
    slab, width = (populations.shape[0], populations.shape[2])
    pieces = 4
    step = width // pieces

    def kernel(pop_ref, field_ref, out_ref, pop, force, post, out, in_sems, out_sems):
        def fetch(k):
            rows = pl.ds(k * step, step)
            return (
                pltpu.make_async_copy(pop_ref.at[:, :, rows, :], pop.at[:, :, rows, :], in_sems.at[0, k]),
                pltpu.make_async_copy(field_ref.at[:, :, rows, :], force.at[:, :, rows, :], in_sems.at[1, k]),
            )

        for k in range(pieces):
            for copy in fetch(k):
                copy.start()

        ranges = []
        for p in range(slab):
            if p > 0:
                ranges.append((p, 0, 5))
            if p < slab - 1:
                ranges.append((p, 5, 19))
            else:
                ranges.append((p, 10, 19))

        def kept(p):
            return [i for i in range(19) if 0 <= p + velocity_z[i] < slab]

        started = []

        def emit(k, low, high):
            @pl.loop(low // 8, high // 8)
            def _(t):
                for p in range(slab):
                    for i in kept(p):
                        x = velocity_x[i]
                        if x == 0:
                            continue
                        q = p + velocity_z[i]
                        near = pl.ds(pl.multiple_of(t * 8 + (0 if x > 0 else 8), 8), 16)
                        value = post[q, i, near, :]
                        value = value[7:15] if x > 0 else value[1:9]
                        out[q, i, pl.ds(pl.multiple_of(t * 8, 8), 8), :] = value

            for r, (p, begin, end) in enumerate(ranges):
                copy = pltpu.make_async_copy(
                    out.at[p, begin:end, low:high, :],
                    out_ref.at[p, begin:end, low:high, :],
                    out_sems.at[r, k],
                )
                copy.start()
                started.append(copy)

        for k in range(pieces):
            for copy in fetch(k):
                copy.wait()

            @pl.loop(k * step // 8, (k + 1) * step // 8)
            def _(t):
                rows = pl.ds(pl.multiple_of(t * 8, 8), 8)
                padded = pl.ds(pl.multiple_of(t * 8 + 8, 8), 8)
                for p in range(slab):
                    f = [pop[p, i, rows, :] for i in range(19)]
                    moved = collided(f, [force[p, c, rows, :] for c in range(3)], kept(p))
                    for i, value in moved.items():
                        if velocity_y[i]:
                            value = pltpu.roll(value, velocity_y[i] % width, 1)
                        q = p + velocity_z[i]
                        if velocity_x[i]:
                            post[q, i, padded, :] = value
                        else:
                            out[q, i, rows, :] = value

            if k < pieces - 1:
                emit(k, 8 if k == 0 else k * step - 8, (k + 1) * step - 8)
        for p in range(slab):
            for i in kept(p):
                q = p + velocity_z[i]
                if velocity_x[i] > 0:
                    post[q, i, 0:8, :] = post[q, i, width : width + 8, :]
                elif velocity_x[i] < 0:
                    post[q, i, width + 8 : width + 16, :] = post[q, i, 8:16, :]
        emit(pieces - 1, (pieces - 1) * step - 8, width)
        emit(pieces, 0, 8)
        for copy in started:
            copy.wait()

    return pl.pallas_call(
        kernel,
        out_shape=jax.ShapeDtypeStruct(populations.shape, jnp.float32),
        in_specs=[HBM, HBM],
        out_specs=HBM,
        scratch_shapes=[
            pltpu.VMEM(populations.shape, jnp.float32),
            pltpu.VMEM(field.shape, jnp.float32),
            pltpu.VMEM((slab, 19, width + 16, width), jnp.float32),
            pltpu.VMEM(populations.shape, jnp.float32),
            pltpu.SemaphoreType.DMA((2, pieces)),
            pltpu.SemaphoreType.DMA((2 * slab, pieces + 1)),
        ],
        compiler_params=pltpu.CompilerParams(vmem_limit_bytes=36 * MIB),
        name="interior",
        cost_estimate=pl.CostEstimate(flops=0, bytes_accessed=25_000_000, transcendentals=0),
    )(populations, field)


def arrivals(new_populations, lows, highs, edges):
    slab = new_populations.shape[0]
    count = len(lows)

    def kernel(*refs):
        parts, out_ref, sems = (refs[1 : 1 + 2 * count], refs[-2], refs[-1])
        copies = []
        for k, (begin, end) in enumerate(edges):
            for s, (part, plane, item) in enumerate(
                ((parts[k], 0, 0), (parts[count + k], slab - 1, 5))
            ):
                copies.append(
                    pltpu.make_async_copy(
                        part, out_ref.at[plane, item : item + 5, begin:end, :], sems.at[s, k]
                    )
                )
        for copy in copies:
            copy.start()
        for copy in copies:
            copy.wait()

    return pl.pallas_call(
        kernel,
        out_shape=jax.ShapeDtypeStruct(new_populations.shape, jnp.float32),
        in_specs=[HBM] + [VMEM] * (2 * count),
        out_specs=HBM,
        scratch_shapes=[pltpu.SemaphoreType.DMA((2, count))],
        input_output_aliases={0: 0},
        compiler_params=pltpu.CompilerParams(vmem_limit_bytes=8 * MIB),
        name="arrivals",
    )(new_populations, *lows, *highs)


def prepared(displacement, tension, bending, offset, owner, cell, cells, width):
    before, after = halos(displacement, "shard", 2, 2)
    _, vesicles, rows, lanes = displacement.shape
    assert lanes == LANES
    index = lax.axis_index("shard")
    outside = jnp.stack(
        [
            jnp.where(index == 0, 0, -1),
            jnp.where(index == lax.axis_size("shard") - 1, rows + 1, -1),
        ]
    ).astype(jnp.int32)
    slab_bits = bits(cells // (width * width))

    def kernel(edge, t_ref, b_ref, x_ref, before_ref, after_ref, o_ref, own_ref, cell_ref, *rest):
        force_ref, key_ref = rest[:2]
        values, (padded, wide_ref) = (rest[2:8], rest[8:])
        place = lax.broadcasted_iota(jnp.int32, (rows + 2, lanes), 0)

        def laplacian(ref, begin, count):
            center = ref[begin : begin + count, :]
            return (
                ref[begin + 1 : begin + count + 1, :]
                + ref[begin - 1 : begin + count - 1, :]
                + pltpu.roll(center, 1, 1)
                + pltpu.roll(center, lanes - 1, 1)
                - 4.0 * center
            )

        for v in range(vesicles):
            at = slice(v * rows, (v + 1) * rows)
            code = cell_ref[v]
            plane, x, y = (
                code >> (2 * bits(width)),
                (code >> bits(width)) & (width - 1),
                code & (width - 1),
            )
            x = (x + LAG) & (width - 1)
            key_ref[at, :] = own_ref[v] * cells + (
                (x << (bits(width) + slab_bits)) | (plane << bits(width)) | y
            )
            for c in range(3):
                values[3 + c][at, :] = o_ref[c, v]
                padded[6:8, :] = before_ref[c, v]
                padded[8 : 8 + rows, :] = x_ref[c, v]
                padded[8 + rows : 10 + rows, :] = after_ref[c, v]
                wide = laplacian(padded, 7, rows + 2)
                hidden = (place == edge[0]) | (place == edge[1])
                wide_ref[7 : 9 + rows, :] = jnp.where(hidden, 0.0, wide)
                second = laplacian(wide_ref, 8, rows)
                force = t_ref[v] * wide_ref[8 : 8 + rows, :] - b_ref[v] * second
                force_ref[c, v] = force
                values[c][at, :] = force

    shape = jax.ShapeDtypeStruct
    flat = (vesicles * rows, lanes)
    out = pl.pallas_call(
        kernel,
        out_shape=(shape(displacement.shape, jnp.float32), shape(flat, jnp.int32))
        + (shape(flat, jnp.float32),) * 6,
        in_specs=[SMEM] * 3 + [VMEM] * 6,
        out_specs=(VMEM,) * 8,
        scratch_shapes=[pltpu.VMEM((rows + 16, lanes), jnp.float32)] * 2,
        name="prepared",
    )(outside, tension, bending, displacement, before, after, offset, owner, cell)
    return out[0], out[1], out[2:]


def packed(starts, columns, device_count, capacity, cells):
    count = columns[0].shape[0]
    lanes = min(capacity, LANES)
    tiles = capacity // lanes

    def kernel(start_ref, *refs):
        columns, out, table = (refs[:7], refs[7], refs[8])
        for i in range(7):
            table[0:count, i, :] = columns[i][...].astype(jnp.float32)
        field = lax.broadcasted_iota(jnp.int32, (7, LANES), 0)
        lane = lax.broadcasted_iota(jnp.int32, (7, LANES), 1)
        for r in range(tiles + 1):
            table[count + r] = jnp.where(field == 0, float(device_count * cells), 0.0)

        @pl.loop(0, device_count, unroll=4)
        def _(d):
            row, shift = (start_ref[d] // LANES, start_ref[d] % LANES)
            turned = [
                pltpu.roll(table[row + j], (LANES - shift) % LANES, 1) for j in range(tiles + 1)
            ]
            before = (d * cells).astype(jnp.float32)
            for j in range(tiles):
                value = jnp.where(lane < LANES - shift, turned[j], turned[j + 1])
                tag = jnp.minimum(value - before, float(cells))
                out[d, :, j, :] = jnp.where(field == 0, tag, value)[:, :lanes]

    return pl.pallas_call(
        kernel,
        out_shape=jax.ShapeDtypeStruct((device_count, 7, tiles, lanes), jnp.float32),
        in_specs=[SMEM] + [VMEM] * 7,
        out_specs=VMEM,
        scratch_shapes=[pltpu.VMEM((count + tiles + 1, 7, LANES), jnp.float32)],
        compiler_params=pltpu.CompilerParams(vmem_limit_bytes=8 * MIB),
        name="packed",
    )(starts, *columns)


def exchanged(send):
    groups, members = (lax.axis_size("ves"), lax.axis_size("shard"))
    count = groups * members

    def kernel(send_ref, got_ref, own_sem, send_sems, got_sems):
        group, member = (lax.axis_index("ves"), lax.axis_index("shard"))
        me = group * members + member
        barrier = pltpu.get_barrier_semaphore()

        def other(k):
            peer = lax.rem(me + k, count)
            return peer, (peer // members, lax.rem(peer, members))

        def greet(k, carry):
            pl.semaphore_signal(
                barrier, inc=1, device_id=other(k)[1], device_id_type=pl.DeviceIdType.MESH
            )
            return carry

        lax.fori_loop(1, count, greet, 0)
        own = pltpu.make_async_copy(send_ref.at[me], got_ref.at[me], own_sem)
        own.start()
        pl.semaphore_wait(barrier, count - 1)

        def copy(k):
            peer, place = other(k)
            return pltpu.make_async_remote_copy(
                src_ref=send_ref.at[peer],
                dst_ref=got_ref.at[me],
                send_sem=send_sems.at[k],
                recv_sem=got_sems.at[k],
                device_id=place,
                device_id_type=pl.DeviceIdType.MESH,
            )

        def begin(k, carry):
            copy(k).start()
            return carry

        def finish(k, carry):
            copy(k).wait()
            return carry

        lax.fori_loop(1, count, begin, 0)
        own.wait()
        lax.fori_loop(1, count, finish, 0)

    return pl.pallas_call(
        kernel,
        out_shape=jax.ShapeDtypeStruct(send.shape, send.dtype),
        in_specs=[ANY],
        out_specs=ANY,
        scratch_shapes=[
            pltpu.SemaphoreType.DMA,
            pltpu.SemaphoreType.DMA((count,)),
            pltpu.SemaphoreType.DMA((count,)),
        ],
        compiler_params=pltpu.CompilerParams(
            collective_id=0, has_side_effects=True, vmem_limit_bytes=4 * MIB
        ),
        name="exchanged",
    )(send)


def dispatched(key, values, owner, device_count, cells):
    capacity = 2 * owner.size // device_count
    devices = jnp.arange(device_count, dtype=jnp.int32)
    starts = jnp.sum((owner.reshape(-1)[None, :] < devices[:, None]).astype(jnp.int32), 1)
    ordered = lax.sort(
        (key.reshape(-1),) + tuple(v.reshape(-1) for v in values), num_keys=1, is_stable=False
    )
    send = packed(
        starts, [v.reshape(-1, LANES) for v in ordered], device_count, capacity, cells
    )
    return exchanged(send)


CUTS = (0, 4, 9, 13, 16)


def one_step(displacement, tension, bending, offset, owner, cell, populations):
    device_count = lax.axis_size("ves") * lax.axis_size("shard")
    slab, width = (populations.shape[0], populations.shape[2])
    cells = slab * width * width
    windows = width // WINDOW
    x_bit = bits(slab) + bits(width)
    membrane_force, key, values = prepared(
        displacement, tension, bending, offset, owner, cell, cells, width
    )
    got = dispatched(key, values, owner, device_count, cells)
    got = [got[:, i].reshape(-1) for i in range(7)]
    key = got[0].astype(jnp.int32)
    bounds = jnp.arange(windows + 1, dtype=jnp.int32) * (WINDOW << x_bit)
    starts = jnp.sum((key[None, :] < bounds[:, None]).astype(jnp.float32), 1)
    ordered = lax.sort(
        (key,) + tuple(got[1:]), num_keys=1, is_stable=False
    )
    columns = list(ordered[1:]) + [ordered[0].astype(jnp.float32)]
    starts = jnp.pad(starts, (0, LANES - windows - 1))
    listed = jnp.concatenate(
        [v.reshape(-1, LANES) for v in columns]
        + [jnp.broadcast_to(starts[None, :], (8, LANES))],
        0,
    )
    below = passed_along(listed, ("ves", "shard"), 1)
    above = passed_along(listed, ("ves", "shard"), -1)
    total = spread_own(listed, slab, width)

    cuts = [cut * windows // CUTS[-1] for cut in CUTS]
    field = carry = head = None
    lows, highs, edges = ([], [], [])
    begin = 0
    for j, (first, last) in enumerate(zip(cuts[:-1], cuts[1:])):
        low, high, carry, field = spread_chunk(
            (below, above), total, carry, head if last == windows else None,
            populations, field, first, last,
        )
        if j == 0:
            head = carry[:, ROWS:]
        edges.append((begin, begin + low.shape[1]))
        begin += low.shape[1]
        lows.append(passed_along(low, ("ves", "shard"), 1))
        highs.append(passed_along(high, ("ves", "shard"), -1))
    new_populations = interior(populations, field)
    new_populations = arrivals(new_populations, lows, highs, edges)
    return (membrane_force, field, new_populations)


def solution(mesh):
    return jax.shard_map(
        one_step,
        mesh=mesh,
        in_specs=(
            P(None, "ves", "shard", None),
            P("ves"),
            P("ves"),
            P(None, "ves", "shard", None),
            P("ves", "shard", None),
            P("ves", "shard", None),
            P(("ves", "shard"), None, None, None),
        ),
        out_specs=(
            P(None, "ves", "shard", None),
            P(("ves", "shard"), None, None, None),
            P(("ves", "shard"), None, None, None),
        ),
        check_vma=False,
    )
```

```python
import math

import jax
import jax.numpy as jnp
from jax import lax
from jax.experimental import pallas as pl
from jax.experimental.pallas import tpu as pltpu
from jax.sharding import PartitionSpec as P


relax_time = 0.8
velocity_x = [0, 1, -1, 0, 0, 0, 1, -1, 0, 0, 0, 1, -1, 0, 0, 1, 1, -1, -1]
velocity_y = [0, 0, 0, 1, -1, 0, 0, 0, 1, -1, 0, 0, 0, 1, -1, 1, -1, 1, -1]
velocity_z = [1, 1, 1, 1, 1, -1, -1, -1, -1, -1, 0, 0, 0, 0, 0, 0, 0, 0, 0]
lattice_weights = [
    1.0 / 18,
    1.0 / 36,
    1.0 / 36,
    1.0 / 36,
    1.0 / 36,
    1.0 / 18,
    1.0 / 36,
    1.0 / 36,
    1.0 / 36,
    1.0 / 36,
    1.0 / 3,
    1.0 / 18,
    1.0 / 18,
    1.0 / 18,
    1.0 / 18,
    1.0 / 36,
    1.0 / 36,
    1.0 / 36,
    1.0 / 36,
]


def passed_along(value, axis, steps):
    count = lax.axis_size(axis)
    pairs = [(source, (source + steps) % count) for source in range(count)]
    return lax.ppermute(value, axis, pairs)


def halos(x, axis, dim, width):
    devices, length = (lax.axis_size(axis), x.shape[dim])
    up = [(i, i + 1) for i in range(devices - 1)]
    down = [(j, i) for i, j in up]
    last = lax.slice_in_dim(x, length - width, length, axis=dim)
    initial = lax.slice_in_dim(x, 0, width, axis=dim)
    return lax.ppermute(last, axis, up), lax.ppermute(initial, axis, down)


WINDOW = 16
ROWS = 24
BLOCK = 256


HALF_PI = 0.5 * math.pi
COSINE = [(-1.0) ** n * HALF_PI ** (2 * n) / math.factorial(2 * n) for n in range(8)]
SINE = [(-1.0) ** n * HALF_PI ** (2 * n + 1) / math.factorial(2 * n + 1) for n in range(8)]


def weights(fraction):
    square = fraction * fraction
    c = jnp.full_like(square, COSINE[-1])
    s = jnp.full_like(square, SINE[-1])
    for n in range(6, -1, -1):
        c = c * square + COSINE[n]
        s = s * square + SINE[n]
    s = s * fraction
    return [0.25 * (1.0 - s), 0.25 * (1.0 + c), 0.25 * (1.0 + s), 0.25 * (1.0 - c)]


def bits(count):
    return (count - 1).bit_length()


LANES = 128
MIB = 1 << 20


def rows_of(planes):
    return 13 + 3 * len(planes)


def spread_list(starts, list_ref, acc, table, shift, planes, slab, ranges):
    width = acc.shape[2]
    count = table.shape[1]
    row_id = lax.broadcasted_iota(jnp.int32, (ROWS, LANES), 0).astype(jnp.float32)
    y_id = lax.broadcasted_iota(jnp.int32, (width, LANES), 0).astype(jnp.bfloat16)

    def prepare(t):
        at = pl.ds(pl.multiple_of(t * 8, 8), 8)
        part = [list_ref[pl.ds(pl.multiple_of(c * count + t * 8, 8), 8), :] for c in range(7)]
        key = part[6].astype(jnp.int32)
        y = key & (width - 1)
        plane = (key >> bits(width)) & (slab - 1)
        table[0, at, :] = (key >> (bits(width) + bits(slab))).astype(jnp.float32)
        phi_x, phi_y, phi_z = (weights(part[c]) for c in (3, 4, 5))
        for k in range(4):
            table[1 + k, at, :] = phi_x[k]
            table[5 + k, at, :] = phi_y[k]
            table[9 + k, at, :] = ((y + (k - 1)) & (width - 1)).astype(jnp.float32)
        for n, q in enumerate(planes):
            rel = q + 1 + shift - plane
            weight = jnp.zeros_like(part[0])
            for k in range(4):
                weight = jnp.where(rel == k, phi_z[k], weight)
            for c in range(3):
                table[13 + n * 3 + c, at, :] = part[c] * weight

    def half(r, base):
        def row(i, like):
            return jnp.broadcast_to(table[i, pl.ds(r, 1), :], like.shape)

        def narrow(i):
            return jnp.broadcast_to(table[i, pl.ds(r, 1), :].astype(jnp.bfloat16), y_id.shape)

        right = jnp.zeros(y_id.shape, jnp.bfloat16)
        for k in range(4):
            right = jnp.where(y_id == narrow(9 + k), narrow(5 + k), right)
        x = table[0, pl.ds(r, 1), :] - base
        x = jnp.where((x >= 0.0) & (x < WINDOW), x, 4.0 * ROWS)
        rel = row_id - x
        weight_x = jnp.zeros(row_id.shape, jnp.float32)
        for k in range(4):
            weight_x = jnp.where(rel == k, row(1 + k, row_id), weight_x)
        lefts = [row(13 + i, row_id) * weight_x for i in range(3 * len(planes))]
        return jnp.concatenate(lefts, 0).astype(jnp.bfloat16), right

    def window(w, offset):
        begin = starts[w] // BLOCK
        end = (starts[w + 1] + (BLOCK - 1)) // BLOCK
        base = (w * WINDOW).astype(jnp.float32)
        at_row = (w + offset) * WINDOW

        @pl.loop(0, (end - begin + 1) // 2)
        def _(pair):
            b = begin + 2 * pair
            more = b + 1 < end
            parts = []
            for block, shifted in (
                (b, base),
                (jnp.where(more, b + 1, b), jnp.where(more, base, -4.0 * ROWS * WINDOW * LANES)),
            ):
                for h in range(BLOCK // LANES):
                    parts.append(half(block * (BLOCK // LANES) + h, shifted))
            product = lax.dot_general(
                jnp.concatenate([p[0] for p in parts], 1),
                jnp.concatenate([p[1] for p in parts], 1),
                (((1,), (1,)), ((), ())),
                preferred_element_type=jnp.float32,
            )
            rows = pl.ds(pl.multiple_of(at_row, 8), ROWS)
            for n, q in enumerate(planes):
                for c in range(3):
                    i = n * 3 + c
                    acc[q * 3 + c, rows, :] += product[i * ROWS : (i + 1) * ROWS]

    for first, last, offset in ranges:
        unit = 8 * LANES
        low = starts[first] // BLOCK * BLOCK // unit
        high = (starts[last] + (BLOCK - 1)) // BLOCK * BLOCK

        @pl.loop(low, (high + (unit - 1)) // unit)
        def _(t):
            prepare(t)

        @pl.loop(first, last)
        def _(w):
            window(w, offset)


VMEM = pl.BlockSpec(memory_space=pltpu.VMEM)
SMEM = pl.BlockSpec(memory_space=pltpu.SMEM)


def cost(flops):
    return pl.CostEstimate(flops=flops, bytes_accessed=4_000_000, transcendentals=0)


def starts_of(listed, windows):
    return listed[-8, : windows + 1].astype(jnp.int32)


def spread_own(listed, slab, width):
    windows = width // WINDOW

    count = (listed.shape[0] - 8) // 7
    assert count % 8 == 0

    def kernel(starts, list_ref, acc, table):
        acc[...] = jnp.zeros_like(acc)
        spread_list(starts, list_ref, acc, table, 0, range(slab), slab, [(0, windows, 0)])

    return pl.pallas_call(
        kernel,
        out_shape=jax.ShapeDtypeStruct((slab * 3, width + ROWS - WINDOW, width), jnp.float32),
        in_specs=[SMEM, VMEM],
        out_specs=VMEM,
        scratch_shapes=[pltpu.VMEM((rows_of(range(slab)), count, LANES), jnp.float32)],
        compiler_params=pltpu.CompilerParams(vmem_limit_bytes=12 * MIB),
        name="spread_own",
        cost_estimate=cost(20_000_000_000),
    )(starts_of(listed, windows), listed)


ANY = pl.BlockSpec(memory_space=pl.ANY)
HBM = pl.BlockSpec(memory_space=pltpu.HBM)
LAG = 7
KEEP = 1.0 - 1.0 / relax_time
FORCING = 1.0 - 0.5 / relax_time


def collided(f, force, items):
    def along(vector, item, start=None):
        total = start
        for e, v in zip((velocity_x[item], velocity_y[item], velocity_z[item]), vector):
            if e == 0:
                continue
            if total is None:
                total = v if e > 0 else -v
            else:
                total = total + v if e > 0 else total - v
        return total

    def tree(values):
        while len(values) > 1:
            values = [
                values[i] + values[i + 1] if i + 1 < len(values) else values[i]
                for i in range(0, len(values), 2)
            ]
        return values[0]

    density = tree(list(f))
    inverse = 1.0 / density
    flow = []
    for axis, table in enumerate((velocity_x, velocity_y, velocity_z)):
        plus = tree([f[i] for i in range(19) if table[i] > 0])
        minus = tree([f[i] for i in range(19) if table[i] < 0])
        flow.append(((plus - minus) + 0.5 * force[axis]) * inverse)
    speed_sq = flow[0] * flow[0] + flow[1] * flow[1] + flow[2] * flow[2]
    work = flow[0] * force[0] + flow[1] * force[1] + flow[2] * force[2]
    scaled = density * (1.0 / relax_time)
    base = scaled - (1.5 * scaled) * speed_sq - (3.0 * FORCING) * work
    linear = 3.0 * scaled
    square = 4.5 * scaled
    pushed = [3.0 * FORCING * v for v in force]
    result = {}
    for item in items:
        cu = along(flow, item)
        if cu is None:
            bracket = base
        else:
            facing = along(pushed, item)
            bracket = base + facing + cu * (linear + square * cu + 3.0 * facing)
        result[item] = KEEP * f[item] + lattice_weights[item] * bracket
    return result


def spread_chunk(lists, total, carry, head, populations, field, first, last):
    below, above = lists
    slab, width = (populations.shape[0], populations.shape[2])
    windows = width // WINDOW
    opening, closing = (first == 0, last == windows)
    begin = 0 if opening else (first - 1) * WINDOW
    end = width if closing else (last - 1) * WINDOW
    n = end - begin
    span = n + ROWS
    planes = (slab - 1, 0)

    def kernel(s0, l0, s1, l1, total_ref, carry_ref, head_ref, pop_ref, field_in, *rest):
        low, high, carry_out, field_out, acc, pop, post, table, sems = rest
        del field_in
        copies = []

        def fetch(source, target):
            copy = pltpu.make_async_copy(source, target, sems.at[len(copies)])
            copy.start()
            copies.append(copy)

        got = 0
        if not opening:
            fetch(carry_ref, acc.at[:, 0:ROWS, :])
            got = ROWS
        stop = min(span, width + ROWS - WINDOW - begin)
        fetch(total_ref.at[:, begin + got : begin + stop, :], acc.at[:, got:stop, :])
        early = len(copies)
        for n_plane, plane in enumerate(planes):
            for x in range(0, 3):
                source, target, size = (
                    ((begin - 8) % width, 0, 8),
                    (begin, 8, n),
                    (end % width, n + 8, 8),
                )[x]
                fetch(
                    pop_ref.at[plane, :, source : source + size, :],
                    pop.at[n_plane, :, target : target + size, :],
                )
        for copy in copies[:early]:
            copy.wait()
        if closing:
            acc[:, stop:span, :] = jnp.zeros((slab * 3, span - stop, width), jnp.float32)
        moves = (first, last, 0 if opening else 1 - first)
        spread_list(s0, l0, acc, table, slab, (0, 1), slab, [moves])
        spread_list(s1, l1, acc, table, -slab, (slab - 1,), slab, [moves])
        if closing:
            acc[:, n : n + 16, :] += head_ref[:, 0:16, :]
        if opening:
            carry_out[:, ROWS : 2 * ROWS, :] = acc[:, 0:ROWS, :]
            carry_out[:, 0:ROWS, :] = acc[:, n : n + ROWS, :]
        elif not closing:
            carry_out[:, 0:ROWS, :] = acc[:, n : n + ROWS, :]
        else:
            carry_out[...] = jnp.zeros_like(carry_out)
        written = [
            pltpu.make_async_copy(
                acc.at[i, 8 : 8 + n, :],
                field_out.at[i // 3, i % 3, begin:end, :],
                sems.at[len(copies) + i],
            )
            for i in range(slab * 3)
        ]
        for copy in written:
            copy.start()
        for copy in copies[early:]:
            copy.wait()

        @pl.loop(0, (n + 16) // 8)
        def _(t):
            rows = pl.ds(pl.multiple_of(t * 8, 8), 8)
            for n_plane, plane in enumerate(planes):
                f = [pop[n_plane, i, rows, :] for i in range(19)]
                force = [acc[plane * 3 + c, rows, :] for c in range(3)]
                items = range(n_plane * 5, n_plane * 5 + 5)
                for i, value in collided(f, force, items).items():
                    post[i, rows, :] = value

        for target, begin_item in ((low, 0), (high, 5)):
            for i in range(5):
                item = begin_item + i
                at = 8 - velocity_x[item]
                value = post[item, at : at + n, :]
                if velocity_y[item]:
                    value = pltpu.roll(value, velocity_y[item] % width, 1)
                target[i] = value
        for copy in written:
            copy.wait()

    shape = jax.ShapeDtypeStruct
    return pl.pallas_call(
        kernel,
        out_shape=(
            shape((5, n, width), jnp.float32),
            shape((5, n, width), jnp.float32),
            shape((slab * 3, 2 * ROWS, width), jnp.float32),
            shape((slab, 3, width, width), jnp.float32),
        ),
        in_specs=[SMEM, VMEM, SMEM, VMEM, HBM, ANY, VMEM, HBM, HBM],
        out_specs=(VMEM, VMEM, VMEM, HBM),
        scratch_shapes=[
            pltpu.VMEM((slab * 3, span, width), jnp.float32),
            pltpu.VMEM((2, 19, n + 16, width), jnp.float32),
            pltpu.VMEM((10, n + 16, width), jnp.float32),
            pltpu.VMEM((rows_of((0, 1)), (below.shape[0] - 8) // 7, LANES), jnp.float32),
            pltpu.SemaphoreType.DMA((8 + slab * 3,)),
        ],
        input_output_aliases={} if field is None else {8: 3},
        compiler_params=pltpu.CompilerParams(vmem_limit_bytes=20 * MIB),
        cost_estimate=cost(8_000_000_000),
    )(
        starts_of(below, windows),
        below,
        starts_of(above, windows),
        above,
        total,
        jnp.zeros((slab * 3, ROWS, width), jnp.float32) if carry is None else carry[:, :ROWS],
        jnp.zeros((slab * 3, ROWS, width), jnp.float32) if head is None else head,
        populations,
        jnp.zeros((8, 128), jnp.float32) if field is None else field,
    )


def interior(populations, field):
    slab, width = (populations.shape[0], populations.shape[2])
    pieces = 4
    step = width // pieces

    def kernel(pop_ref, field_ref, out_ref, pop, force, post, out, in_sems, out_sems):
        def fetch(k):
            rows = pl.ds(k * step, step)
            return (
                pltpu.make_async_copy(pop_ref.at[:, :, rows, :], pop.at[:, :, rows, :], in_sems.at[0, k]),
                pltpu.make_async_copy(field_ref.at[:, :, rows, :], force.at[:, :, rows, :], in_sems.at[1, k]),
            )

        for k in range(pieces):
            for copy in fetch(k):
                copy.start()

        ranges = []
        for p in range(slab):
            if p > 0:
                ranges.append((p, 0, 5))
            if p < slab - 1:
                ranges.append((p, 5, 19))
            else:
                ranges.append((p, 10, 19))

        def kept(p):
            return [i for i in range(19) if 0 <= p + velocity_z[i] < slab]

        started = []

        def emit(k, low, high):
            @pl.loop(low // 8, high // 8)
            def _(t):
                for p in range(slab):
                    for i in kept(p):
                        x = velocity_x[i]
                        if x == 0:
                            continue
                        q = p + velocity_z[i]
                        near = pl.ds(pl.multiple_of(t * 8 + (0 if x > 0 else 8), 8), 16)
                        value = post[q, i, near, :]
                        value = value[7:15] if x > 0 else value[1:9]
                        out[q, i, pl.ds(pl.multiple_of(t * 8, 8), 8), :] = value

            for r, (p, begin, end) in enumerate(ranges):
                copy = pltpu.make_async_copy(
                    out.at[p, begin:end, low:high, :],
                    out_ref.at[p, begin:end, low:high, :],
                    out_sems.at[r, k],
                )
                copy.start()
                started.append(copy)

        for k in range(pieces):
            for copy in fetch(k):
                copy.wait()

            @pl.loop(k * step // 8, (k + 1) * step // 8)
            def _(t):
                rows = pl.ds(pl.multiple_of(t * 8, 8), 8)
                padded = pl.ds(pl.multiple_of(t * 8 + 8, 8), 8)
                for p in range(slab):
                    f = [pop[p, i, rows, :] for i in range(19)]
                    moved = collided(f, [force[p, c, rows, :] for c in range(3)], kept(p))
                    for i, value in moved.items():
                        if velocity_y[i]:
                            value = pltpu.roll(value, velocity_y[i] % width, 1)
                        q = p + velocity_z[i]
                        if velocity_x[i]:
                            post[q, i, padded, :] = value
                        else:
                            out[q, i, rows, :] = value

            if k < pieces - 1:
                emit(k, 8 if k == 0 else k * step - 8, (k + 1) * step - 8)
        for p in range(slab):
            for i in kept(p):
                q = p + velocity_z[i]
                if velocity_x[i] > 0:
                    post[q, i, 0:8, :] = post[q, i, width : width + 8, :]
                elif velocity_x[i] < 0:
                    post[q, i, width + 8 : width + 16, :] = post[q, i, 8:16, :]
        emit(pieces - 1, (pieces - 1) * step - 8, width)
        emit(pieces, 0, 8)
        for copy in started:
            copy.wait()

    return pl.pallas_call(
        kernel,
        out_shape=jax.ShapeDtypeStruct(populations.shape, jnp.float32),
        in_specs=[HBM, HBM],
        out_specs=HBM,
        scratch_shapes=[
            pltpu.VMEM(populations.shape, jnp.float32),
            pltpu.VMEM(field.shape, jnp.float32),
            pltpu.VMEM((slab, 19, width + 16, width), jnp.float32),
            pltpu.VMEM(populations.shape, jnp.float32),
            pltpu.SemaphoreType.DMA((2, pieces)),
            pltpu.SemaphoreType.DMA((2 * slab, pieces + 1)),
        ],
        compiler_params=pltpu.CompilerParams(vmem_limit_bytes=36 * MIB),
        name="interior",
        cost_estimate=pl.CostEstimate(flops=0, bytes_accessed=25_000_000, transcendentals=0),
    )(populations, field)


def arrivals(new_populations, lows, highs, edges):
    slab = new_populations.shape[0]
    count = len(lows)

    def kernel(*refs):
        parts, out_ref, sems = (refs[1 : 1 + 2 * count], refs[-2], refs[-1])
        copies = []
        for k, (begin, end) in enumerate(edges):
            for s, (part, plane, item) in enumerate(
                ((parts[k], 0, 0), (parts[count + k], slab - 1, 5))
            ):
                copies.append(
                    pltpu.make_async_copy(
                        part, out_ref.at[plane, item : item + 5, begin:end, :], sems.at[s, k]
                    )
                )
        for copy in copies:
            copy.start()
        for copy in copies:
            copy.wait()

    return pl.pallas_call(
        kernel,
        out_shape=jax.ShapeDtypeStruct(new_populations.shape, jnp.float32),
        in_specs=[HBM] + [VMEM] * (2 * count),
        out_specs=HBM,
        scratch_shapes=[pltpu.SemaphoreType.DMA((2, count))],
        input_output_aliases={0: 0},
        compiler_params=pltpu.CompilerParams(vmem_limit_bytes=8 * MIB),
        name="arrivals",
    )(new_populations, *lows, *highs)


def prepared(displacement, tension, bending, offset, owner, cell, cells, width):
    before, after = halos(displacement, "shard", 2, 2)
    _, vesicles, rows, lanes = displacement.shape
    assert lanes == LANES
    index = lax.axis_index("shard")
    outside = jnp.stack(
        [
            jnp.where(index == 0, 0, -1),
            jnp.where(index == lax.axis_size("shard") - 1, rows + 1, -1),
        ]
    ).astype(jnp.int32)
    slab_bits = bits(cells // (width * width))

    def kernel(edge, t_ref, b_ref, x_ref, before_ref, after_ref, o_ref, own_ref, cell_ref, *rest):
        force_ref, key_ref = rest[:2]
        values, (padded, wide_ref) = (rest[2:8], rest[8:])
        place = lax.broadcasted_iota(jnp.int32, (rows + 2, lanes), 0)

        def laplacian(ref, begin, count):
            center = ref[begin : begin + count, :]
            return (
                ref[begin + 1 : begin + count + 1, :]
                + ref[begin - 1 : begin + count - 1, :]
                + pltpu.roll(center, 1, 1)
                + pltpu.roll(center, lanes - 1, 1)
                - 4.0 * center
            )

        for v in range(vesicles):
            at = slice(v * rows, (v + 1) * rows)
            code = cell_ref[v]
            plane, x, y = (
                code >> (2 * bits(width)),
                (code >> bits(width)) & (width - 1),
                code & (width - 1),
            )
            x = (x + LAG) & (width - 1)
            key_ref[at, :] = own_ref[v] * cells + (
                (x << (bits(width) + slab_bits)) | (plane << bits(width)) | y
            )
            for c in range(3):
                values[3 + c][at, :] = o_ref[c, v]
                padded[6:8, :] = before_ref[c, v]
                padded[8 : 8 + rows, :] = x_ref[c, v]
                padded[8 + rows : 10 + rows, :] = after_ref[c, v]
                wide = laplacian(padded, 7, rows + 2)
                hidden = (place == edge[0]) | (place == edge[1])
                wide_ref[7 : 9 + rows, :] = jnp.where(hidden, 0.0, wide)
                second = laplacian(wide_ref, 8, rows)
                force = t_ref[v] * wide_ref[8 : 8 + rows, :] - b_ref[v] * second
                force_ref[c, v] = force
                values[c][at, :] = force

    shape = jax.ShapeDtypeStruct
    flat = (vesicles * rows, lanes)
    out = pl.pallas_call(
        kernel,
        out_shape=(shape(displacement.shape, jnp.float32), shape(flat, jnp.int32))
        + (shape(flat, jnp.float32),) * 6,
        in_specs=[SMEM] * 3 + [VMEM] * 6,
        out_specs=(VMEM,) * 8,
        scratch_shapes=[pltpu.VMEM((rows + 16, lanes), jnp.float32)] * 2,
        name="prepared",
    )(outside, tension, bending, displacement, before, after, offset, owner, cell)
    return out[0], out[1], out[2:]


def packed(starts, columns, device_count, capacity, cells):
    count = columns[0].shape[0]
    lanes = min(capacity, LANES)
    tiles = capacity // lanes

    def kernel(start_ref, *refs):
        columns, out, table = (refs[:7], refs[7], refs[8])
        for i in range(7):
            table[0:count, i, :] = columns[i][...].astype(jnp.float32)
        field = lax.broadcasted_iota(jnp.int32, (7, LANES), 0)
        lane = lax.broadcasted_iota(jnp.int32, (7, LANES), 1)
        for r in range(tiles + 1):
            table[count + r] = jnp.where(field == 0, float(device_count * cells), 0.0)

        @pl.loop(0, device_count, unroll=4)
        def _(d):
            row, shift = (start_ref[d] // LANES, start_ref[d] % LANES)
            turned = [
                pltpu.roll(table[row + j], (LANES - shift) % LANES, 1) for j in range(tiles + 1)
            ]
            before = (d * cells).astype(jnp.float32)
            for j in range(tiles):
                value = jnp.where(lane < LANES - shift, turned[j], turned[j + 1])
                tag = jnp.minimum(value - before, float(cells))
                out[d, :, j, :] = jnp.where(field == 0, tag, value)[:, :lanes]

    return pl.pallas_call(
        kernel,
        out_shape=jax.ShapeDtypeStruct((device_count, 7, tiles, lanes), jnp.float32),
        in_specs=[SMEM] + [VMEM] * 7,
        out_specs=VMEM,
        scratch_shapes=[pltpu.VMEM((count + tiles + 1, 7, LANES), jnp.float32)],
        compiler_params=pltpu.CompilerParams(vmem_limit_bytes=8 * MIB),
        name="packed",
    )(starts, *columns)


def exchanged(send):
    groups, members = (lax.axis_size("ves"), lax.axis_size("shard"))
    count = groups * members

    def kernel(send_ref, got_ref, own_sem, send_sems, got_sems):
        group, member = (lax.axis_index("ves"), lax.axis_index("shard"))
        me = group * members + member
        barrier = pltpu.get_barrier_semaphore()

        def other(k):
            peer = lax.rem(me + k, count)
            return peer, (peer // members, lax.rem(peer, members))

        def greet(k, carry):
            pl.semaphore_signal(
                barrier, inc=1, device_id=other(k)[1], device_id_type=pl.DeviceIdType.MESH
            )
            return carry

        lax.fori_loop(1, count, greet, 0)
        own = pltpu.make_async_copy(send_ref.at[me], got_ref.at[me], own_sem)
        own.start()
        pl.semaphore_wait(barrier, count - 1)

        def copy(k):
            peer, place = other(k)
            return pltpu.make_async_remote_copy(
                src_ref=send_ref.at[peer],
                dst_ref=got_ref.at[me],
                send_sem=send_sems.at[k],
                recv_sem=got_sems.at[k],
                device_id=place,
                device_id_type=pl.DeviceIdType.MESH,
            )

        def begin(k, carry):
            copy(k).start()
            return carry

        def finish(k, carry):
            copy(k).wait()
            return carry

        lax.fori_loop(1, count, begin, 0)
        own.wait()
        lax.fori_loop(1, count, finish, 0)

    return pl.pallas_call(
        kernel,
        out_shape=jax.ShapeDtypeStruct(send.shape, send.dtype),
        in_specs=[ANY],
        out_specs=ANY,
        scratch_shapes=[
            pltpu.SemaphoreType.DMA,
            pltpu.SemaphoreType.DMA((count,)),
            pltpu.SemaphoreType.DMA((count,)),
        ],
        compiler_params=pltpu.CompilerParams(
            collective_id=0, has_side_effects=True, vmem_limit_bytes=4 * MIB
        ),
        name="exchanged",
    )(send)


def dispatched(key, values, owner, device_count, cells):
    capacity = 2 * owner.size // device_count
    devices = jnp.arange(device_count, dtype=jnp.int32)
    starts = jnp.sum((owner.reshape(-1)[None, :] < devices[:, None]).astype(jnp.int32), 1)
    ordered = lax.sort(
        (key.reshape(-1),) + tuple(v.reshape(-1) for v in values), num_keys=1, is_stable=False
    )
    send = packed(
        starts, [v.reshape(-1, LANES) for v in ordered], device_count, capacity, cells
    )
    return exchanged(send)


CUTS = (0, 4, 9, 13, 16)
OFFSET_BITS = (16, 16, 14)


def one_step(displacement, tension, bending, offset, owner, cell, populations):
    device_count = lax.axis_size("ves") * lax.axis_size("shard")
    slab, width = (populations.shape[0], populations.shape[2])
    cells = slab * width * width
    windows = width // WINDOW
    x_bit = bits(slab) + bits(width)
    membrane_force, key, values = prepared(
        displacement, tension, bending, offset, owner, cell, cells, width
    )
    got = dispatched(key, values, owner, device_count, cells)
    got = [got[:, i].reshape(-1) for i in range(7)]
    key = got[0].astype(jnp.int32)
    bounds = jnp.arange(windows + 1, dtype=jnp.int32) * (WINDOW << x_bit)
    starts = jnp.sum((key[None, :] < bounds[:, None]).astype(jnp.float32), 1)
    fixed = [
        jnp.floor(v * (2.0**n - 1.0) + 0.5).astype(jnp.int32)
        for v, n in zip(got[4:], OFFSET_BITS)
    ]
    top = width << x_bit
    ordered = lax.sort(
        (
            ((key - top) << OFFSET_BITS[2]) + fixed[2],
            ((fixed[0] - (1 << 15)) << OFFSET_BITS[1]) + fixed[1],
        )
        + tuple(got[1:4]),
        num_keys=1,
        is_stable=False,
    )
    code = (ordered[0] >> OFFSET_BITS[2]) + top
    fixed = [
        (ordered[1] >> OFFSET_BITS[1]) + (1 << 15),
        ordered[1] & ((1 << OFFSET_BITS[1]) - 1),
        ordered[0] & ((1 << OFFSET_BITS[2]) - 1),
    ]
    columns = (
        list(ordered[2:])
        + [v.astype(jnp.float32) * (1.0 / (2.0**n - 1.0)) for v, n in zip(fixed, OFFSET_BITS)]
        + [code.astype(jnp.float32)]
    )
    starts = jnp.pad(starts, (0, LANES - windows - 1))
    listed = jnp.concatenate(
        [v.reshape(-1, LANES) for v in columns]
        + [jnp.broadcast_to(starts[None, :], (8, LANES))],
        0,
    )
    below = passed_along(listed, ("ves", "shard"), 1)
    above = passed_along(listed, ("ves", "shard"), -1)
    total = spread_own(listed, slab, width)

    cuts = [cut * windows // CUTS[-1] for cut in CUTS]
    field = carry = head = None
    lows, highs, edges = ([], [], [])
    begin = 0
    for j, (first, last) in enumerate(zip(cuts[:-1], cuts[1:])):
        low, high, carry, field = spread_chunk(
            (below, above), total, carry, head if last == windows else None,
            populations, field, first, last,
        )
        if j == 0:
            head = carry[:, ROWS:]
        edges.append((begin, begin + low.shape[1]))
        begin += low.shape[1]
        lows.append(passed_along(low, ("ves", "shard"), 1))
        highs.append(passed_along(high, ("ves", "shard"), -1))
    new_populations = interior(populations, field)
    new_populations = arrivals(new_populations, lows, highs, edges)
    return (membrane_force, field, new_populations)


def solution(mesh):
    return jax.shard_map(
        one_step,
        mesh=mesh,
        in_specs=(
            P(None, "ves", "shard", None),
            P("ves"),
            P("ves"),
            P(None, "ves", "shard", None),
            P("ves", "shard", None),
            P("ves", "shard", None),
            P(("ves", "shard"), None, None, None),
        ),
        out_specs=(
            P(None, "ves", "shard", None),
            P(("ves", "shard"), None, None, None),
            P(("ves", "shard"), None, None, None),
        ),
        check_vma=False,
    )
```
